32 devices in a mesh: seq: 4 (over x, core), dp: 8 (over z, y).
Axes of the slice: x: 2, y: 2, z: 4, core: 2. Of those that a mesh axis runs over, the one named last changes fastest.
Arguments:
- tokens: bfloat16 [8, 1024, 1024], P('dp', 'seq'), may hold values from -6 to 6
- first_values: bfloat16 [8, 1024, 1024], P('dp', 'seq'), may hold values from -6 to 6
- value_grad_acc: float32 [8, 1024, 1024], P('dp', 'seq'), may hold values from -3 to 3
- segment_ids: int32 [8, 1024], P('dp'), may hold values from 0 to 5, never falling along the last dimension, each value on 1 to 512 neighbouring positions
- query_weight: bfloat16 [1024, 1024], P(('seq', 'dp')), may hold values from -0.1875 to 0.1875
- key_weight: bfloat16 [1024, 1024], P(('seq', 'dp')), may hold values from -0.1875 to 0.1875
- value_weight: bfloat16 [1024, 1024], P(('seq', 'dp')), may hold values from -0.1875 to 0.1875
- out_weight: bfloat16 [1024, 1024], P(('seq', 'dp')), may hold values from -1.5 to 1.5
- attn_gain: bfloat16 [1024], P(('seq', 'dp')), may hold values from 0.099609375 to 1.8984375
- gate_weight: bfloat16 [1024, 2816], P(('seq', 'dp')), may hold values from -0.1875 to 0.1875
- up_weight: bfloat16 [1024, 2816], P(('seq', 'dp')), may hold values from -0.1875 to 0.1875
- down_weight: bfloat16 [2816, 1024], P(('seq', 'dp')), may hold values from -0.109375 to 0.109375
- mlp_gain: bfloat16 [1024], P(('seq', 'dp')), may hold values from 0.099609375 to 1.8984375
- out_grad: bfloat16 [8, 1024, 1024], P('dp', 'seq'), may hold values from -6 to 6
Outputs:
- layer_out: bfloat16 [8, 1024, 1024], P('dp', 'seq')
- token_grad: bfloat16 [8, 1024, 1024], P('dp', 'seq')
- value_grad_out: float32 [8, 1024, 1024], P('dp', 'seq')
- grad_query: float32 [1024, 1024], P(('seq', 'dp'))
- grad_key: float32 [1024, 1024], P(('seq', 'dp'))
- grad_value: float32 [1024, 1024], P(('seq', 'dp'))
- grad_out: float32 [1024, 1024], P(('seq', 'dp'))
- grad_attn_gain: float32 [1024], P(('seq', 'dp'))
- grad_gate: float32 [1024, 2816], P(('seq', 'dp'))
- grad_up: float32 [1024, 2816], P(('seq', 'dp'))
- grad_down: float32 [2816, 1024], P(('seq', 'dp'))
- grad_mlp_gain: float32 [1024], P(('seq', 'dp'))
The draws below stay inside these ranges and needn't reach their ends.
Inputs may be any that keep to these rules, and one draw needn't show every extreme that they name: `segment_ids`: along each sequence the ids never fall; a document holds 1 to 512 tokens, and one holds exactly 512.
All inputs are finite; a program needn't handle non-finite values.
Results may differ from the reference program's by a relative error of at most 0.015.
Values may be sent and summed in bfloat16 or wider, within the bound.
No kernel may reach another device: no remote copies, remote signals or barrier semaphores. Data moves between devices by JAX's collectives and lax.ppermute only.
A program may use at most 192 MiB of HBM per device.

```python
import math
import jax
import jax.numpy as jnp
import numpy as np
from jax import lax

D = 1024
HEADS = 16
FF = 2816
HEAD_DIM = 64
LEN = 1024
SEQS = 8
DOCS = 6
DOC_MOST = 512


def levels(rng, extent, cuts, low, top_value):
    def one(dim, blocks):
        heights = jax.random.uniform(jax.random.fold_in(jax.random.fold_in(rng, 6), dim), (blocks,), jnp.float32, low / len(cuts), top_value / len(cuts))
        return jnp.repeat(jnp.exp(heights), extent[dim] // blocks).reshape((-1,) + (1,) * (len(extent) - dim - 1))

    loudness = one(*cuts[0])
    for cut in cuts[1:]:
        loudness = loudness * one(*cut)
    return loudness


def length_profile(amount, total, bound, slope):
    portions = [(1 << 20) // math.isqrt(standing ** slope) + 1 for standing in range(2, amount + 1)]
    surplus, counts = total - bound - (amount - 1), [1] * (amount - 1)
    while surplus > 0:
        free = [i for i in range(amount - 1) if counts[i] < bound]
        mass, left = sum([portions[i] for i in free]), surplus
        for i in free:
            extra = min(bound - counts[i], max(1, left * portions[i] // mass), surplus)
            counts[i] = counts[i] + extra
            surplus = surplus - extra
    return np.array([bound] + counts)


def uneven(stream_key, amount, total, reach, lean):
    if amount == 2:
        one = jax.random.randint(stream_key, (), max(1, total - reach), min(reach, total - 1) + 1)
        return jnp.stack([one, total - one])
    lengths = jnp.asarray(length_profile(amount, total, reach, lean), jnp.int32)
    couples = (amount - 1) // 2
    source_of, receiver = lengths[1:1 + 2 * couples:2], lengths[2:2 + 2 * couples:2]
    slack = jnp.minimum(source_of - 1, reach - receiver)
    moved = jax.random.randint(jax.random.fold_in(stream_key, 1), (couples,), 0, 1 << 20) % (slack + 1)
    lengths = lengths.at[1:1 + 2 * couples:2].set(source_of - moved).at[2:2 + 2 * couples:2].set(receiver + moved)
    return lengths[jax.random.permutation(jax.random.fold_in(stream_key, 2), amount)]


def noise(stream_key, shape, spread, limit, pieces=(), kind=jnp.bfloat16):
    values = jax.random.normal(stream_key, shape, jnp.float32) * spread
    if len(pieces) > 0:
        values = levels(stream_key, shape, pieces, -0.22, 0.18) * values
    return jnp.clip(values, min=-limit, max=limit).astype(kind)


def setup_inputs(seed: int = 0) -> dict:
    seeds = jax.random.split(jax.random.key(seed), 15)
    tokens = noise(seeds[0], (SEQS, LEN, D), 1.0, 6.0, ((0, 8), (1, 4)))
    first_values = noise(seeds[1], (SEQS, LEN, D), 1.0, 6.0, ((0, 8), (1, 4)))
    value_grad_acc = noise(seeds[2], (SEQS, LEN, D), 0.5, 3.0, ((0, 8), (1, 4)), jnp.float32)
    segment_ids = jax.vmap(lambda own: jnp.searchsorted(jnp.cumsum(uneven(own, DOCS, LEN, DOC_MOST, 2)), jnp.arange(LEN), side="right"))(jax.random.split(seeds[3], SEQS)).reshape((SEQS, LEN)).astype(jnp.int32)
    query_weight = noise(seeds[4], (D, D), D ** -0.5, 0.1875, ((0, 32),))
    key_weight = noise(seeds[5], (D, D), D ** -0.5, 0.1875, ((0, 32),))
    value_weight = noise(seeds[6], (D, D), D ** -0.5, 0.1875, ((0, 32),))
    out_weight = noise(seeds[7], (D, D), (D // 64) ** -0.5, 1.5, ((0, 32),))
    attn_gain = jnp.clip(1.0 + 0.18 * jax.random.normal(seeds[8], (D,), jnp.float32), 0.099609375, 1.8984375).astype(jnp.bfloat16)
    gate_weight = noise(seeds[9], (D, FF), D ** -0.5, 0.1875, ((0, 32),))
    up_weight = noise(seeds[10], (D, FF), D ** -0.5, 0.1875, ((0, 32),))
    down_weight = noise(seeds[11], (FF, D), FF ** -0.5, 0.109375, ((0, 32),))
    mlp_gain = jnp.clip(1.0 + 0.18 * jax.random.normal(seeds[12], (D,), jnp.float32), 0.099609375, 1.8984375).astype(jnp.bfloat16)
    out_grad = noise(seeds[13], (SEQS, LEN, D), 1.0, 6.0, ((0, 8), (1, 4)))
    return dict(tokens=tokens, first_values=first_values, value_grad_acc=value_grad_acc, segment_ids=segment_ids, query_weight=query_weight, key_weight=key_weight, value_weight=value_weight, out_weight=out_weight, attn_gain=attn_gain, gate_weight=gate_weight, up_weight=up_weight, down_weight=down_weight, mlp_gain=mlp_gain, out_grad=out_grad)


@jax.custom_vjp
def low(v):
    return lax.optimization_barrier(v.astype(jnp.bfloat16)).astype(jnp.float32)

@jax.custom_vjp
def low_back(v):
    return v

def low_keep(v):
    return (low(v), None)

def low_pass(kept, grad):
    return (grad,)

def back_keep(v):
    return (v, None)

def back_low(kept, grad):
    return (low(grad),)
low.defvjp(low_keep, low_pass)
low_back.defvjp(back_keep, back_low)
epsilon = 1e-06
masked_value = -1e+30
highest = lax.Precision.HIGHEST

def angles(positions, head_width):
    pairs = jnp.arange(head_width // 2, dtype=jnp.float32)
    freq = jnp.exp(pairs * (-2.0 * math.log(10000.0) / head_width))
    theta = positions.astype(jnp.float32)[:, None] * freq[None, :]
    return (jnp.cos(theta)[:, None, :], jnp.sin(theta)[:, None, :])

def rotate(field, cos_table, sin_table):
    half = cos_table.shape[-1]
    first = field[..., :half]
    second = field[..., half:]
    return jnp.concatenate([first * cos_table - second * sin_table, second * cos_table + first * sin_table], axis=-1)

def norm(field, gain):
    scale = lax.rsqrt(lax.optimization_barrier(jnp.mean(field * field, axis=-1, keepdims=True)) + epsilon)
    return field * scale * gain

def layer(tokens, first_values, weights, segment_row):
    query_weight, key_weight, value_weight, out_weight, attn_gain, gate_weight, up_weight, down_weight, mlp_gain = weights
    length = tokens.shape[0]
    normed_in = low(norm(tokens, attn_gain))
    positions = jnp.arange(length)
    cos_table, sin_table = angles(positions, HEAD_DIM)
    query_lin = low_back(jnp.dot(normed_in, query_weight, precision=highest)).reshape(length, HEADS, HEAD_DIM)
    key_lin = low_back(jnp.dot(normed_in, key_weight, precision=highest)).reshape(length, HEADS, HEAD_DIM)
    value_lin = low_back(jnp.dot(normed_in, value_weight, precision=highest))
    queries = low(rotate(query_lin, cos_table, sin_table))
    keys = low(rotate(key_lin, cos_table, sin_table))
    values = low(0.5 * value_lin + 0.5 * first_values).reshape(length, HEADS, HEAD_DIM)
    scores = low_back(jnp.einsum('ihd,jhd->hij', queries, keys, precision=highest) / math.sqrt(HEAD_DIM))
    allowed = (segment_row[:, None] == segment_row[None, :]) & (positions[None, :] <= positions[:, None])
    masked = jnp.where(allowed[None], scores, masked_value)
    row_top = lax.optimization_barrier(jnp.max(masked, axis=-1, keepdims=True))
    expos = jnp.exp(masked - row_top)
    probs = expos / lax.optimization_barrier(jnp.sum(expos, axis=-1, keepdims=True))
    probs_low = low(probs)
    attended = jnp.einsum('hij,jhd->ihd', probs_low, values, precision=highest).reshape(length, HEADS * HEAD_DIM)
    attended = low(low_back(attended))
    branch = low_back(jnp.dot(attended, out_weight, precision=highest))
    middle = tokens + branch
    normed_mid = low(norm(middle, mlp_gain))
    gate_proj = low_back(jnp.dot(normed_mid, gate_weight, precision=highest))
    up_proj = low_back(jnp.dot(normed_mid, up_weight, precision=highest))
    hidden = low(gate_proj * jax.nn.sigmoid(gate_proj) * up_proj)
    return middle + jnp.dot(hidden, down_weight, precision=highest)

def reference(tokens, first_values, value_grad_acc, segment_ids, query_weight, key_weight, value_weight, out_weight, attn_gain, gate_weight, up_weight, down_weight, mlp_gain, out_grad):
    weights = tuple((w.astype(jnp.float32) for w in (query_weight, key_weight, value_weight, out_weight, attn_gain, gate_weight, up_weight, down_weight, mlp_gain)))

    def one_sequence(running, inputs):
        row_tokens, row_first, row_segments, row_grad = inputs

        def forward(tok_f, first_f, weight_f):
            return layer(tok_f, first_f, weight_f, row_segments)
        result, pull = jax.vjp(forward, row_tokens.astype(jnp.float32), row_first.astype(jnp.float32), weights)
        d_tokens, d_first, d_weights = pull(row_grad.astype(jnp.float32))
        running = jax.tree.map(jnp.add, running, d_weights)
        return (running, (result.astype(jnp.bfloat16), d_tokens.astype(jnp.bfloat16), d_first))
    zeros = jax.tree.map(jnp.zeros_like, weights)
    totals, (layer_out, token_grad, first_grad) = lax.scan(one_sequence, zeros, (tokens, first_values, segment_ids, out_grad))
    return (layer_out, token_grad, value_grad_acc + first_grad, totals[0], totals[1], totals[2], totals[3], totals[4], totals[5], totals[6], totals[7], totals[8])
```

```python
import functools
import math

import jax
import jax.numpy as jnp
from jax import lax
from jax.experimental import pallas as pl
from jax.experimental.pallas import tpu as pltpu
from jax.sharding import PartitionSpec as P

HEADS = 16
DOC_MOST = 512
SEQ = 4
BLOCK = 256

epsilon = 1e-06
masked_value = -1e30
bf16 = jnp.bfloat16
f32 = jnp.float32
VMEM_LIMIT = 56 << 20


def mul(a, b, ca, cb):
    return lax.dot_general(a, b, (((ca,), (cb,)), ((), ())), preferred_element_type=f32)


def params(limit=VMEM_LIMIT):
    return pltpu.CompilerParams(vmem_limit_bytes=limit)


def half_swap(field):
    lanes = field.shape[-1]
    lane = lax.broadcasted_iota(jnp.int32, field.shape, 1)
    up = pltpu.roll(field, lanes - 32, 1)
    down = pltpu.roll(field, 32, 1)
    return jnp.where(lane % 64 < 32, up, down)


def qkv_kernel(me_ref, tok_ref, first_ref, w_ref, gain_ref, cos_ref, sin_ref, nin_ref, q_ref, k_ref, v_ref):
    x = tok_ref[...].astype(f32)
    scale = lax.rsqrt(jnp.mean(x * x, axis=-1, keepdims=True) + epsilon)
    nin = (x * scale * gain_ref[...]).astype(bf16)
    nin_ref[...] = nin
    lin = mul(nin, w_ref[...], 1, 0)
    cos = jnp.concatenate([cos_ref[...]] * 2, axis=1)
    sin = jnp.concatenate([sin_ref[...]] * 2, axis=1)
    part = lin.shape[1] // 3
    q = lin[:, :part]
    q_ref[...] = ((q * cos + half_swap(q) * sin).astype(bf16).astype(f32) * 0.125).astype(bf16)
    k = lin[:, part : 2 * part]
    k_ref[...] = (k * cos + half_swap(k) * sin).astype(bf16)
    v_ref[...] = (0.5 * lin[:, 2 * part :] + 0.5 * first_ref[...].astype(f32)).astype(bf16)


def qkv_call(me, tok_rel, first_rel, w, gain, cos, sin):
    length, width = tok_rel.shape
    part = w.shape[1] // 3
    rows = length // SEQ
    rel = lambda k, m: (k, 0)
    here = lambda k, m: (m[0] ^ k, 0)
    whole = lambda k, m: (0, 0)
    return pl.pallas_call(
        qkv_kernel,
        name="qkv",
        grid_spec=pltpu.PrefetchScalarGridSpec(
            num_scalar_prefetch=1,
            grid=(SEQ,),
            in_specs=[
                pl.BlockSpec((rows, width), rel),
                pl.BlockSpec((rows, part), rel),
                pl.BlockSpec(w.shape, whole),
                pl.BlockSpec((1, width), whole),
                pl.BlockSpec((rows, 128), here),
                pl.BlockSpec((rows, 128), here),
            ],
            out_specs=[pl.BlockSpec((rows, width), here)] + [pl.BlockSpec((rows, part), here)] * 3,
        ),
        out_shape=[jax.ShapeDtypeStruct((length, width), bf16)]
        + [jax.ShapeDtypeStruct((length, part), bf16)] * 3,
        compiler_params=params(),
    )(me, tok_rel, first_rel, w, gain, cos, sin)


def key_range(block):
    return max(0, block * BLOCK - (DOC_MOST // BLOCK) * BLOCK), (block + 1) * BLOCK


def allowed_pairs(seg_col, seg_row, block, low, high):
    keys = lax.broadcasted_iota(jnp.int32, (high - low, BLOCK), 0) + low
    rows = lax.broadcasted_iota(jnp.int32, (high - low, BLOCK), 1) + block * BLOCK
    return (seg_col[low:high, :] == seg_row[:, block * BLOCK : (block + 1) * BLOCK]) & (keys <= rows)


def head_lanes(field, head):
    lane = lax.broadcasted_iota(jnp.int32, field.shape, 1)
    return jnp.where(lane // 64 == head, field, jnp.zeros_like(field))


def attend_kernel(q_ref, k_ref, v_ref, seg_col, seg_row, o_ref, lse_ref):
    length = q_ref.shape[0]
    turned = v_ref[...].astype(f32).T.astype(bf16)
    for block in range(length // BLOCK):
        low, high = key_range(block)
        allowed = allowed_pairs(seg_col, seg_row, block, low, high)
        here = slice(block * BLOCK, (block + 1) * BLOCK)
        outs = []
        for head in range(2):
            scores = mul(k_ref[low:high, :], head_lanes(q_ref[here, :], head), 1, 1)
            scores = jnp.where(allowed, scores, masked_value)
            top = jnp.max(scores, axis=0, keepdims=True)
            expo = jnp.exp(scores - top)
            total = jnp.sum(expo, axis=0, keepdims=True)
            probs = (expo * (1.0 / total)).astype(bf16)
            outs.append(mul(turned[head * 64 : head * 64 + 64, low:high], probs, 1, 0))
            lse_ref[0, head : head + 1, here] = top + jnp.log(total)
        o_ref[here, :] = jnp.concatenate(outs, axis=0).T.astype(bf16)


def attend_call(q, k, v, seg_col, seg_row):
    length, part = q.shape
    pairs = part // 128
    lanes = pl.BlockSpec((length, 128), lambda p: (0, p))
    return pl.pallas_call(
        attend_kernel,
        name="attend",
        grid=(pairs,),
        in_specs=[lanes] * 3
        + [pl.BlockSpec((length, 1), lambda p: (0, 0)), pl.BlockSpec((1, length), lambda p: (0, 0))],
        out_specs=[lanes, pl.BlockSpec((1, 2, length), lambda p: (p, 0, 0))],
        out_shape=[
            jax.ShapeDtypeStruct((length, part), bf16),
            jax.ShapeDtypeStruct((pairs, 2, length), f32),
        ],
        compiler_params=params(),
    )(q, k, v, seg_col, seg_row)


def attend_back_kernel(
    q_ref, k_ref, v_ref, da_ref, lse_ref, seg_col, seg_row, cos_ref, sin_ref, dq_ref, dk_ref, dv_ref, dk_sum, dv_sum
):
    length = q_ref.shape[0]
    dk_sum[...] = jnp.zeros_like(dk_sum)
    dv_sum[...] = jnp.zeros_like(dv_sum)
    turned = k_ref[...].astype(f32).T.astype(bf16)
    for block in range(length // BLOCK):
        low, high = key_range(block)
        allowed = allowed_pairs(seg_col, seg_row, block, low, high)
        here = slice(block * BLOCK, (block + 1) * BLOCK)
        outs = []
        dk_part = jnp.zeros((high - low, 128), f32)
        dv_part = jnp.zeros((high - low, 128), f32)
        for head in range(2):
            q_head = head_lanes(q_ref[here, :], head)
            da_head = head_lanes(da_ref[here, :], head)
            scores = mul(k_ref[low:high, :], q_head, 1, 1)
            probs = jnp.where(allowed, jnp.exp(scores - lse_ref[0, head : head + 1, here]), 0.0)
            d_probs = mul(v_ref[low:high, :], da_head, 1, 1)
            delta = jnp.sum(probs * d_probs, axis=0, keepdims=True)
            d_scores = (probs * (d_probs - delta)).astype(bf16)
            outs.append(mul(turned[head * 64 : head * 64 + 64, low:high], d_scores, 1, 0))
            dk_part = dk_part + mul(d_scores, q_head, 1, 0)
            dv_part = dv_part + mul(probs.astype(bf16), da_head, 1, 0)
        dk_sum[low:high, :] += dk_part
        dv_sum[low:high, :] += dv_part
        dq = jnp.concatenate(outs, axis=0).T * 0.125
        dq_ref[here, :] = (dq * cos_ref[here, :] - half_swap(dq) * sin_ref[here, :]).astype(bf16)
    dk = dk_sum[...]
    dk_ref[...] = (dk * cos_ref[...] - half_swap(dk) * sin_ref[...]).astype(bf16)
    dv_ref[...] = (0.5 * dv_sum[...]).astype(bf16)


def attend_back_call(q, k, v, da, lse, seg_col, seg_row, cos, sin):
    length, part = q.shape
    lanes = pl.BlockSpec((length, 128), lambda p: (0, p))
    whole = lambda *shape: pl.BlockSpec(shape, lambda p: (0, 0))
    return pl.pallas_call(
        attend_back_kernel,
        name="attend_back",
        grid=(part // 128,),
        in_specs=[lanes] * 4
        + [
            pl.BlockSpec((1, 2, length), lambda p: (p, 0, 0)),
            whole(length, 1),
            whole(1, length),
            whole(length, 128),
            whole(length, 128),
        ],
        out_specs=[lanes] * 3,
        out_shape=[jax.ShapeDtypeStruct((length, part), bf16)] * 3,
        scratch_shapes=[pltpu.VMEM((length, 128), f32)] * 2,
        compiler_params=params(),
    )(q, k, v, da, lse, seg_col, seg_row, cos, sin)


def ffn_kernel(
    me_ref, tok_ref, og_ref, a0, a1, a2, a3, wo_ref, gain_ref, wg_ref, wu_ref, wd_ref,
    mid_ref, nm_ref, hid_ref, dg_ref, du_ref, dnm_ref, lo_ref, gain_grad_ref,
):
    step = pl.program_id(0)
    mid = tok_ref[...].astype(f32)
    part = a0.shape[1]
    for j, a in enumerate((a0, a1, a2, a3)):
        mid = mid + mul(a[...], wo_ref[j * part : (j + 1) * part, :], 1, 0)
    scale = lax.rsqrt(jnp.mean(mid * mid, axis=-1, keepdims=True) + epsilon)
    unit = mid * scale
    nm = (unit * gain_ref[...]).astype(bf16)
    nm_ref[...] = nm
    gate = mul(nm, wg_ref[...], 1, 0)
    up = mul(nm, wu_ref[...], 1, 0)
    sig = jax.nn.sigmoid(gate)
    silu = gate * sig
    hidden = (silu * up).astype(bf16)
    hid_ref[...] = hidden
    d_hidden = mul(og_ref[...], wd_ref[...], 1, 1)
    d_gate = (d_hidden * up * (sig * (1.0 + gate * (1.0 - sig)))).astype(bf16)
    d_up = (d_hidden * silu).astype(bf16)
    dg_ref[...] = d_gate
    du_ref[...] = d_up
    dnm = mul(d_gate, wg_ref[...], 1, 1) + mul(d_up, wu_ref[...], 1, 1)
    dnm_ref[...] = dnm.astype(bf16)
    lo_ref[...] = mul(hidden, wd_ref[...], 1, 0).astype(bf16)
    gain_part = jnp.sum(dnm * unit, axis=0, keepdims=True)

    @pl.when(step == 0)
    def _():
        gain_grad_ref[...] = gain_part

    @pl.when(step > 0)
    def _():
        gain_grad_ref[...] += gain_part

    @pl.when(step == SEQ - 1)
    def _():
        mid_ref[...] = mid


def ffn_call(me, tok_rel, og_rel, att, wo_rel, gain, wg, wu, wd):
    length, width = tok_rel.shape
    rows = length // SEQ
    inner = wg.shape[1]
    part = att[0].shape[1]
    rel = lambda k, m: (SEQ - 1 - k, 0)
    here = lambda k, m: (m[0] ^ (SEQ - 1 - k), 0)
    whole = lambda k, m: (0, 0)
    one = lambda shape: pl.BlockSpec(shape, whole, pipeline_mode=pl.Buffered(1))
    return pl.pallas_call(
        ffn_kernel,
        name="ffn",
        grid_spec=pltpu.PrefetchScalarGridSpec(
            num_scalar_prefetch=1,
            grid=(SEQ,),
            in_specs=[pl.BlockSpec((rows, width), rel)] * 2
            + [pl.BlockSpec((rows, part), here)] * 4
            + [one(wo_rel.shape), one((1, width)), one(wg.shape), one(wu.shape), one(wd.shape)],
            out_specs=[
                one((rows, width)),
                pl.BlockSpec((rows, width), rel),
                pl.BlockSpec((rows, inner), rel),
                pl.BlockSpec((rows, inner), rel),
                pl.BlockSpec((rows, inner), rel),
                pl.BlockSpec((rows, width), rel),
                pl.BlockSpec((rows, width), rel),
                one((1, width)),
            ],
        ),
        out_shape=[
            jax.ShapeDtypeStruct((rows, width), f32),
            jax.ShapeDtypeStruct((length, width), bf16),
            jax.ShapeDtypeStruct((length, inner), bf16),
            jax.ShapeDtypeStruct((length, inner), bf16),
            jax.ShapeDtypeStruct((length, inner), bf16),
            jax.ShapeDtypeStruct((length, width), bf16),
            jax.ShapeDtypeStruct((length, width), bf16),
            jax.ShapeDtypeStruct((1, width), f32),
        ],
        compiler_params=params(),
    )(me, tok_rel, og_rel, *att, wo_rel, gain, wg, wu, wd)


def to_core(value):
    return lax.ppermute(value, "seq", [(i, i ^ 1) for i in range(SEQ)])


def to_chip(value):
    return lax.ppermute(value, "seq", [(i, i ^ 2) for i in range(SEQ)])


def gather_rel(value):
    far = to_chip(value)
    near = to_core(value)
    return value, near, far, to_core(far)


def exchange_rel(pieces):
    return (
        pieces[0],
        to_core(pieces[1]),
        to_chip(pieces[2]),
        lax.ppermute(pieces[3], "seq", [(i, i ^ 3) for i in range(SEQ)]),
    )


def scatter_sum(blocks):
    far = blocks[2].astype(f32) + to_core(blocks[3]).astype(f32)
    far = to_chip(far.astype(bf16))
    near = blocks[0].astype(f32) + to_core(blocks[1]).astype(f32)
    return near + far.astype(f32)


def by_index(me, pieces):
    a = jnp.where(me & 1, jnp.stack([pieces[1], pieces[0], pieces[3], pieces[2]]), jnp.stack(pieces))
    return jnp.where(me & 2, jnp.concatenate([a[2:], a[:2]]), a)


def body(
    tokens, first_values, value_grad_acc, segment_ids, query_weight, key_weight, value_weight, out_weight,
    attn_gain, gate_weight, up_weight, down_weight, mlp_gain, out_grad,
):
    dp = lax.axis_size("dp")
    rows, width = tokens.shape[1:]
    length = segment_ids.shape[1]
    w_rows = query_weight.shape[0]
    d_rows = down_weight.shape[0]
    part = width // SEQ
    inner = gate_weight.shape[1] // SEQ
    head_width = width // HEADS
    me = lax.axis_index("seq")
    mine = lax.axis_index("dp")
    me_arg = me.astype(jnp.int32)[None]

    def columns(weight, count):
        return weight.reshape(w_rows, SEQ, count).transpose(1, 0, 2)

    owner = jnp.arange(width) // w_rows == me * dp + mine

    def spread(gain):
        full = jnp.where(owner, jnp.tile(gain, width // w_rows), jnp.zeros((), bf16))
        cut = 3 * part
        return jnp.stack([full[:cut], jnp.pad(full[cut:], (0, 2 * cut - width))])

    gains = jnp.concatenate([spread(attn_gain), spread(mlp_gain), jnp.zeros((4, 3 * part), bf16)])
    attn_cols = jnp.concatenate([columns(w, part) for w in (query_weight, key_weight, value_weight)], axis=2)
    attn_cols = jnp.concatenate([attn_cols, jnp.broadcast_to(gains[None], (SEQ,) + gains.shape)], axis=1)
    mlp_cols = jnp.concatenate([columns(w, inner) for w in (gate_weight, up_weight)], axis=2)
    attn_cols = lax.all_to_all(attn_cols, "seq", split_axis=0, concat_axis=0, tiled=True)
    mlp_cols = lax.all_to_all(mlp_cols, "seq", split_axis=0, concat_axis=0, tiled=True)
    attn_all = lax.all_gather(attn_cols.reshape(-1, 3 * part), "dp", axis=0, tiled=True)
    attn_all = attn_all.reshape(dp, SEQ, w_rows + 8, 3 * part)
    w_qkv = attn_all[:, :, :w_rows].transpose(1, 0, 2, 3).reshape(width, 3 * part)
    gain_all = jnp.sum(attn_all[:, :, w_rows : w_rows + 4].astype(f32), axis=(0, 1))
    attn_gain_all = jnp.concatenate([gain_all[0], gain_all[1]])[None, :width]
    mlp_gain_all = jnp.concatenate([gain_all[2], gain_all[3]])[None, :width]
    rows_all = lax.all_gather(jnp.concatenate([out_weight, down_weight]), "dp", axis=0, tiled=True)
    rows_all = rows_all.reshape(dp, w_rows + d_rows, width)
    w_out = rows_all[:, :w_rows].reshape(part, width)
    w_down = rows_all[:, w_rows:].reshape(inner, width)
    mlp_all = lax.all_gather(mlp_cols.reshape(-1, 2 * inner), "dp", axis=0, tiled=True)
    mlp_all = mlp_all.reshape(dp, SEQ, w_rows, 2 * inner).transpose(1, 0, 2, 3).reshape(width, 2 * inner)
    w_gate, w_up = mlp_all[:, :inner], mlp_all[:, inner:]

    tok_rel = jnp.concatenate(gather_rel(tokens[0]))
    first_cols = first_values[0].reshape(rows, SEQ, part)
    first_rel = jnp.concatenate(
        exchange_rel([lax.dynamic_index_in_dim(first_cols, me ^ k, 1, keepdims=False) for k in range(SEQ)])
    )
    og_rel = jnp.concatenate(gather_rel(out_grad[0]))

    pairs = jnp.arange(head_width // 2, dtype=f32)
    freq = jnp.exp(pairs * (-2.0 * math.log(10000.0) / head_width))
    theta = jnp.arange(length, dtype=jnp.int32).astype(f32)[:, None] * freq[None, :]
    cos, sin = jnp.cos(theta), jnp.sin(theta)
    cos = jnp.concatenate([cos] * 4, axis=1)
    sin = jnp.concatenate([-sin, sin] * 2, axis=1)
    seg_row = segment_ids
    seg_col = segment_ids.reshape(length, 1)

    nin, q, k, v = qkv_call(me_arg, tok_rel, first_rel, w_qkv, attn_gain_all, cos, sin)
    attended, lse = attend_call(q, k, v, seg_col, seg_row)
    att = gather_rel(attended)
    wo_rel = jnp.concatenate(gather_rel(w_out))
    mid, nm, hidden, d_gate, d_up, dnm, lo, mlp_gain_part = ffn_call(
        me_arg, tok_rel, og_rel, att, wo_rel, mlp_gain_all, w_gate, w_up, w_down
    )
    blocks = lambda a: [a[i * rows : (i + 1) * rows] for i in range(SEQ)]

    dnm_own = scatter_sum(blocks(dnm))
    scale_mid = lax.rsqrt(jnp.mean(mid * mid, axis=-1, keepdims=True) + epsilon)
    unit_mid = mid * scale_mid
    pressed = dnm_own * mlp_gain_all
    d_middle = out_grad[0].astype(f32) + scale_mid * (
        pressed - unit_mid * jnp.mean(pressed * unit_mid, axis=-1, keepdims=True)
    )
    d_branch = by_index(me, gather_rel(d_middle.astype(bf16))).reshape(length, width)
    layer_out = (mid + scatter_sum(blocks(lo))).astype(bf16)

    d_attended = mul(d_branch, w_out, 1, 1).astype(bf16)
    g_out = mul(attended, d_branch, 0, 0)
    dq, dk, dv = attend_back_call(q, k, v, d_attended, lse, seg_col, seg_row, cos, sin)
    d_qkv = jnp.concatenate([dq, dk, dv], axis=1)

    g_gate = mul(nm, d_gate, 0, 0)
    g_up = mul(nm, d_up, 0, 0)
    g_down = mul(hidden, og_rel, 0, 0)
    g_qkv = mul(nin, d_qkv, 0, 0)
    dnin = mul(d_qkv, w_qkv, 1, 1)
    tok_abs = by_index(me, [tok_rel[i * rows : (i + 1) * rows] for i in range(SEQ)]).reshape(length, width).astype(f32)
    unit_abs = tok_abs * lax.rsqrt(jnp.mean(tok_abs * tok_abs, axis=-1, keepdims=True) + epsilon)
    attn_gain_part = jnp.sum(dnin * unit_abs, axis=0, keepdims=True)
    dnin_rel = [lax.dynamic_slice_in_dim(dnin.astype(bf16), (me ^ i) * rows, rows, 0) for i in range(SEQ)]
    dnin_own = scatter_sum(dnin_rel)
    x = tokens[0].astype(f32)
    scale_in = lax.rsqrt(jnp.mean(x * x, axis=-1, keepdims=True) + epsilon)
    unit_in = x * scale_in
    pressed = dnin_own * attn_gain_all
    token_grad = d_middle + scale_in * (pressed - unit_in * jnp.mean(pressed * unit_in, axis=-1, keepdims=True))

    dv_back = exchange_rel([lax.dynamic_slice_in_dim(dv, (me ^ i) * rows, rows, 0) for i in range(SEQ)])
    dv_own = by_index(me, list(dv_back)).transpose(1, 0, 2).reshape(rows, width)
    value_grad_out = value_grad_acc[0] + dv_own.astype(f32)

    def by_owner(grad):
        return grad.astype(bf16).reshape(SEQ, dp, w_rows, -1).transpose(1, 0, 2, 3)

    def gain_rows(gain):
        return gain.astype(bf16).reshape(SEQ, dp, w_rows).transpose(1, 0, 2)

    gu = jnp.concatenate([by_owner(g_gate), by_owner(g_up)], axis=3)
    gu = lax.psum_scatter(gu.reshape(dp * SEQ * w_rows, 2 * inner), "dp", scatter_dimension=0, tiled=True)
    od = jnp.concatenate(
        [g_out.astype(bf16).reshape(dp, w_rows, width), g_down.astype(bf16).reshape(dp, d_rows, width)], axis=1
    )
    od = lax.psum_scatter(od.reshape(-1, width), "dp", scatter_dimension=0, tiled=True)
    qkv_rows = by_owner(g_qkv)
    gain_parts = jnp.stack([gain_rows(attn_gain_part), gain_rows(mlp_gain_part)], axis=2)
    gain_parts = jnp.pad(gain_parts, ((0, 0), (0, 0), (0, 6), (0, 3 * part - w_rows)))
    qkv_rows = jnp.concatenate([qkv_rows, gain_parts], axis=2).reshape(-1, 3 * part)
    qkv_rows = lax.psum_scatter(qkv_rows, "dp", scatter_dimension=0, tiled=True)
    gu = lax.all_to_all(gu.reshape(SEQ, w_rows, 2 * inner), "seq", split_axis=0, concat_axis=0, tiled=True)
    qkv_rows = lax.all_to_all(
        qkv_rows.reshape(SEQ, w_rows + 8, 3 * part), "seq", split_axis=0, concat_axis=0, tiled=True
    )

    def assemble(pieces):
        return pieces.astype(f32).transpose(1, 0, 2).reshape(w_rows, -1)

    g_q, g_k, g_v = [assemble(qkv_rows[:, :w_rows, i * part : (i + 1) * part]) for i in range(3)]
    gain_sums = jnp.sum(qkv_rows[:, w_rows : w_rows + 2, :w_rows].astype(f32), axis=0)
    return (
        layer_out[None],
        token_grad.astype(bf16)[None],
        value_grad_out[None],
        g_q,
        g_k,
        g_v,
        od[:w_rows].astype(f32),
        gain_sums[0],
        assemble(gu[:, :, :inner]),
        assemble(gu[:, :, inner:]),
        od[w_rows:].astype(f32),
        gain_sums[1],
    )


def solution(mesh):
    token = P("dp", "seq", None)
    weight = P(("seq", "dp"), None)
    gain = P(("seq", "dp"))
    return jax.shard_map(
        body,
        mesh=mesh,
        in_specs=(token, token, token, P("dp", None), weight, weight, weight, weight, gain, weight, weight, weight, gain, token),
        out_specs=(token, token, token, weight, weight, weight, weight, gain, weight, weight, weight, gain),
        check_vma=False,
    )
```

```python
import functools
import math

import jax
import jax.numpy as jnp
from jax import lax
from jax.experimental import pallas as pl
from jax.experimental.pallas import tpu as pltpu
from jax.sharding import PartitionSpec as P

HEADS = 16
DOC_MOST = 512
SEQ = 4
BLOCK = 256

epsilon = 1e-06
masked_value = -1e30
bf16 = jnp.bfloat16
f32 = jnp.float32


def mul(a, b, ca, cb):
    return lax.dot_general(a, b, (((ca,), (cb,)), ((), ())), preferred_element_type=f32)


def params(mib):
    return pltpu.CompilerParams(vmem_limit_bytes=mib << 20)


VMEM = pl.BlockSpec(memory_space=pltpu.VMEM)
SMEM = pl.BlockSpec(memory_space=pltpu.SMEM)


def fixed(shape):
    return pl.BlockSpec(shape, lambda *_: (0,) * len(shape), pipeline_mode=pl.Buffered(1))


def sync(*values):
    return lax.optimization_barrier(values)


def after(value, *earlier):
    return lax.optimization_barrier((value, *earlier))[0]


def half_swap(field):
    lanes = field.shape[-1]
    lane = lax.broadcasted_iota(jnp.int32, field.shape, 1)
    up = pltpu.roll(field, lanes - 32, 1)
    down = pltpu.roll(field, 32, 1)
    return jnp.where(lane % 64 < 32, up, down)


def qkv_kernel(me_ref, tok_ref, first_ref, w_ref, gain_ref, cos_ref, sin_ref, nin_ref, q_ref, k_ref, v_ref):
    x = tok_ref[...].astype(f32)
    scale = lax.rsqrt(jnp.mean(x * x, axis=-1, keepdims=True) + epsilon)
    nin = (x * scale * gain_ref[...]).astype(bf16)
    nin_ref[...] = nin
    lin = mul(nin, w_ref[...], 1, 0)
    cos = jnp.concatenate([cos_ref[...]] * 2, axis=1)
    sin = jnp.concatenate([sin_ref[...]] * 2, axis=1)
    part = lin.shape[1] // 3
    q = lin[:, :part]
    q_ref[...] = ((q * cos + half_swap(q) * sin).astype(bf16).astype(f32) * 0.125).astype(bf16)
    k = lin[:, part : 2 * part]
    k_ref[...] = (k * cos + half_swap(k) * sin).astype(bf16)
    v_ref[...] = (0.5 * lin[:, 2 * part :] + 0.5 * first_ref[...].astype(f32)).astype(bf16)


def qkv_call(me, tok, first, w, gain, cos, sin):
    length, width = tok.shape
    rows = length // SEQ
    part = w.shape[1] // 3
    here = lambda k, m: (m[0] ^ k, 0)
    rel = lambda k, m: (k, 0)
    return pl.pallas_call(
        qkv_kernel,
        name="qkv",
        grid_spec=pltpu.PrefetchScalarGridSpec(
            num_scalar_prefetch=1,
            grid=(SEQ,),
            in_specs=[
                pl.BlockSpec((rows, width), rel),
                pl.BlockSpec((rows, part), rel),
                fixed(w.shape),
                fixed((1, width)),
                pl.BlockSpec((rows, 128), here),
                pl.BlockSpec((rows, 128), here),
            ],
            out_specs=[pl.BlockSpec((rows, width), here)] + [pl.BlockSpec((rows, part), here)] * 3,
        ),
        out_shape=[jax.ShapeDtypeStruct((length, width), bf16)]
        + [jax.ShapeDtypeStruct((length, part), bf16)] * 3,
        compiler_params=params(16),
    )(me, tok, first, w, gain, cos, sin)


def key_range(block):
    return max(0, block * BLOCK - (DOC_MOST // BLOCK) * BLOCK), (block + 1) * BLOCK


def column_of(row_ref):
    return jnp.broadcast_to(row_ref[...].astype(f32), (8, row_ref.shape[1])).T[:, :1]


def allowed_pairs(seg_col, seg_row, block, low, high):
    keys = lax.broadcasted_iota(jnp.int32, (high - low, BLOCK), 0) + low
    rows = lax.broadcasted_iota(jnp.int32, (high - low, BLOCK), 1) + block * BLOCK
    row = seg_row[:, block * BLOCK : (block + 1) * BLOCK].astype(f32)
    return (seg_col[low:high, :] == row) & (keys <= rows)


def head_lanes(field, head):
    lane = lax.broadcasted_iota(jnp.int32, field.shape, 1)
    return jnp.where(lane // 64 == head, field, jnp.zeros_like(field))


def half_rows(head):
    return pl.ds(pl.multiple_of(head * 64, 64), 64)


def attend_kernel(q_ref, k_ref, v_ref, seg_row, o_ref, lse_ref, turned, turned_out):
    length = q_ref.shape[0]
    seg_col = column_of(seg_row)
    turned[...] = v_ref[...].astype(f32).T.astype(bf16)

    def one_head(head, carry):
        for block in range(length // BLOCK):
            low, high = key_range(block)
            allowed = allowed_pairs(seg_col, seg_row, block, low, high)
            here = slice(block * BLOCK, (block + 1) * BLOCK)
            scores = mul(k_ref[low:high, :], head_lanes(q_ref[here, :], head), 1, 1)
            scores = jnp.where(allowed, scores, masked_value)
            top = jnp.max(scores, axis=0, keepdims=True)
            expo = jnp.exp(scores - top)
            total = jnp.sum(expo, axis=0, keepdims=True)
            probs = (expo * (1.0 / total)).astype(bf16)
            turned_out[half_rows(head), here] = mul(turned[half_rows(head), low:high], probs, 1, 0)
            lse_ref[0, pl.ds(head, 1), here] = top + jnp.log(total)
        return carry

    lax.fori_loop(0, 2, one_head, 0)
    for block in range(length // BLOCK):
        here = slice(block * BLOCK, (block + 1) * BLOCK)
        o_ref[here, :] = turned_out[:, here].T.astype(bf16)


def attend_call(q, k, v, seg_row):
    length, part = q.shape
    pairs = part // 128
    lanes = pl.BlockSpec((length, 128), lambda p: (0, p))
    return pl.pallas_call(
        attend_kernel,
        name="attend",
        grid=(pairs,),
        in_specs=[lanes] * 3 + [fixed((1, length))],
        out_specs=[lanes, pl.BlockSpec((1, 2, length), lambda p: (p, 0, 0))],
        out_shape=[jax.ShapeDtypeStruct((length, part), bf16), jax.ShapeDtypeStruct((pairs, 2, length), f32)],
        scratch_shapes=[pltpu.VMEM((128, length), bf16), pltpu.VMEM((128, length), f32)],
        compiler_params=params(24),
    )(q, k, v, seg_row)


def attend_back_kernel(
    dp, pieces, place_ref, q_ref, k_ref, v_ref, d0, d1, d2, d3, lse_ref, seg_row, cos_ref, sin_ref, nin_ref,
    *refs,
):
    outs, (da_ref, dk_sum, dv_sum, work, turned, turned_dq) = refs[:-6], refs[-6:]
    *along, d_ref = outs[: len(outs) - 2 * pieces]
    outs = outs[len(outs) - 2 * pieces :]
    length = q_ref.shape[0]
    rows = d0.shape[0]
    for k, ref in enumerate((d0, d1, d2, d3)):
        da_ref[pl.ds(pl.multiple_of((place_ref[0] ^ k) * rows, rows), rows), :] = ref[...]
    seg_col = column_of(seg_row)
    dk_sum[...] = jnp.zeros_like(dk_sum)
    dv_sum[...] = jnp.zeros_like(dv_sum)
    turned[...] = k_ref[...].astype(f32).T.astype(bf16)

    def one_head(head, carry):
        for block in range(length // BLOCK):
            low, high = key_range(block)
            allowed = allowed_pairs(seg_col, seg_row, block, low, high)
            here = slice(block * BLOCK, (block + 1) * BLOCK)
            q_head = head_lanes(q_ref[here, :], head)
            da_head = head_lanes(da_ref[here, :], head)
            scores = mul(k_ref[low:high, :], q_head, 1, 1)
            probs = jnp.where(allowed, jnp.exp(scores - lse_ref[0, pl.ds(head, 1), here]), 0.0)
            d_probs = mul(v_ref[low:high, :], da_head, 1, 1)
            delta = jnp.sum(probs * d_probs, axis=0, keepdims=True)
            d_scores = (probs * (d_probs - delta)).astype(bf16)
            turned_dq[half_rows(head), here] = mul(turned[half_rows(head), low:high], d_scores, 1, 0)
            dk_sum[low:high, :] += mul(d_scores, q_head, 1, 0)
            dv_sum[low:high, :] += mul(probs.astype(bf16), da_head, 1, 0)
        return carry

    lax.fori_loop(0, 2, one_head, 0)
    for block in range(length // BLOCK):
        here = slice(block * BLOCK, (block + 1) * BLOCK)
        dq = turned_dq[:, here].T * 0.125
        d_ref[here, :128] = (dq * cos_ref[here, :] - half_swap(dq) * sin_ref[here, :]).astype(bf16)
    dk = dk_sum[...]
    d_ref[:, 128:256] = (dk * cos_ref[...] - half_swap(dk) * sin_ref[...]).astype(bf16)
    d_ref[:, 256:] = (0.5 * dv_sum[...]).astype(bf16)
    if not outs:
        return
    kept_ref, sent_ref = outs
    part = work.shape[0]
    w_rows = part // dp
    first = 0
    if along:
        first = along[0].shape[0]
        sent_ref[:first, :] = along[0][...]
    for s in range(SEQ):
        work[...] = mul(nin_ref[:, s * part : (s + 1) * part], d_ref[...], 0, 0).astype(bf16)
        for slot in range(dp):
            here = pl.ds(pl.multiple_of(owner_index(place_ref, dp, slot) * w_rows, w_rows), w_rows)
            for t in range(3):
                at = (s * 3 + t) * w_rows
                piece = work[here, t * 128 : t * 128 + 128]
                if slot < dp // 2:
                    kept_ref[slot, at : at + w_rows, :] = piece
                else:
                    at += first + (slot - dp // 2) * kept_ref.shape[1]
                    sent_ref[at : at + w_rows, :] = piece


def attend_back_call(pair, place, q, k, v, da, lse, seg_row, cos, sin, nin, dp, pieces, along=()):
    length, width = nin.shape
    part = width // SEQ
    lanes = pl.BlockSpec((length, 128), lambda _: (0, pair), pipeline_mode=pl.Buffered(1))
    outs = [(length, 384)]
    if pieces:
        rows = 3 * width // dp
        outs += [(dp // 2, rows, 128), (sum(x.shape[0] for x in along) + dp // 2 * rows, 128)]
    return pl.pallas_call(
        functools.partial(attend_back_kernel, dp, pieces),
        name="attend_back",
        grid=(1,),
        in_specs=[SMEM]
        + [lanes] * 3
        + [pl.BlockSpec((length // SEQ, 128), lambda _: (0, pair), pipeline_mode=pl.Buffered(1))] * 4
        + [pl.BlockSpec((1, 2, length), lambda _: (pair, 0, 0)), fixed((1, length))]
        + [fixed((length, 128))] * 2
        + [fixed(nin.shape)]
        + [fixed(x.shape) for x in along],
        out_specs=[fixed(x) for x in outs],
        out_shape=[jax.ShapeDtypeStruct(x, bf16) for x in outs],
        scratch_shapes=[pltpu.VMEM((length, 128), bf16)]
        + [pltpu.VMEM((length, 128), f32)] * 2
        + [pltpu.VMEM((part, 384), bf16), pltpu.VMEM((128, length), bf16), pltpu.VMEM((128, length), f32)],
        compiler_params=params(60),
    )(place, q, k, v, *da, lse, seg_row, cos, sin, nin, *along)


def main_lanes(inner):
    return inner // 128 * 128


def pack_attn_kernel(
    place_ref, q_ref, k_ref, v_ref, o_ref, d_ref, ag_ref, mg_ref, tok_ref, c0, c1, c2, c3, orows_ref, drows_ref, *halves_refs
):
    me, owner = place_ref[0], place_ref[1]
    w_rows, width = q_ref.shape
    part = width // SEQ
    lane = lax.broadcasted_iota(jnp.int32, (1, 128), 1)
    spot = lane // w_rows == owner % (128 // w_rows)

    def spread(gain):
        return jnp.where(spot, jnp.concatenate([gain[...].astype(f32)] * (128 // w_rows), axis=1), 0.0)

    row = lax.broadcasted_iota(jnp.int32, (16, 128), 0)
    gains = jnp.where(row == 0, spread(ag_ref), jnp.where(row == 1, spread(mg_ref), 0.0)).astype(bf16)
    for k, out in enumerate((c0, c1, c2, c3)):
        at = 0
        for ref in (q_ref, k_ref, v_ref):
            for t in range(part // 128):
                lanes = pl.ds(pl.multiple_of((me ^ k) * part + t * 128, 128), 128)
                out[at : at + w_rows, :] = ref[:, lanes]
                at += w_rows
        out[at : at + 16, :] = gains
    for ref, out in ((o_ref, orows_ref), (d_ref, drows_ref)):
        rows = ref.shape[0]
        for t in range(width // 128):
            out[t * rows : (t + 1) * rows, :] = ref[:, t * 128 : t * 128 + 128]
    for i, out in enumerate(halves_refs):
        rows = out.shape[0]
        out[...] = tok_ref[i * rows : (i + 1) * rows, :]


def pack_attn(place, wq, wk, wv, wo, wd, attn_gain, mlp_gain, tok):
    w_rows, width = wq.shape
    tiles = width // 128
    shapes = [(3 * tiles // SEQ * w_rows + 16, 128)] * 4 + [(tiles * w_rows, 128), (tiles * wd.shape[0], 128)]
    shapes += [(tok.shape[0] // 2, width)] * 2
    return pl.pallas_call(
        pack_attn_kernel,
        name="pack_attn",
        grid=(1,),
        in_specs=[SMEM] + [fixed(w.shape) for w in (wq, wk, wv, wo, wd)] + [fixed((1, w_rows))] * 2 + [fixed(tok.shape)],
        out_specs=[fixed(x) for x in shapes],
        out_shape=[jax.ShapeDtypeStruct(x, bf16) for x in shapes],
        compiler_params=params(60),
    )(place, wq, wk, wv, wo, wd, attn_gain[None], mlp_gain[None], tok)


def pack_ffn_kernel(place_ref, g_ref, u_ref, c0, c1, c2, c3):
    me = place_ref[0]
    w_rows = g_ref.shape[0]
    inner = g_ref.shape[1] // SEQ
    main = main_lanes(inner)
    for s in range(SEQ):
        gate, up = g_ref[:, s * inner : (s + 1) * inner], u_ref[:, s * inner : (s + 1) * inner]
        tiles = [field[:, t * 128 : t * 128 + 128] for field in (gate, up) for t in range(main // 128)]
        tiles.append(jnp.concatenate([gate[:, main:], up[:, main:]], axis=1))
        for k, out in enumerate((c0, c1, c2, c3)):

            @pl.when(me ^ k == s)
            def _():
                for t, tile in enumerate(tiles):
                    out[t * w_rows : (t + 1) * w_rows, :] = tile


def pack_ffn(place, wg, wu):
    w_rows = wg.shape[0]
    inner = wg.shape[1] // SEQ
    return pl.pallas_call(
        pack_ffn_kernel,
        name="pack_ffn",
        grid=(1,),
        in_specs=[SMEM] + [fixed(w.shape) for w in (wg, wu)],
        out_specs=[fixed((2 * inner // 128 * w_rows, 128))] * 4,
        out_shape=[jax.ShapeDtypeStruct((2 * inner // 128 * w_rows, 128), bf16)] * 4,
        compiler_params=params(60),
    )(place, wg, wu)


def source_of(place_ref, dp, slot):
    groups = dp // 2
    b, j = slot // groups, slot % groups
    z, y = place_ref[2] // 2, place_ref[2] % 2
    return ((z + groups - j) % groups) * 2 + (y ^ b)


def assemble_attn_kernel(place_ref, *refs):
    dp = len(refs) - 4
    pieces, (w_ref, wo_ref, ag_ref, mg_ref) = refs[:dp], refs[dp:]
    width, lanes = w_ref.shape
    w_rows = width // (SEQ * dp)
    part = width // SEQ
    chunk = lanes // 128 * w_rows + 16
    ag_ref[...] = jnp.zeros_like(ag_ref)
    mg_ref[...] = jnp.zeros_like(mg_ref)
    for slot, piece in enumerate(pieces):
        src = source_of(place_ref, dp, slot)
        for k in range(SEQ):
            s = place_ref[0] ^ k
            row = pl.multiple_of(s * part + src * w_rows, w_rows)
            for t in range(lanes // 128):
                at = k * chunk + t * w_rows
                w_ref[pl.ds(row, w_rows), t * 128 : t * 128 + 128] = piece[at : at + w_rows, :]
            gains = piece[(k + 1) * chunk - 16 : (k + 1) * chunk, :].astype(f32)
            tile = (s * dp + src) * w_rows // 128
            ag_ref[pl.ds(tile, 1), :] += gains[0:1, :]
            mg_ref[pl.ds(tile, 1), :] += gains[1:2, :]
        row = pl.multiple_of(src * w_rows, w_rows)
        for t in range(width // 128):
            at = SEQ * chunk + t * w_rows
            wo_ref[pl.ds(row, w_rows), t * 128 : t * 128 + 128] = piece[at : at + w_rows, :]


def assemble_attn(place, pieces, width):
    shapes = [(width, 3 * width // SEQ), (width // SEQ, width), (width // 128, 128), (width // 128, 128)]
    return pl.pallas_call(
        assemble_attn_kernel,
        name="assemble_attn",
        grid=(1,),
        in_specs=[SMEM] + [fixed(x.shape) for x in pieces],
        out_specs=[fixed(x) for x in shapes],
        out_shape=[jax.ShapeDtypeStruct(x, t) for x, t in zip(shapes, (bf16, bf16, f32, f32))],
        compiler_params=params(12),
    )(place, *pieces)


def assemble_rows_kernel(place_ref, *refs):
    dp = len(refs) - 1
    pieces, out_ref = refs[:dp], refs[dp]
    count = out_ref.shape[0] // dp
    for slot, piece in enumerate(pieces):
        row = pl.multiple_of(source_of(place_ref, dp, slot) * count, 8)
        for t in range(out_ref.shape[1] // 128):
            out_ref[pl.ds(row, count), t * 128 : t * 128 + 128] = piece[t * count : (t + 1) * count, :]


def assemble_rows(place, pieces, width, inner):
    return pl.pallas_call(
        assemble_rows_kernel,
        name="assemble_rows",
        grid=(1,),
        in_specs=[SMEM] + [fixed(x.shape) for x in pieces],
        out_specs=fixed((inner, width)),
        out_shape=jax.ShapeDtypeStruct((inner, width), bf16),
        compiler_params=params(12),
    )(place, *pieces)


def ffn_kernel(me_ref, tok_ref, og_ref, a0, a1, a2, a3, wo0, wo1, wo2, wo3, gain_ref, w_ref, wd_ref, *outs):
    nm_ref, hid_ref, dgu_ref, mid_ref, *lists = outs
    step = pl.program_id(0)
    if len(w_ref.shape) == 3:
        pieces, w_ref = w_ref, lists.pop()
        dp = pieces.shape[0]
        width, lanes = w_ref.shape
        w_rows = width // (SEQ * dp)
        chunk = lanes // 128 * w_rows

        @pl.when(step == 0)
        def _():
            for k in range(SEQ):
                for src in range(dp):
                    row = pl.multiple_of((me_ref[0] ^ k) * (width // SEQ) + src * w_rows, w_rows)
                    for t in range(lanes // 128):
                        at = k * chunk + t * w_rows
                        w_ref[pl.ds(row, w_rows), t * 128 : t * 128 + 128] = pieces[src, at : at + w_rows, :]

    mid = tok_ref[...].astype(f32)
    inner = wd_ref.shape[0]
    main = main_lanes(inner)
    for a, wo in zip((a0, a1, a2, a3), (wo0, wo1, wo2, wo3)):
        mid = mid + mul(a[...], wo[...], 1, 0)
    scale = lax.rsqrt(jnp.mean(mid * mid, axis=-1, keepdims=True) + epsilon)
    nm = (mid * scale * gain_ref[...]).astype(bf16)
    nm_ref[...] = nm
    d_hidden = mul(og_ref[...], wd_ref[...], 1, 1)
    both = mul(nm, w_ref[...], 1, 0)

    def gated(gate, up, grad):
        sig = jax.nn.sigmoid(gate)
        silu = gate * sig
        return (
            (silu * up).astype(bf16),
            (grad * up * (sig * (1.0 + gate * (1.0 - sig)))).astype(bf16),
            (grad * silu).astype(bf16),
        )

    hid_main, dg_main, du_main = gated(both[:, :main], both[:, main : 2 * main], d_hidden[:, :main])
    last = both[:, 2 * main :]
    hid_last, dg_last, du_last = gated(last[:, : inner - main], last[:, inner - main :], d_hidden[:, main:])
    hid_ref[:, :main] = hid_main
    hid_ref[:, main:] = hid_last
    dgu_ref[:, :main] = dg_main
    dgu_ref[:, main : 2 * main] = du_main
    dgu_ref[:, 2 * main :] = jnp.concatenate([dg_last, du_last], axis=1)
    dnm = mul(dgu_ref[...], w_ref[...], 1, 1).astype(bf16)
    lo = mul(hid_ref[...], wd_ref[...], 1, 0).astype(bf16)
    dnm_kept, dnm_sent, lo_kept, lo_sent = lists
    rows = tok_ref.shape[0]
    for k in range(SEQ):

        @pl.when(step == SEQ - 1 - k)
        def _():
            here = slice(k // 2 * rows, (k // 2 + 1) * rows)
            (dnm_sent if k % 2 else dnm_kept)[here, :] = dnm
            (lo_sent if k % 2 else lo_kept)[here, :] = lo

    @pl.when(step == SEQ - 1)
    def _():
        mid_ref[...] = mid


def ffn_call(me, tok, og, att, wo, gain, w, wd):
    length, width = tok.shape
    rows = length // SEQ
    inner = wd.shape[0]
    part = att[0].shape[1]
    rel = lambda k, m: (SEQ - 1 - k, 0)
    here = lambda k, m: (m[0] ^ (SEQ - 1 - k), 0)
    return pl.pallas_call(
        ffn_kernel,
        name="ffn",
        grid_spec=pltpu.PrefetchScalarGridSpec(
            num_scalar_prefetch=1,
            grid=(SEQ,),
            in_specs=[pl.BlockSpec((rows, width), rel)] * 2
            + [pl.BlockSpec((rows, part), here)] * 4
            + [fixed(x.shape) for x in wo]
            + [fixed((1, width)), fixed(w.shape), fixed(wd.shape)],
            out_specs=[
                pl.BlockSpec((rows, width), rel),
                pl.BlockSpec((rows, inner), rel),
                pl.BlockSpec((rows, 2 * inner), rel),
                fixed((rows, width)),
            ]
            + [fixed((2 * rows, width))] * 4,
            scratch_shapes=[pltpu.VMEM((width, 2 * inner), bf16)] * (w.ndim - 2),
        ),
        out_shape=[
            jax.ShapeDtypeStruct((length, width), bf16),
            jax.ShapeDtypeStruct((length, inner), bf16),
            jax.ShapeDtypeStruct((length, 2 * inner), bf16),
            jax.ShapeDtypeStruct((rows, width), f32),
        ]
        + [jax.ShapeDtypeStruct((2 * rows, width), bf16)] * 4,
        compiler_params=params(60),
    )(me, tok, og, *att, *wo, gain, w, wd)


def owner_index(place_ref, dp, slot):
    groups = dp // 2
    b, j = slot // groups, slot % groups
    z, y = place_ref[2] // 2, place_ref[2] % 2
    return ((z + j) % groups) * 2 + (y ^ b)


def columns_grad_kernel(place_ref, act_ref, grad_ref, *refs):
    outs, work = refs[:-1], refs[-1]
    dp = len(outs)
    work[...] = mul(act_ref[...], grad_ref[...], 0, 0).astype(bf16)
    w_rows = work.shape[0] // dp
    for slot, ref in enumerate(outs):
        here = pl.ds(pl.multiple_of(owner_index(place_ref, dp, slot) * w_rows, w_rows), w_rows)
        for t in range(work.shape[1] // 128):
            ref[t * w_rows : (t + 1) * w_rows, :] = work[here, t * 128 : t * 128 + 128]


def columns_grad_plain(act, grad, dp):
    width, lanes = act.shape[1], grad.shape[1]
    w_rows = width // (SEQ * dp)
    grad = mul(act, grad, 0, 0).astype(bf16).reshape(SEQ, dp, w_rows, lanes // 128, 128)
    return grad.transpose(1, 0, 3, 2, 4).reshape(dp, -1, 128)


def columns_grad(place, act, grad, dp):
    length, width = act.shape
    lanes = grad.shape[1]
    part = width // SEQ
    chunk = lanes // 128 * (part // dp)
    return pl.pallas_call(
        columns_grad_kernel,
        name="columns_grad",
        grid_spec=pltpu.PrefetchScalarGridSpec(
            num_scalar_prefetch=1,
            grid=(SEQ,),
            in_specs=[pl.BlockSpec((length, part), lambda s, m: (0, s)), fixed(grad.shape)],
            out_specs=[pl.BlockSpec((chunk, 128), lambda s, m: (s, 0))] * dp,
            scratch_shapes=[pltpu.VMEM((part, lanes), bf16)],
        ),
        out_shape=[jax.ShapeDtypeStruct((SEQ * chunk, 128), bf16)] * dp,
        compiler_params=params(60),
    )(place, act, grad)


def out_grad_kernel(place_ref, act_ref, d0, d1, d2, d3, kept_ref, sent_ref, work):
    rows = d0.shape[0]
    total = 0.0
    for k, ref in enumerate((d0, d1, d2, d3)):
        act = act_ref[pl.ds(pl.multiple_of((place_ref[0] ^ k) * rows, rows), rows), :]
        total = total + mul(act, ref[...], 0, 0)
    work[...] = total.astype(bf16)
    dp = 2 * kept_ref.shape[0]
    count = work.shape[0] // dp
    at = 0
    for slot in range(dp):
        here = pl.ds(pl.multiple_of(owner_index(place_ref, dp, slot) * count, count), count)
        for t in range(work.shape[1] // 128):
            piece = work[here, t * 128 : t * 128 + 128]
            if slot < dp // 2:
                kept_ref[slot, t * count : (t + 1) * count, :] = piece
            else:
                sent_ref[at : at + count, :] = piece
                at += count


def out_projection_grad(place, act, d_branch, dp):
    width = d_branch[0].shape[1]
    part = act.shape[1]
    shape = (dp // 2, width // 128 * (part // dp), 128)
    sent = (shape[0] * shape[1], 128)
    return pl.pallas_call(
        out_grad_kernel,
        name="out_projection_grad",
        grid=(1,),
        in_specs=[SMEM, fixed(act.shape)] + [fixed(x.shape) for x in d_branch],
        out_specs=[fixed(shape), fixed(sent)],
        out_shape=[jax.ShapeDtypeStruct(shape, bf16), jax.ShapeDtypeStruct(sent, bf16)],
        scratch_shapes=[pltpu.VMEM((part, width), bf16)],
        compiler_params=params(24),
    )(place, act, *d_branch)


def down_grad_kernel(act_ref, grad_ref, out_ref):
    out_ref[...] = mul(act_ref[...], grad_ref[...], 0, 0).astype(bf16)


def down_grad(act, grad):
    length, width = grad.shape
    step = 256
    return pl.pallas_call(
        down_grad_kernel,
        name="down_grad",
        grid=(width // step,),
        in_specs=[fixed(act.shape), pl.BlockSpec((length, step), lambda c: (0, c))],
        out_specs=pl.BlockSpec((act.shape[1], step), lambda c: (0, c)),
        out_shape=jax.ShapeDtypeStruct((act.shape[1], width), bf16),
        compiler_params=params(60),
    )(act, grad)


def simple(kernel, name, args, outs, limit=24):
    return pl.pallas_call(
        kernel,
        name=name,
        grid=(1,),
        in_specs=[SMEM if x.dtype == jnp.int32 else fixed(x.shape) for x in args],
        out_specs=[fixed(x.shape) for x in outs],
        out_shape=outs,
        compiler_params=params(limit),
    )(*args)


def shaped(dtype, *shape):
    return jax.ShapeDtypeStruct(shape, dtype)


def sum_kernel(*refs):
    *ins, out = refs
    out[...] = sum(x[...].astype(f32) for x in ins).astype(out.dtype)


def total(*pieces):
    return simple(sum_kernel, "total", pieces, [shaped(bf16, *pieces[0].shape)])[0]


def halves_kernel(kept_ref, got_ref, near_ref, far_ref):
    rows = near_ref.shape[0]
    near_ref[...] = kept_ref[:rows, :].astype(f32) + got_ref[:rows, :].astype(f32)
    far_ref[...] = (kept_ref[rows:, :].astype(f32) + got_ref[rows:, :].astype(f32)).astype(bf16)


def halves(kept, got):
    rows, width = kept.shape[0] // 2, kept.shape[1]
    return simple(halves_kernel, "halves", (kept, got), [shaped(f32, rows, width), shaped(bf16, rows, width)])


def slots_kernel(kept_ref, got_ref, *outs):
    count = kept_ref.shape[1]
    at = got_ref.shape[0] - len(outs) * count
    for j, out in enumerate(outs):
        got = got_ref[at + j * count : at + (j + 1) * count, :]
        out[...] = (kept_ref[j].astype(f32) + got.astype(f32)).astype(out.dtype)


def slots(kept, got):
    shape = kept.shape[1:]
    outs = [shaped(f32, *shape)] + [shaped(bf16, *shape)] * (kept.shape[0] - 1)
    return simple(slots_kernel, "slots", (kept, got), outs)


def back_through_norm(grad, field, gain):
    scale = lax.rsqrt(jnp.mean(field * field, axis=-1, keepdims=True) + epsilon)
    unit = field * scale
    pressed = grad * gain
    return scale * (pressed - unit * jnp.mean(pressed * unit, axis=-1, keepdims=True))


def branch_kernel(near_ref, far_ref, mid_ref, og_ref, gain_ref, w0, w1, w2, w3, d_mid_ref, d_ref, a0, a1, a2, a3):
    grad = near_ref[...] + far_ref[...].astype(f32)
    d_mid = og_ref[...].astype(f32) + back_through_norm(grad, mid_ref[...], gain_ref[...])
    d_mid_ref[...] = d_mid
    d_branch = d_mid.astype(bf16)
    d_ref[...] = d_branch
    for w, a in ((w0, a0), (w1, a1), (w2, a2), (w3, a3)):
        a[...] = mul(d_branch, w[...], 1, 1).astype(bf16)


def token_grad_kernel(near_ref, far_ref, tok_ref, gain_ref, d_mid_ref, out_ref):
    grad = near_ref[...] + far_ref[...].astype(f32)
    out_ref[...] = (d_mid_ref[...] + back_through_norm(grad, tok_ref[...].astype(f32), gain_ref[...])).astype(bf16)


def cut_kernel(me_ref, *refs):
    ins, d_ref, (mine_ref, near_ref, far_ref) = refs[:-4], refs[-4], refs[-3:]
    groups = [ins[:4], ins[4:8], ins[8:]]
    count = far_ref.shape[0] - 2 * mine_ref.shape[0]
    far_ref[2 * mine_ref.shape[0] :, :] = d_ref[pl.ds(pl.multiple_of(((me_ref[0] >> 1) ^ 1) * count, count), count), 256:]
    me = me_ref[0]
    at = 0
    for pieces in groups:
        chunk = pieces[0].shape[0] // SEQ

        def chunk_of(s):
            here = pl.ds(pl.multiple_of(s * chunk, 8), chunk)
            return sum(x[here, :].astype(f32) for x in pieces).astype(bf16)

        mine_ref[at : at + chunk, :] = chunk_of(me)
        near_ref[at : at + chunk, :] = chunk_of(me ^ 1)
        for core in range(2):
            row = core * mine_ref.shape[0] + at
            far_ref[row : row + chunk, :] = chunk_of(((me >> 1) ^ 1) * 2 + core)
        at += chunk


def cut(me, attn, ffn, d_pair):
    rows = (attn[0][0].shape[0] * 2 + ffn[0].shape[0]) // SEQ
    outs = [shaped(bf16, n, 128) for n in (rows, rows, 2 * rows + d_pair.shape[0] // 2)]
    return simple(cut_kernel, "cut", (me, *attn[0], *attn[1], *ffn, d_pair), outs)


def relay_kernel(me_ref, near, far, d0_ref, d1_ref, far0_ref, out_ref):
    me = me_ref[0]
    core = (me & 1) ^ 1
    count = near.shape[0]
    out_ref[:count, :] = near[...]
    out_ref[count : 2 * count, :] = far[pl.ds(pl.multiple_of(core * count, 8), count), :]
    at = 2 * count
    rows = far0_ref.shape[0] // 2
    first = pl.multiple_of((me ^ 1) * rows, rows)
    for d_ref, far_ref, row in ((d0_ref, far0_ref, 0), (d1_ref, far, 2 * count)):
        out_ref[at : at + rows, :] = d_ref[pl.ds(first, rows), 256:]
        out_ref[at + rows : at + 2 * rows, :] = far_ref[pl.ds(pl.multiple_of(row + core * rows, 8), rows), :]
        at += 2 * rows


def value_grad_kernel(me_ref, acc_ref, d0_ref, d1_ref, far0_ref, far, got_ref, out_ref):
    me = me_ref[0]
    rows = acc_ref.shape[0]
    first = pl.multiple_of(me * rows, rows)
    at = far.shape[0] - 2 * rows

    for p, (d_ref, far_ref, row) in enumerate(((d0_ref, far0_ref, 0), (d1_ref, far, at))):
        pieces = (
            d_ref[pl.ds(first, rows), 256:],
            got_ref[at : at + rows, :],
            far_ref[pl.ds(pl.multiple_of(row + (me & 1) * rows, 8), rows), :],
            got_ref[at + rows : at + 2 * rows, :],
        )
        for k, piece in enumerate(pieces):
            lanes = pl.ds(pl.multiple_of((me ^ k) * 256 + p * 128, 128), 128)
            out_ref[:, lanes] = acc_ref[:, lanes] + piece.astype(f32)
        at += 2 * rows


def finish_kernel(
    me_ref, mine, far, got_ref, o0, o1, o2, o3, wq, wk, wv, wg, wu, ga_ref, gm_ref, down_ref,
    gq_ref, gk_ref, gv_ref, go_ref, gga_ref, gg_ref, gu_ref, ggm_ref, gd_ref, cols_a, cols_f,
):
    me = me_ref[0]
    gd_ref[...] = down_ref[...].astype(f32)
    count = mine.shape[0]
    at = 0
    for cols in (cols_a, cols_f):
        chunk = cols.shape[1]
        cols[0] = mine[at : at + chunk, :]
        cols[2] = far[pl.ds(pl.multiple_of((me & 1) * count + at, 8), chunk), :]
        cols[1] = got_ref[at : at + chunk, :]
        cols[3] = got_ref[count + at : count + at + chunk, :]
        at += chunk
    out = sum(x[...].astype(f32) for x in (o0, o1, o2, o3))
    w_rows, width = gq_ref.shape
    for t in range(width // 128):
        go_ref[:, t * 128 : t * 128 + 128] = out[t * w_rows : (t + 1) * w_rows, :]
    unpack_attn(me, cols_a, gq_ref, gk_ref, gv_ref)
    gga_ref[...] = gain_grad(((wq, gq_ref), (wk, gk_ref), (wv, gv_ref)), ga_ref)
    unpack_ffn(me, cols_f, gg_ref, gu_ref)
    ggm_ref[...] = gain_grad(((wg, gg_ref), (wu, gu_ref)), gm_ref)


def gain_grad(pairs, gain_ref):
    column = sum(jnp.sum(w[...].astype(f32) * g[...], axis=1, keepdims=True) for w, g in pairs)
    rows = column.shape[0]
    same = lax.broadcasted_iota(jnp.int32, (rows, rows), 0) == lax.broadcasted_iota(jnp.int32, (rows, rows), 1)
    return jnp.sum(jnp.where(same, column, 0.0), axis=0, keepdims=True) / gain_ref[...].astype(f32)


def unpack_attn(me, cols_ref, *outs):
    w_rows, width = outs[0].shape
    part = width // SEQ
    for s in range(SEQ):
        at = 0
        for t in range(part // 128):
            for ref in outs:
                lanes = slice(s * part + t * 128, s * part + t * 128 + 128)
                ref[:, lanes] = cols_ref[me ^ s, at : at + w_rows, :].astype(f32)
                at += w_rows


def unpack_ffn(me, cols_ref, gg_ref, gu_ref):
    w_rows = gg_ref.shape[0]
    inner = gg_ref.shape[1] // SEQ
    main = main_lanes(inner)
    rest = inner - main
    half = main // 128
    for s in range(SEQ):
        slot = me ^ s
        tiles = [cols_ref[slot, t * w_rows : (t + 1) * w_rows, :].astype(f32) for t in range(2 * inner // 128)]
        gg_ref[:, s * inner : (s + 1) * inner] = jnp.concatenate(tiles[:half] + [tiles[-1][:, :rest]], axis=1)
        gu_ref[:, s * inner : (s + 1) * inner] = jnp.concatenate(tiles[half : 2 * half] + [tiles[-1][:, rest:]], axis=1)


def unpack_kernel(me_ref, cols_a, cols_f, wq, wk, wv, wg, wu, ga_ref, gm_ref, gq_ref, gk_ref, gv_ref, gga_ref, gg_ref, gu_ref, ggm_ref):
    unpack_attn(me_ref[0], cols_a, gq_ref, gk_ref, gv_ref)
    gga_ref[...] = gain_grad(((wq, gq_ref), (wk, gk_ref), (wv, gv_ref)), ga_ref)
    unpack_ffn(me_ref[0], cols_f, gg_ref, gu_ref)
    ggm_ref[...] = gain_grad(((wg, gg_ref), (wu, gu_ref)), gm_ref)


def input_grad_kernel(me_ref, *refs):
    *d_refs, w_ref, kept_ref, sent_ref = refs
    step = pl.program_id(0)
    d_qkv = [d[:, i * 128 : i * 128 + 128] for i in range(3) for d in d_refs]
    grad = mul(jnp.concatenate(d_qkv, axis=1), w_ref[...], 1, 1).astype(bf16)
    rows = grad.shape[0]
    for k in range(SEQ):

        @pl.when(step == SEQ - 1 - k)
        def _():
            (sent_ref if k % 2 else kept_ref)[k // 2 * rows : (k // 2 + 1) * rows, :] = grad


def input_grad(me, d_qkv, w):
    length, part = d_qkv[0].shape
    width = w.shape[0]
    rows = length // SEQ
    here = lambda k, m: (m[0] ^ (SEQ - 1 - k), 0)
    return pl.pallas_call(
        input_grad_kernel,
        name="input_grad",
        grid_spec=pltpu.PrefetchScalarGridSpec(
            num_scalar_prefetch=1,
            grid=(SEQ,),
            in_specs=[pl.BlockSpec((rows, part), here)] * len(d_qkv) + [fixed(w.shape)],
            out_specs=[fixed((2 * rows, width))] * 2,
        ),
        out_shape=[jax.ShapeDtypeStruct((2 * rows, width), bf16)] * 2,
        compiler_params=params(16),
    )(me, *d_qkv, w)


def to_core(value):
    return lax.ppermute(value, "seq", [(i, i ^ 1) for i in range(SEQ)])


def to_chip(value):
    return lax.ppermute(value, "seq", [(i, i ^ 2) for i in range(SEQ)])


def to_both(value):
    return lax.ppermute(value, "seq", [(i, i ^ 3) for i in range(SEQ)])


def gather_rel(value):
    far = to_chip(value)
    return value, to_core(value), far, to_core(far)


def exchange_rel(pieces):
    return [pieces[0], to_core(pieces[1]), to_chip(pieces[2]), to_both(pieces[3])]


def scatter_sum(kept, sent):
    sums = add(kept, to_core(sent))
    rows = kept.shape[0] // 2
    return sums[:rows] + to_chip(sums[rows:].astype(bf16)).astype(f32)


def add(a, b):
    return a.astype(f32) + b.astype(f32)


def to_y(value):
    dp = lax.axis_size("dp")
    return lax.ppermute(value, "dp", [(i, i ^ 1) for i in range(dp)])


def to_z(value, hops=1):
    dp = lax.axis_size("dp")
    return lax.ppermute(value, "dp", [(i, (i + 2 * hops) % dp) for i in range(dp)])


def rotary(length, head_width):
    pairs = jnp.arange(head_width // 2, dtype=f32)
    freq = jnp.exp(pairs * (-2.0 * math.log(10000.0) / head_width))
    theta = jnp.arange(length, dtype=jnp.int32).astype(f32)[:, None] * freq[None, :]
    cos, sin = jnp.cos(theta), jnp.sin(theta)
    return jnp.concatenate([cos] * 4, axis=1), jnp.concatenate([-sin, sin] * 2, axis=1)


class Stage:
    def fence(self):
        names = list(vars(self))
        for name, value in zip(names, sync(*[getattr(self, name) for name in names])):
            setattr(self, name, value)


def body_direct(
    tokens, first_values, value_grad_acc, segment_ids, query_weight, key_weight, value_weight, out_weight,
    attn_gain, gate_weight, up_weight, down_weight, mlp_gain, out_grad,
):
    dp = lax.axis_size("dp")
    zs = dp // 2
    rows, width = tokens.shape[1:]
    length = segment_ids.shape[1]
    w_rows = query_weight.shape[0]
    part = width // SEQ
    inner = gate_weight.shape[1] // SEQ
    me = lax.axis_index("seq").astype(jnp.int32)
    mine = lax.axis_index("dp").astype(jnp.int32)
    me_arg = me[None]
    place = jnp.stack([me, me * dp + mine, mine])
    s = Stage()

    half = rows // 2
    *s.cols, s.orows, drows, tok_a, tok_b = pack_attn(
        place, query_weight, key_weight, value_weight, out_weight, down_weight, attn_gain, mlp_gain, tokens[0]
    )
    s.r, s.tok_far = [drows], [tok_a, tok_b]
    s.tokens, s.first, s.out_grad, s.segments = tokens[0], first_values[0], out_grad[0], segment_ids
    s.gate, s.up = gate_weight, up_weight
    s.fence()
    s.cols = exchange_rel(s.cols)
    s.ry = [to_y(s.r[0])]
    s.r.append(to_z(s.r[0]))
    s.fence()
    s.a = [jnp.concatenate([*s.cols, s.orows])]
    del s.cols, s.orows
    s.tok_far[0] = to_chip(s.tok_far[0])
    s.ay = [to_y(s.a[0])]
    s.a.append(to_z(s.a[0]))
    s.fcols = pack_ffn(place, s.gate, s.up)
    del s.gate, s.up
    s.fence()
    s.ay.append(to_y(s.a[1]))
    s.a.append(to_z(s.a[1]))
    s.f_piece = jnp.concatenate(exchange_rel(s.fcols))
    s.cos, s.sin = rotary(length, width // HEADS)
    del s.fcols
    s.fence()
    ffn_all = lax.all_gather(s.f_piece, "dp", axis=0, tiled=False)
    del s.f_piece
    s.tok_far[1] = to_chip(s.tok_far[1])
    s.ay.append(to_y(s.a[2]))
    s.a.append(to_z(s.a[2]))
    s.tok_near = to_core(s.tokens)
    s.first = [lax.dynamic_slice_in_dim(s.first, (me ^ k) * part, part, 1) for k in range(SEQ)]
    s.og_far = [s.out_grad[:half], s.out_grad[half:]]
    s.fence()
    s.ay.append(to_y(s.a[3]))
    s.first = jnp.concatenate(exchange_rel(s.first))
    tok_far = jnp.concatenate(s.tok_far)
    s.tok = jnp.concatenate([s.tokens, s.tok_near, tok_far, to_core(tok_far)])
    del s.tok_far, s.tok_near
    s.fence()
    s.ry.append(to_y(s.r[1]))
    s.r.append(to_z(s.r[1]))
    s.og_far[0] = to_chip(s.og_far[0])
    s.og = [s.out_grad, to_core(s.out_grad)]
    s.w_qkv, s.w_out, attn_gain_all, mlp_gain_all = assemble_attn(place, s.a + s.ay, width)
    s.attn_gain, s.mlp_gain = attn_gain_all.reshape(1, width), mlp_gain_all.reshape(1, width)
    s.nin, s.q, s.k, s.v = qkv_call(me_arg, s.tok, s.first, s.w_qkv, s.attn_gain, s.cos, s.sin)
    del s.a, s.ay, s.first
    s.fence()
    s.og_far[1] = to_chip(s.og_far[1])
    s.wo = [s.w_out, to_core(s.w_out), to_chip(s.w_out)]
    s.ry.append(to_y(s.r[2]))
    s.r.append(to_z(s.r[2]))
    s.attended, s.lse = attend_call(s.q, s.k, s.v, s.segments)
    del s.w_out
    s.fence()
    att_far = to_chip(s.attended)
    s.ry.append(to_y(s.r[3]))
    s.att = [s.attended, to_core(s.attended), att_far]
    s.wo.append(to_core(s.wo[2]))
    og_far = jnp.concatenate(s.og_far)
    s.og = jnp.concatenate([*s.og, og_far, to_core(og_far)])
    s.fence()
    s.att.append(to_core(s.att[2]))
    s.w_down = assemble_rows(place, s.r + s.ry, width, inner)
    del s.r, s.ry, s.og_far
    s.fence()
    s.nm, s.hidden, s.d_gu, s.mid, s.dnm, dnm_sent, s.lo, s.lo_sent = ffn_call(
        me_arg, s.tok, s.og, s.att, s.wo, s.mlp_gain, ffn_all, s.w_down
    )
    s.dnm, s.dnm_far = halves(s.dnm, to_core(dnm_sent))
    del s.tok, s.att, s.w_down
    s.fence()
    s.dnm_far = to_chip(s.dnm_far)
    pieces = list(columns_grad(place, s.nm, s.d_gu, dp))
    s.f_kept, s.f_sent = pieces[:zs], pieces[zs:]
    s.g_down = down_grad(after(s.hidden, pieces[0]), s.og)
    g_down = lax.psum_scatter(s.g_down, "dp", scatter_dimension=0, tiled=True)
    del s.nm, s.d_gu, s.hidden, s.og
    s.fence()
    s.f_sent[3] = to_y(s.f_sent[3])
    lo_got = to_core(s.lo_sent)
    s.d_middle, s.d_branch, *s.d_att = simple(
        branch_kernel,
        "branch",
        (s.dnm, s.dnm_far, s.mid, s.out_grad, s.mlp_gain, *s.wo),
        [shaped(f32, rows, width), shaped(bf16, rows, width)] + [shaped(bf16, rows, part)] * SEQ,
    )
    s.lo, s.lo_far = halves(s.lo, lo_got)
    del s.dnm, s.dnm_far, s.wo, s.lo_sent, s.g_down
    s.fence()
    s.d_att = exchange_rel(s.d_att)
    s.f_sent[2] = to_y(s.f_sent[2])
    s.f = to_z(total(s.f_kept[3], s.f_sent[3]))
    s.fence()

    def back(pair, *along):
        return attend_back_call(
            pair, place, s.q, s.k, s.v, s.d_att, s.lse, s.segments, s.cos, s.sin, s.nin, dp, True, along
        )

    def other_chip_values(d_pair):
        return lax.dynamic_slice(d_pair, (((me >> 1) ^ 1) * 2 * rows, 256), (2 * rows, 128))

    s.f_sent[1] = to_y(s.f_sent[1])
    s.f = to_z(total(s.f_kept[2], s.f_sent[2], s.f))
    s.d_branch = [s.d_branch, to_core(s.d_branch), to_chip(s.d_branch)]
    d_pair, kept, sent = back(0, s.f_sent[0])
    s.d_qkv, s.kept, s.sent = [d_pair], [kept], [sent]
    s.fence()
    s.sent[0] = to_y(s.sent[0])
    s.f = to_z(total(s.f_kept[1], s.f_sent[1], s.f))
    s.lo_far = to_chip(s.lo_far)
    s.d_branch.append(to_core(s.d_branch[2]))
    s.values_far = to_chip(other_chip_values(s.d_qkv[0]))
    d_pair, kept, sent = back(1)
    s.d_qkv.append(d_pair)
    s.dnin, s.dnin_sent = input_grad(me_arg, s.d_qkv, s.w_qkv)
    s.kept.append(kept)
    s.sent.append(sent)
    del s.nin, s.d_att, s.w_qkv
    s.fence()

    def over_z(first, *others):
        return [first] + [to_z(piece, j + 1) for j, piece in enumerate(others)]

    s.sent[1] = to_y(s.sent[1])
    s.kept[0] = over_z(*slots(s.kept[0], s.sent[0]))
    s.dnin, s.dnin_far = halves(s.dnin, to_core(s.dnin_sent))
    s.out_kept, s.out_sent = out_projection_grad(place, s.attended, s.d_branch, dp)
    del s.d_branch, s.attended, s.dnin_sent
    s.fence()
    s.kept[1] = over_z(*slots(s.kept[1], s.sent[1]))
    s.out_sent = to_y(s.out_sent)
    s.dnin_far = to_chip(s.dnin_far)
    s.layer_out = total(s.mid, s.lo, s.lo_far)
    del s.lo, s.lo_far, s.mid
    s.fence()
    s.mine, s.near, far = cut(me_arg, s.kept, (s.f_kept[0], s.sent[0], s.f), s.d_qkv[1])
    s.far = to_chip(far)
    s.out_kept = over_z(*slots(s.out_kept, s.out_sent))
    s.token_grad = simple(
        token_grad_kernel,
        "token_grad",
        (s.dnin, s.dnin_far, s.tokens, s.attn_gain, s.d_middle),
        [shaped(bf16, rows, width)],
        60,
    )[0]
    s.g_down = g_down
    del s.kept, s.sent, s.out_sent, s.dnin, s.d_middle, s.f, s.f_kept, s.f_sent
    s.fence()
    count = s.mine.shape[0]
    args = (me_arg, s.near, s.far, *s.d_qkv, s.values_far)
    got = to_core(simple(relay_kernel, "relay", args, [shaped(bf16, 2 * count + SEQ * rows, 128)])[0])
    weights = (query_weight, key_weight, value_weight, gate_weight, up_weight)
    shapes = [(w_rows, width)] * 4 + [(1, w_rows)] + [(w_rows, SEQ * inner)] * 2 + [(1, w_rows), g_down.shape]
    args = (s.mine, s.far, got, *s.out_kept, *weights, attn_gain[None], mlp_gain[None], s.g_down)
    a_rows = 3 * part // 128 * w_rows
    g_q, g_k, g_v, g_out, attn_gain_grad, g_gate, g_up, mlp_gain_grad, g_down = pl.pallas_call(
        finish_kernel,
        name="finish",
        grid=(1,),
        in_specs=[SMEM] + [fixed(x.shape) for x in args],
        out_specs=[fixed(x) for x in shapes],
        out_shape=[shaped(f32, *x) for x in shapes],
        scratch_shapes=[pltpu.VMEM((SEQ, a_rows, 128), bf16), pltpu.VMEM((SEQ, count - a_rows, 128), bf16)],
        compiler_params=params(24),
    )(me_arg, *args)
    value_grad_out = simple(
        value_grad_kernel,
        "value_grad",
        (me_arg, value_grad_acc[0], *s.d_qkv, s.values_far, s.far, got),
        [shaped(f32, rows, width)],
    )[0]
    return (
        s.layer_out[None],
        s.token_grad[None],
        value_grad_out[None],
        g_q,
        g_k,
        g_v,
        g_out,
        attn_gain_grad[0],
        g_gate,
        g_up,
        g_down,
        mlp_gain_grad[0],
    )


def body_plain(
    tokens, first_values, value_grad_acc, segment_ids, query_weight, key_weight, value_weight, out_weight,
    attn_gain, gate_weight, up_weight, down_weight, mlp_gain, out_grad,
):
    dp = lax.axis_size("dp")
    rows, width = tokens.shape[1:]
    length = segment_ids.shape[1]
    w_rows, d_rows = query_weight.shape[0], down_weight.shape[0]
    part = width // SEQ
    inner = gate_weight.shape[1] // SEQ
    main = main_lanes(inner)
    me = lax.axis_index("seq").astype(jnp.int32)
    mine = lax.axis_index("dp").astype(jnp.int32)
    me_arg = me[None]
    place = jnp.stack([me, me * dp + mine, mine])

    def columns(weight, count):
        return weight.reshape(w_rows, SEQ, count).transpose(1, 0, 2)

    owner = jnp.arange(width) // w_rows == me * dp + mine

    def spread(gain):
        full = jnp.where(owner, jnp.tile(gain, width // w_rows), jnp.zeros((), bf16))
        cut = 3 * part
        return jnp.stack([full[:cut], jnp.pad(full[cut:], (0, 2 * cut - width))])

    gains = jnp.concatenate([spread(attn_gain), spread(mlp_gain), jnp.zeros((4, 3 * part), bf16)])
    attn_cols = jnp.concatenate([columns(w, part) for w in (query_weight, key_weight, value_weight)], axis=2)
    attn_cols = jnp.concatenate([attn_cols, jnp.broadcast_to(gains[None], (SEQ,) + gains.shape)], axis=1)
    gate_cols, up_cols = columns(gate_weight, inner), columns(up_weight, inner)
    ffn_cols = jnp.concatenate(
        [gate_cols[:, :, :main], up_cols[:, :, :main], gate_cols[:, :, main:], up_cols[:, :, main:]], axis=2
    )
    attn_cols = lax.all_to_all(attn_cols, "seq", split_axis=0, concat_axis=0, tiled=True)
    ffn_cols = lax.all_to_all(ffn_cols, "seq", split_axis=0, concat_axis=0, tiled=True)
    attn_all = lax.all_gather(attn_cols.reshape(-1, 3 * part), "dp", axis=0, tiled=True)
    attn_all = attn_all.reshape(dp, SEQ, w_rows + 8, 3 * part)
    w_qkv = attn_all[:, :, :w_rows].transpose(1, 0, 2, 3).reshape(width, 3 * part)
    gain_all = jnp.sum(attn_all[:, :, w_rows : w_rows + 4].astype(f32), axis=(0, 1))
    attn_gain_all = jnp.concatenate([gain_all[0], gain_all[1]])[None, :width]
    mlp_gain_all = jnp.concatenate([gain_all[2], gain_all[3]])[None, :width]
    w_out = lax.all_gather(out_weight, "dp", axis=0, tiled=True)
    w_down = lax.all_gather(down_weight, "dp", axis=0, tiled=True)
    ffn_all = lax.all_gather(ffn_cols.reshape(-1, 2 * inner), "dp", axis=0, tiled=True)
    w_ffn = ffn_all.reshape(dp, SEQ, w_rows, 2 * inner).transpose(1, 0, 2, 3).reshape(width, 2 * inner)

    cos, sin = rotary(length, width // HEADS)
    tok = jnp.concatenate(gather_rel(tokens[0]))
    og = jnp.concatenate(gather_rel(out_grad[0]))
    first_cols = first_values[0].reshape(rows, SEQ, part)
    first = exchange_rel([lax.dynamic_index_in_dim(first_cols, me ^ k, 1, keepdims=False) for k in range(SEQ)])
    nin, q, k, v = qkv_call(me_arg, tok, jnp.concatenate(first), w_qkv, attn_gain_all, cos, sin)
    attended, lse = attend_call(q, k, v, segment_ids)
    wo = gather_rel(w_out)
    nm, hidden, d_gu, mid, *sums = ffn_call(me_arg, tok, og, gather_rel(attended), wo, mlp_gain_all, w_ffn, w_down)
    layer_out = (mid + scatter_sum(*sums[2:])).astype(bf16)
    d_middle = out_grad[0].astype(f32) + back_through_norm(scatter_sum(*sums[:2]), mid, mlp_gain_all)
    d_branch = d_middle.astype(bf16)
    d_att = exchange_rel([mul(d_branch, w, 1, 1).astype(bf16) for w in wo])
    d_branch_all = jnp.stack(gather_rel(d_branch))[me ^ jnp.arange(SEQ)].reshape(length, width)
    d_qkv = [
        attend_back_call(pair, place, q, k, v, d_att, lse, segment_ids, cos, sin, nin, dp, False)[0] for pair in range(2)
    ]
    dnin = scatter_sum(*input_grad(me_arg, d_qkv, w_qkv))
    token_grad = d_middle + back_through_norm(dnin, tokens[0].astype(f32), attn_gain_all)
    dv = jnp.concatenate([d[:, 256:] for d in d_qkv], axis=1)
    dv = exchange_rel([lax.dynamic_slice_in_dim(dv, (me ^ i) * rows, rows, 0) for i in range(SEQ)])
    dv = jnp.stack(dv)[me ^ jnp.arange(SEQ)].transpose(1, 0, 2).reshape(rows, width)
    value_grad_out = value_grad_acc[0] + dv.astype(f32)

    def over_dp(grads):
        return lax.psum_scatter(grads.reshape(-1, 128), "dp", scatter_dimension=0, tiled=True)

    def to_rows(sums):
        sums = sums.reshape(SEQ, -1, 128)
        return jnp.stack(exchange_rel([lax.dynamic_index_in_dim(sums, me ^ i, 0, keepdims=False) for i in range(SEQ)]))

    attn_sums = over_dp(columns_grad_plain(nin, jnp.concatenate(d_qkv, axis=1), dp))
    ffn_sums = over_dp(columns_grad_plain(nm, d_gu, dp))
    g_out = lax.psum_scatter(mul(attended, d_branch_all, 0, 0).astype(bf16), "dp", scatter_dimension=0, tiled=True)
    g_down = lax.psum_scatter(mul(hidden, og, 0, 0).astype(bf16), "dp", scatter_dimension=0, tiled=True)
    weights = (query_weight, key_weight, value_weight, gate_weight, up_weight)
    shapes = [(w_rows, width)] * 3 + [(1, w_rows)] + [(w_rows, SEQ * inner)] * 2 + [(1, w_rows)]
    args = (me_arg, to_rows(attn_sums), to_rows(ffn_sums), *weights, attn_gain[None], mlp_gain[None])
    g_q, g_k, g_v, attn_gain_grad, g_gate, g_up, mlp_gain_grad = simple(
        unpack_kernel, "unpack", args, [shaped(f32, *x) for x in shapes]
    )
    return (
        layer_out[None],
        token_grad.astype(bf16)[None],
        value_grad_out[None],
        g_q,
        g_k,
        g_v,
        g_out.astype(f32),
        attn_gain_grad[0],
        g_gate,
        g_up,
        g_down.astype(f32),
        mlp_gain_grad[0],
    )


def solution(mesh):
    token = P("dp", "seq", None)
    weight = P(("seq", "dp"), None)
    gain = P(("seq", "dp"))
    return jax.shard_map(
        body_direct if mesh.shape["dp"] == 8 else body_plain,
        mesh=mesh,
        in_specs=(token, token, token, P("dp", None), weight, weight, weight, weight, gain, weight, weight, weight, gain, token),
        out_specs=(token, token, token, weight, weight, weight, weight, gain, weight, weight, weight, gain),
        check_vma=False,
    )
```

```python
import functools
import math

import jax
import jax.numpy as jnp
from jax import lax
from jax.experimental import pallas as pl
from jax.experimental.pallas import tpu as pltpu
from jax.sharding import PartitionSpec as P

HEADS = 16
DOC_MOST = 512
SEQ = 4
BLOCK = 256

epsilon = 1e-06
masked_value = -1e30
bf16 = jnp.bfloat16
f32 = jnp.float32


def mul(a, b, ca, cb):
    return lax.dot_general(a, b, (((ca,), (cb,)), ((), ())), preferred_element_type=f32)


def params(mib):
    return pltpu.CompilerParams(vmem_limit_bytes=mib << 20)


VMEM = pl.BlockSpec(memory_space=pltpu.VMEM)
SMEM = pl.BlockSpec(memory_space=pltpu.SMEM)


def fixed(shape):
    return pl.BlockSpec(shape, lambda *_: (0,) * len(shape), pipeline_mode=pl.Buffered(1))


def sync(*values):
    return lax.optimization_barrier(values)


def after(value, *earlier):
    return lax.optimization_barrier((value, *earlier))[0]


def half_swap(field):
    lanes = field.shape[-1]
    lane = lax.broadcasted_iota(jnp.int32, field.shape, 1)
    up = pltpu.roll(field, lanes - 32, 1)
    down = pltpu.roll(field, 32, 1)
    return jnp.where(lane % 64 < 32, up, down)


def qkv_kernel(me_ref, tok_ref, first_ref, w_ref, gain_ref, cos_ref, sin_ref, nin_ref, q_ref, k_ref, v_ref):
    x = tok_ref[...].astype(f32)
    scale = lax.rsqrt(jnp.mean(x * x, axis=-1, keepdims=True) + epsilon)
    nin = (x * scale * gain_ref[...]).astype(bf16)
    nin_ref[...] = nin
    lin = mul(nin, w_ref[...], 1, 0)
    cos = jnp.concatenate([cos_ref[...]] * 2, axis=1)
    sin = jnp.concatenate([sin_ref[...]] * 2, axis=1)
    part = lin.shape[1] // 3
    q = lin[:, :part]
    q_ref[...] = ((q * cos + half_swap(q) * sin).astype(bf16).astype(f32) * 0.125).astype(bf16)
    k = lin[:, part : 2 * part]
    k_ref[...] = (k * cos + half_swap(k) * sin).astype(bf16)
    v_ref[...] = (0.5 * lin[:, 2 * part :] + 0.5 * first_ref[...].astype(f32)).astype(bf16)


def qkv_call(me, tok, first, w, gain, cos, sin):
    length, width = tok.shape
    rows = length // SEQ
    part = w.shape[1] // 3
    here = lambda k, m: (m[0] ^ k, 0)
    rel = lambda k, m: (k, 0)
    return pl.pallas_call(
        qkv_kernel,
        name="qkv",
        grid_spec=pltpu.PrefetchScalarGridSpec(
            num_scalar_prefetch=1,
            grid=(SEQ,),
            in_specs=[
                pl.BlockSpec((rows, width), rel),
                pl.BlockSpec((rows, part), rel),
                fixed(w.shape),
                fixed((1, width)),
                pl.BlockSpec((rows, 128), here),
                pl.BlockSpec((rows, 128), here),
            ],
            out_specs=[pl.BlockSpec((rows, width), here)] + [pl.BlockSpec((rows, part), here)] * 3,
        ),
        out_shape=[jax.ShapeDtypeStruct((length, width), bf16)]
        + [jax.ShapeDtypeStruct((length, part), bf16)] * 3,
        compiler_params=params(16),
    )(me, tok, first, w, gain, cos, sin)


def key_range(block):
    return max(0, block * BLOCK - (DOC_MOST // BLOCK) * BLOCK), (block + 1) * BLOCK


def column_of(row_ref):
    return jnp.broadcast_to(row_ref[...].astype(f32), (8, row_ref.shape[1])).T[:, :1]


def allowed_pairs(seg_col, seg_row, block, low, high):
    keys = lax.broadcasted_iota(jnp.int32, (high - low, BLOCK), 0) + low
    rows = lax.broadcasted_iota(jnp.int32, (high - low, BLOCK), 1) + block * BLOCK
    row = seg_row[:, block * BLOCK : (block + 1) * BLOCK].astype(f32)
    return (seg_col[low:high, :] == row) & (keys <= rows)


def head_lanes(field, head):
    lane = lax.broadcasted_iota(jnp.int32, field.shape, 1)
    return jnp.where(lane // 64 == head, field, jnp.zeros_like(field))


def half_rows(head):
    return pl.ds(pl.multiple_of(head * 64, 64), 64)


def attend_kernel(q_ref, k_ref, v_ref, seg_row, o_ref, lse_ref, turned, turned_out):
    length = q_ref.shape[0]
    seg_col = column_of(seg_row)
    turned[...] = v_ref[...].astype(f32).T.astype(bf16)

    def one_head(head, carry):
        for block in range(length // BLOCK):
            low, high = key_range(block)
            allowed = allowed_pairs(seg_col, seg_row, block, low, high)
            here = slice(block * BLOCK, (block + 1) * BLOCK)
            scores = mul(k_ref[low:high, :], head_lanes(q_ref[here, :], head), 1, 1)
            scores = jnp.where(allowed, scores, masked_value)
            top = jnp.max(scores, axis=0, keepdims=True)
            expo = jnp.exp(scores - top)
            total = jnp.sum(expo, axis=0, keepdims=True)
            probs = (expo * (1.0 / total)).astype(bf16)
            turned_out[half_rows(head), here] = mul(turned[half_rows(head), low:high], probs, 1, 0)
            lse_ref[0, pl.ds(head, 1), here] = top + jnp.log(total)
        return carry

    lax.fori_loop(0, 2, one_head, 0)
    for block in range(length // BLOCK):
        here = slice(block * BLOCK, (block + 1) * BLOCK)
        o_ref[here, :] = turned_out[:, here].T.astype(bf16)


def attend_call(q, k, v, seg_row):
    length, part = q.shape
    pairs = part // 128
    lanes = pl.BlockSpec((length, 128), lambda p: (0, p))
    return pl.pallas_call(
        attend_kernel,
        name="attend",
        grid=(pairs,),
        in_specs=[lanes] * 3 + [fixed((1, length))],
        out_specs=[lanes, pl.BlockSpec((1, 2, length), lambda p: (p, 0, 0))],
        out_shape=[jax.ShapeDtypeStruct((length, part), bf16), jax.ShapeDtypeStruct((pairs, 2, length), f32)],
        scratch_shapes=[pltpu.VMEM((128, length), bf16), pltpu.VMEM((128, length), f32)],
        compiler_params=params(24),
    )(q, k, v, seg_row)


def attend_back_kernel(
    dp, pieces, place_ref, q_ref, k_ref, v_ref, d0, d1, d2, d3, lse_ref, seg_row, cos_ref, sin_ref, nin_ref,
    *refs,
):
    outs, (da_ref, dk_sum, dv_sum, work, turned, turned_dq) = refs[:-6], refs[-6:]
    *along, d_ref = outs[: len(outs) - 2 * pieces]
    outs = outs[len(outs) - 2 * pieces :]
    length = q_ref.shape[0]
    rows = d0.shape[0]
    for k, ref in enumerate((d0, d1, d2, d3)):
        da_ref[pl.ds(pl.multiple_of((place_ref[0] ^ k) * rows, rows), rows), :] = ref[...]
    seg_col = column_of(seg_row)
    dk_sum[...] = jnp.zeros_like(dk_sum)
    dv_sum[...] = jnp.zeros_like(dv_sum)
    turned[...] = k_ref[...].astype(f32).T.astype(bf16)

    def one_head(head, carry):
        for block in range(length // BLOCK):
            low, high = key_range(block)
            allowed = allowed_pairs(seg_col, seg_row, block, low, high)
            here = slice(block * BLOCK, (block + 1) * BLOCK)
            q_head = head_lanes(q_ref[here, :], head)
            da_head = head_lanes(da_ref[here, :], head)
            scores = mul(k_ref[low:high, :], q_head, 1, 1)
            probs = jnp.where(allowed, jnp.exp(scores - lse_ref[0, pl.ds(head, 1), here]), 0.0)
            d_probs = mul(v_ref[low:high, :], da_head, 1, 1)
            delta = jnp.sum(probs * d_probs, axis=0, keepdims=True)
            d_scores = (probs * (d_probs - delta)).astype(bf16)
            turned_dq[half_rows(head), here] = mul(turned[half_rows(head), low:high], d_scores, 1, 0)
            dk_sum[low:high, :] += mul(d_scores, q_head, 1, 0)
            dv_sum[low:high, :] += mul(probs.astype(bf16), da_head, 1, 0)
        return carry

    lax.fori_loop(0, 2, one_head, 0)
    for block in range(length // BLOCK):
        here = slice(block * BLOCK, (block + 1) * BLOCK)
        dq = turned_dq[:, here].T * 0.125
        d_ref[here, :128] = (dq * cos_ref[here, :] - half_swap(dq) * sin_ref[here, :]).astype(bf16)
    dk = dk_sum[...]
    d_ref[:, 128:256] = (dk * cos_ref[...] - half_swap(dk) * sin_ref[...]).astype(bf16)
    d_ref[:, 256:] = (0.5 * dv_sum[...]).astype(bf16)
    if not outs:
        return
    kept_ref, sent_ref = outs
    part = work.shape[0]
    w_rows = part // dp
    first = 0
    if along:
        first = along[0].shape[0]
        sent_ref[:first, :] = along[0][...]
    for s in range(SEQ):
        work[...] = mul(nin_ref[:, s * part : (s + 1) * part], d_ref[...], 0, 0).astype(bf16)
        for slot in range(dp):
            here = pl.ds(pl.multiple_of(owner_index(place_ref, dp, slot) * w_rows, w_rows), w_rows)
            for t in range(3):
                at = (s * 3 + t) * w_rows
                piece = work[here, t * 128 : t * 128 + 128]
                if slot < dp // 2:
                    kept_ref[slot, at : at + w_rows, :] = piece
                else:
                    at += first + (slot - dp // 2) * kept_ref.shape[1]
                    sent_ref[at : at + w_rows, :] = piece


def attend_back_call(pair, place, q, k, v, da, lse, seg_row, cos, sin, nin, dp, pieces, along=()):
    length, width = nin.shape
    part = width // SEQ
    lanes = pl.BlockSpec((length, 128), lambda _: (0, pair), pipeline_mode=pl.Buffered(1))
    outs = [(length, 384)]
    if pieces:
        rows = 3 * width // dp
        outs += [(dp // 2, rows, 128), (sum(x.shape[0] for x in along) + dp // 2 * rows, 128)]
    return pl.pallas_call(
        functools.partial(attend_back_kernel, dp, pieces),
        name="attend_back",
        grid=(1,),
        in_specs=[SMEM]
        + [lanes] * 3
        + [pl.BlockSpec((length // SEQ, 128), lambda _: (0, pair), pipeline_mode=pl.Buffered(1))] * 4
        + [pl.BlockSpec((1, 2, length), lambda _: (pair, 0, 0)), fixed((1, length))]
        + [fixed((length, 128))] * 2
        + [fixed(nin.shape)]
        + [fixed(x.shape) for x in along],
        out_specs=[fixed(x) for x in outs],
        out_shape=[jax.ShapeDtypeStruct(x, bf16) for x in outs],
        scratch_shapes=[pltpu.VMEM((length, 128), bf16)]
        + [pltpu.VMEM((length, 128), f32)] * 2
        + [pltpu.VMEM((part, 384), bf16), pltpu.VMEM((128, length), bf16), pltpu.VMEM((128, length), f32)],
        compiler_params=params(60),
    )(place, q, k, v, *da, lse, seg_row, cos, sin, nin, *along)


def main_lanes(inner):
    return inner // 128 * 128


def pack_attn_kernel(
    q_ref, k_ref, v_ref, o_ref, d_ref, ag_ref, mg_ref, tok_ref, c0, c1, c2, c3, orows_ref, drows_ref, *halves_refs
):
    me = lax.axis_index("seq")
    owner = me * lax.axis_size("dp") + lax.axis_index("dp")
    w_rows, width = q_ref.shape
    part = width // SEQ
    lane = lax.broadcasted_iota(jnp.int32, (1, 128), 1)
    spot = lane // w_rows == owner % (128 // w_rows)

    def spread(gain):
        return jnp.where(spot, jnp.concatenate([gain[...].astype(f32)] * (128 // w_rows), axis=1), 0.0)

    row = lax.broadcasted_iota(jnp.int32, (16, 128), 0)
    gains = jnp.where(row == 0, spread(ag_ref), jnp.where(row == 1, spread(mg_ref), 0.0)).astype(bf16)
    for k, out in enumerate((c0, c1, c2, c3)):
        at = 0
        for ref in (q_ref, k_ref, v_ref):
            for t in range(part // 128):
                lanes = pl.ds(pl.multiple_of((me ^ k) * part + t * 128, 128), 128)
                out[at : at + w_rows, :] = ref[:, lanes]
                at += w_rows
        out[at : at + 16, :] = gains
    for ref, out in ((o_ref, orows_ref), (d_ref, drows_ref)):
        rows = ref.shape[0]
        for t in range(width // 128):
            out[t * rows : (t + 1) * rows, :] = ref[:, t * 128 : t * 128 + 128]
    for i, out in enumerate(halves_refs):
        rows = out.shape[0]
        out[...] = tok_ref[i * rows : (i + 1) * rows, :]


def pack_attn(wq, wk, wv, wo, wd, attn_gain, mlp_gain, tok):
    w_rows, width = wq.shape
    tiles = width // 128
    shapes = [(3 * tiles // SEQ * w_rows + 16, 128)] * 4 + [(tiles * w_rows, 128), (tiles * wd.shape[0], 128)]
    shapes += [(tok.shape[0] // 2, width)] * 2
    return pl.pallas_call(
        pack_attn_kernel,
        name="pack_attn",
        grid=(1,),
        in_specs=[fixed(w.shape) for w in (wq, wk, wv, wo, wd)] + [fixed((1, w_rows))] * 2 + [fixed(tok.shape)],
        out_specs=[fixed(x) for x in shapes],
        out_shape=[jax.ShapeDtypeStruct(x, bf16) for x in shapes],
        compiler_params=params(60),
    )(wq, wk, wv, wo, wd, attn_gain[None], mlp_gain[None], tok)


def pack_ffn_kernel(place_ref, g_ref, u_ref, c0, c1, c2, c3):
    me = place_ref[0]
    w_rows = g_ref.shape[0]
    inner = g_ref.shape[1] // SEQ
    main = main_lanes(inner)
    for s in range(SEQ):
        gate, up = g_ref[:, s * inner : (s + 1) * inner], u_ref[:, s * inner : (s + 1) * inner]
        tiles = [field[:, t * 128 : t * 128 + 128] for field in (gate, up) for t in range(main // 128)]
        tiles.append(jnp.concatenate([gate[:, main:], up[:, main:]], axis=1))
        for k, out in enumerate((c0, c1, c2, c3)):

            @pl.when(me ^ k == s)
            def _():
                for t, tile in enumerate(tiles):
                    out[t * w_rows : (t + 1) * w_rows, :] = tile


def pack_ffn(place, wg, wu):
    w_rows = wg.shape[0]
    inner = wg.shape[1] // SEQ
    return pl.pallas_call(
        pack_ffn_kernel,
        name="pack_ffn",
        grid=(1,),
        in_specs=[SMEM] + [fixed(w.shape) for w in (wg, wu)],
        out_specs=[fixed((2 * inner // 128 * w_rows, 128))] * 4,
        out_shape=[jax.ShapeDtypeStruct((2 * inner // 128 * w_rows, 128), bf16)] * 4,
        compiler_params=params(60),
    )(place, wg, wu)


def source_of(place_ref, dp, slot):
    groups = dp // 2
    b, j = slot // groups, slot % groups
    z, y = place_ref[2] // 2, place_ref[2] % 2
    return ((z + groups - j) % groups) * 2 + (y ^ b)


def assemble_attn_kernel(place_ref, *refs):
    dp = len(refs) - 4
    pieces, (w_ref, wo_ref, ag_ref, mg_ref) = refs[:dp], refs[dp:]
    width, lanes = w_ref.shape
    w_rows = width // (SEQ * dp)
    part = width // SEQ
    chunk = lanes // 128 * w_rows + 16
    ag_ref[...] = jnp.zeros_like(ag_ref)
    mg_ref[...] = jnp.zeros_like(mg_ref)
    for slot, piece in enumerate(pieces):
        src = source_of(place_ref, dp, slot)
        for k in range(SEQ):
            s = place_ref[0] ^ k
            row = pl.multiple_of(s * part + src * w_rows, w_rows)
            for t in range(lanes // 128):
                at = k * chunk + t * w_rows
                w_ref[pl.ds(row, w_rows), t * 128 : t * 128 + 128] = piece[at : at + w_rows, :]
            gains = piece[(k + 1) * chunk - 16 : (k + 1) * chunk, :].astype(f32)
            tile = (s * dp + src) * w_rows // 128
            ag_ref[pl.ds(tile, 1), :] += gains[0:1, :]
            mg_ref[pl.ds(tile, 1), :] += gains[1:2, :]
        row = pl.multiple_of(src * w_rows, w_rows)
        for t in range(width // 128):
            at = SEQ * chunk + t * w_rows
            wo_ref[pl.ds(row, w_rows), t * 128 : t * 128 + 128] = piece[at : at + w_rows, :]


def assemble_attn(place, pieces, width):
    shapes = [(width, 3 * width // SEQ), (width // SEQ, width), (width // 128, 128), (width // 128, 128)]
    return pl.pallas_call(
        assemble_attn_kernel,
        name="assemble_attn",
        grid=(1,),
        in_specs=[SMEM] + [fixed(x.shape) for x in pieces],
        out_specs=[fixed(x) for x in shapes],
        out_shape=[jax.ShapeDtypeStruct(x, t) for x, t in zip(shapes, (bf16, bf16, f32, f32))],
        compiler_params=params(12),
    )(place, *pieces)


def assemble_rows_kernel(place_ref, *refs):
    dp = len(refs) - 1
    pieces, out_ref = refs[:dp], refs[dp]
    count = out_ref.shape[0] // dp
    for slot, piece in enumerate(pieces):
        row = pl.multiple_of(source_of(place_ref, dp, slot) * count, 8)
        for t in range(out_ref.shape[1] // 128):
            out_ref[pl.ds(row, count), t * 128 : t * 128 + 128] = piece[t * count : (t + 1) * count, :]


def assemble_rows(place, pieces, width, inner):
    return pl.pallas_call(
        assemble_rows_kernel,
        name="assemble_rows",
        grid=(1,),
        in_specs=[SMEM] + [fixed(x.shape) for x in pieces],
        out_specs=fixed((inner, width)),
        out_shape=jax.ShapeDtypeStruct((inner, width), bf16),
        compiler_params=params(12),
    )(place, *pieces)


def ffn_kernel(me_ref, tok_ref, og_ref, a0, a1, a2, a3, wo0, wo1, wo2, wo3, gain_ref, w_ref, wd_ref, *outs):
    nm_ref, hid_ref, dgu_ref, mid_ref, *lists = outs
    step = pl.program_id(0)
    if len(w_ref.shape) == 3:
        pieces, w_ref = w_ref, lists.pop()
        dp = pieces.shape[0]
        width, lanes = w_ref.shape
        w_rows = width // (SEQ * dp)
        chunk = lanes // 128 * w_rows

        @pl.when(step == 0)
        def _():
            for k in range(SEQ):
                for src in range(dp):
                    row = pl.multiple_of((me_ref[0] ^ k) * (width // SEQ) + src * w_rows, w_rows)
                    for t in range(lanes // 128):
                        at = k * chunk + t * w_rows
                        w_ref[pl.ds(row, w_rows), t * 128 : t * 128 + 128] = pieces[src, at : at + w_rows, :]

    mid = tok_ref[...].astype(f32)
    inner = wd_ref.shape[0]
    main = main_lanes(inner)
    for a, wo in zip((a0, a1, a2, a3), (wo0, wo1, wo2, wo3)):
        mid = mid + mul(a[...], wo[...], 1, 0)
    scale = lax.rsqrt(jnp.mean(mid * mid, axis=-1, keepdims=True) + epsilon)
    nm = (mid * scale * gain_ref[...]).astype(bf16)
    nm_ref[...] = nm
    d_hidden = mul(og_ref[...], wd_ref[...], 1, 1)
    both = mul(nm, w_ref[...], 1, 0)

    def gated(gate, up, grad):
        sig = jax.nn.sigmoid(gate)
        silu = gate * sig
        return (
            (silu * up).astype(bf16),
            (grad * up * (sig * (1.0 + gate * (1.0 - sig)))).astype(bf16),
            (grad * silu).astype(bf16),
        )

    hid_main, dg_main, du_main = gated(both[:, :main], both[:, main : 2 * main], d_hidden[:, :main])
    last = both[:, 2 * main :]
    hid_last, dg_last, du_last = gated(last[:, : inner - main], last[:, inner - main :], d_hidden[:, main:])
    hid_ref[:, :main] = hid_main
    hid_ref[:, main:] = hid_last
    dgu_ref[:, :main] = dg_main
    dgu_ref[:, main : 2 * main] = du_main
    dgu_ref[:, 2 * main :] = jnp.concatenate([dg_last, du_last], axis=1)
    dnm = mul(dgu_ref[...], w_ref[...], 1, 1).astype(bf16)
    lo = mul(hid_ref[...], wd_ref[...], 1, 0).astype(bf16)
    dnm_kept, dnm_sent, lo_kept, lo_sent = lists
    rows = tok_ref.shape[0]
    for k in range(SEQ):

        @pl.when(step == SEQ - 1 - k)
        def _():
            here = slice(k // 2 * rows, (k // 2 + 1) * rows)
            (dnm_sent if k % 2 else dnm_kept)[here, :] = dnm
            (lo_sent if k % 2 else lo_kept)[here, :] = lo

    @pl.when(step == SEQ - 1)
    def _():
        mid_ref[...] = mid


def ffn_call(me, tok, og, att, wo, gain, w, wd):
    length, width = tok.shape
    rows = length // SEQ
    inner = wd.shape[0]
    part = att[0].shape[1]
    rel = lambda k, m: (SEQ - 1 - k, 0)
    here = lambda k, m: (m[0] ^ (SEQ - 1 - k), 0)
    return pl.pallas_call(
        ffn_kernel,
        name="ffn",
        grid_spec=pltpu.PrefetchScalarGridSpec(
            num_scalar_prefetch=1,
            grid=(SEQ,),
            in_specs=[pl.BlockSpec((rows, width), rel)] * 2
            + [pl.BlockSpec((rows, part), here)] * 4
            + [fixed(x.shape) for x in wo]
            + [fixed((1, width)), fixed(w.shape), fixed(wd.shape)],
            out_specs=[
                pl.BlockSpec((rows, width), rel),
                pl.BlockSpec((rows, inner), rel),
                pl.BlockSpec((rows, 2 * inner), rel),
                fixed((rows, width)),
            ]
            + [fixed((2 * rows, width))] * 4,
            scratch_shapes=[pltpu.VMEM((width, 2 * inner), bf16)] * (w.ndim - 2),
        ),
        out_shape=[
            jax.ShapeDtypeStruct((length, width), bf16),
            jax.ShapeDtypeStruct((length, inner), bf16),
            jax.ShapeDtypeStruct((length, 2 * inner), bf16),
            jax.ShapeDtypeStruct((rows, width), f32),
        ]
        + [jax.ShapeDtypeStruct((2 * rows, width), bf16)] * 4,
        compiler_params=params(60),
    )(me, tok, og, *att, *wo, gain, w, wd)


def owner_index(place_ref, dp, slot):
    groups = dp // 2
    b, j = slot // groups, slot % groups
    z, y = place_ref[2] // 2, place_ref[2] % 2
    return ((z + j) % groups) * 2 + (y ^ b)


def columns_grad_kernel(place_ref, act_ref, grad_ref, *refs):
    outs, work = refs[:-1], refs[-1]
    dp = len(outs)
    work[...] = mul(act_ref[...], grad_ref[...], 0, 0).astype(bf16)
    w_rows = work.shape[0] // dp
    for slot, ref in enumerate(outs):
        here = pl.ds(pl.multiple_of(owner_index(place_ref, dp, slot) * w_rows, w_rows), w_rows)
        for t in range(work.shape[1] // 128):
            ref[t * w_rows : (t + 1) * w_rows, :] = work[here, t * 128 : t * 128 + 128]


def columns_grad_plain(act, grad, dp):
    width, lanes = act.shape[1], grad.shape[1]
    w_rows = width // (SEQ * dp)
    grad = mul(act, grad, 0, 0).astype(bf16).reshape(SEQ, dp, w_rows, lanes // 128, 128)
    return grad.transpose(1, 0, 3, 2, 4).reshape(dp, -1, 128)


def columns_grad(place, act, grad, dp):
    length, width = act.shape
    lanes = grad.shape[1]
    part = width // SEQ
    chunk = lanes // 128 * (part // dp)
    return pl.pallas_call(
        columns_grad_kernel,
        name="columns_grad",
        grid_spec=pltpu.PrefetchScalarGridSpec(
            num_scalar_prefetch=1,
            grid=(SEQ,),
            in_specs=[pl.BlockSpec((length, part), lambda s, m: (0, s)), fixed(grad.shape)],
            out_specs=[pl.BlockSpec((chunk, 128), lambda s, m: (s, 0))] * dp,
            scratch_shapes=[pltpu.VMEM((part, lanes), bf16)],
        ),
        out_shape=[jax.ShapeDtypeStruct((SEQ * chunk, 128), bf16)] * dp,
        compiler_params=params(60),
    )(place, act, grad)


def out_grad_kernel(place_ref, act_ref, d0, d1, d2, d3, kept_ref, sent_ref, work):
    rows = d0.shape[0]
    total = 0.0
    for k, ref in enumerate((d0, d1, d2, d3)):
        act = act_ref[pl.ds(pl.multiple_of((place_ref[0] ^ k) * rows, rows), rows), :]
        total = total + mul(act, ref[...], 0, 0)
    work[...] = total.astype(bf16)
    dp = 2 * kept_ref.shape[0]
    count = work.shape[0] // dp
    at = 0
    for slot in range(dp):
        here = pl.ds(pl.multiple_of(owner_index(place_ref, dp, slot) * count, count), count)
        for t in range(work.shape[1] // 128):
            piece = work[here, t * 128 : t * 128 + 128]
            if slot < dp // 2:
                kept_ref[slot, t * count : (t + 1) * count, :] = piece
            else:
                sent_ref[at : at + count, :] = piece
                at += count


def out_projection_grad(place, act, d_branch, dp):
    width = d_branch[0].shape[1]
    part = act.shape[1]
    shape = (dp // 2, width // 128 * (part // dp), 128)
    sent = (shape[0] * shape[1], 128)
    return pl.pallas_call(
        out_grad_kernel,
        name="out_projection_grad",
        grid=(1,),
        in_specs=[SMEM, fixed(act.shape)] + [fixed(x.shape) for x in d_branch],
        out_specs=[fixed(shape), fixed(sent)],
        out_shape=[jax.ShapeDtypeStruct(shape, bf16), jax.ShapeDtypeStruct(sent, bf16)],
        scratch_shapes=[pltpu.VMEM((part, width), bf16)],
        compiler_params=params(24),
    )(place, act, *d_branch)


def down_grad_kernel(act_ref, grad_ref, out_ref):
    out_ref[...] = mul(act_ref[...], grad_ref[...], 0, 0).astype(bf16)


def down_grad(act, grad):
    length, width = grad.shape
    step = 256
    return pl.pallas_call(
        down_grad_kernel,
        name="down_grad",
        grid=(width // step,),
        in_specs=[fixed(act.shape), pl.BlockSpec((length, step), lambda c: (0, c))],
        out_specs=pl.BlockSpec((act.shape[1], step), lambda c: (0, c)),
        out_shape=jax.ShapeDtypeStruct((act.shape[1], width), bf16),
        compiler_params=params(60),
    )(act, grad)


def simple(kernel, name, args, outs, limit=24):
    return pl.pallas_call(
        kernel,
        name=name,
        grid=(1,),
        in_specs=[SMEM if x.dtype == jnp.int32 else fixed(x.shape) for x in args],
        out_specs=[fixed(x.shape) for x in outs],
        out_shape=outs,
        compiler_params=params(limit),
    )(*args)


def shaped(dtype, *shape):
    return jax.ShapeDtypeStruct(shape, dtype)


def sum_kernel(*refs):
    *ins, out = refs
    out[...] = sum(x[...].astype(f32) for x in ins).astype(out.dtype)


def total(*pieces):
    return simple(sum_kernel, "total", pieces, [shaped(bf16, *pieces[0].shape)])[0]


def halves_kernel(kept_ref, got_ref, near_ref, far_ref):
    rows = near_ref.shape[0]
    near_ref[...] = kept_ref[:rows, :].astype(f32) + got_ref[:rows, :].astype(f32)
    far_ref[...] = (kept_ref[rows:, :].astype(f32) + got_ref[rows:, :].astype(f32)).astype(bf16)


def halves(kept, got):
    rows, width = kept.shape[0] // 2, kept.shape[1]
    return simple(halves_kernel, "halves", (kept, got), [shaped(f32, rows, width), shaped(bf16, rows, width)])


def slots_kernel(kept_ref, got_ref, *outs):
    count = kept_ref.shape[1]
    at = got_ref.shape[0] - len(outs) * count
    for j, out in enumerate(outs):
        got = got_ref[at + j * count : at + (j + 1) * count, :]
        out[...] = (kept_ref[j].astype(f32) + got.astype(f32)).astype(out.dtype)


def slots(kept, got):
    shape = kept.shape[1:]
    outs = [shaped(f32, *shape)] + [shaped(bf16, *shape)] * (kept.shape[0] - 1)
    return simple(slots_kernel, "slots", (kept, got), outs)


def back_through_norm(grad, field, gain):
    scale = lax.rsqrt(jnp.mean(field * field, axis=-1, keepdims=True) + epsilon)
    unit = field * scale
    pressed = grad * gain
    return scale * (pressed - unit * jnp.mean(pressed * unit, axis=-1, keepdims=True))


def branch_kernel(near_ref, far_ref, mid_ref, og_ref, gain_ref, w0, w1, w2, w3, d_mid_ref, d_ref, a0, a1, a2, a3):
    grad = near_ref[...] + far_ref[...].astype(f32)
    d_mid = og_ref[...].astype(f32) + back_through_norm(grad, mid_ref[...], gain_ref[...])
    d_mid_ref[...] = d_mid
    d_branch = d_mid.astype(bf16)
    d_ref[...] = d_branch
    for w, a in ((w0, a0), (w1, a1), (w2, a2), (w3, a3)):
        a[...] = mul(d_branch, w[...], 1, 1).astype(bf16)


def token_grad_kernel(near_ref, far_ref, tok_ref, gain_ref, d_mid_ref, out_ref):
    grad = near_ref[...] + far_ref[...].astype(f32)
    out_ref[...] = (d_mid_ref[...] + back_through_norm(grad, tok_ref[...].astype(f32), gain_ref[...])).astype(bf16)


def cut_kernel(me_ref, *refs):
    ins, d_ref, (mine_ref, near_ref, far_ref) = refs[:-4], refs[-4], refs[-3:]
    groups = [ins[:4], ins[4:8], ins[8:]]
    count = far_ref.shape[0] - 2 * mine_ref.shape[0]
    far_ref[2 * mine_ref.shape[0] :, :] = d_ref[pl.ds(pl.multiple_of(((me_ref[0] >> 1) ^ 1) * count, count), count), 256:]
    me = me_ref[0]
    at = 0
    for pieces in groups:
        chunk = pieces[0].shape[0] // SEQ

        def chunk_of(s):
            here = pl.ds(pl.multiple_of(s * chunk, 8), chunk)
            return sum(x[here, :].astype(f32) for x in pieces).astype(bf16)

        mine_ref[at : at + chunk, :] = chunk_of(me)
        near_ref[at : at + chunk, :] = chunk_of(me ^ 1)
        for core in range(2):
            row = core * mine_ref.shape[0] + at
            far_ref[row : row + chunk, :] = chunk_of(((me >> 1) ^ 1) * 2 + core)
        at += chunk


def cut(me, attn, ffn, d_pair):
    rows = (attn[0][0].shape[0] * 2 + ffn[0].shape[0]) // SEQ
    outs = [shaped(bf16, n, 128) for n in (rows, rows, 2 * rows + d_pair.shape[0] // 2)]
    return simple(cut_kernel, "cut", (me, *attn[0], *attn[1], *ffn, d_pair), outs)


def relay_kernel(me_ref, near, far, d0_ref, d1_ref, far0_ref, out_ref):
    me = me_ref[0]
    core = (me & 1) ^ 1
    count = near.shape[0]
    out_ref[:count, :] = near[...]
    out_ref[count : 2 * count, :] = far[pl.ds(pl.multiple_of(core * count, 8), count), :]
    at = 2 * count
    rows = far0_ref.shape[0] // 2
    first = pl.multiple_of((me ^ 1) * rows, rows)
    for d_ref, far_ref, row in ((d0_ref, far0_ref, 0), (d1_ref, far, 2 * count)):
        out_ref[at : at + rows, :] = d_ref[pl.ds(first, rows), 256:]
        out_ref[at + rows : at + 2 * rows, :] = far_ref[pl.ds(pl.multiple_of(row + core * rows, 8), rows), :]
        at += 2 * rows


def value_grad_kernel(me_ref, acc_ref, d0_ref, d1_ref, far0_ref, far, got_ref, out_ref):
    me = me_ref[0]
    rows = acc_ref.shape[0]
    first = pl.multiple_of(me * rows, rows)
    at = far.shape[0] - 2 * rows

    for p, (d_ref, far_ref, row) in enumerate(((d0_ref, far0_ref, 0), (d1_ref, far, at))):
        pieces = (
            d_ref[pl.ds(first, rows), 256:],
            got_ref[at : at + rows, :],
            far_ref[pl.ds(pl.multiple_of(row + (me & 1) * rows, 8), rows), :],
            got_ref[at + rows : at + 2 * rows, :],
        )
        for k, piece in enumerate(pieces):
            lanes = pl.ds(pl.multiple_of((me ^ k) * 256 + p * 128, 128), 128)
            out_ref[:, lanes] = acc_ref[:, lanes] + piece.astype(f32)
        at += 2 * rows


def finish_kernel(
    me_ref, mine, far, got_ref, o0, o1, o2, o3, wq, wk, wv, wg, wu, ga_ref, gm_ref, down_ref,
    gq_ref, gk_ref, gv_ref, go_ref, gga_ref, gg_ref, gu_ref, ggm_ref, gd_ref, cols_a, cols_f,
):
    me = me_ref[0]
    gd_ref[...] = down_ref[...].astype(f32)
    count = mine.shape[0]
    at = 0
    for cols in (cols_a, cols_f):
        chunk = cols.shape[1]
        cols[0] = mine[at : at + chunk, :]
        cols[2] = far[pl.ds(pl.multiple_of((me & 1) * count + at, 8), chunk), :]
        cols[1] = got_ref[at : at + chunk, :]
        cols[3] = got_ref[count + at : count + at + chunk, :]
        at += chunk
    out = sum(x[...].astype(f32) for x in (o0, o1, o2, o3))
    w_rows, width = gq_ref.shape
    for t in range(width // 128):
        go_ref[:, t * 128 : t * 128 + 128] = out[t * w_rows : (t + 1) * w_rows, :]
    unpack_attn(me, cols_a, gq_ref, gk_ref, gv_ref)
    gga_ref[...] = gain_grad(((wq, gq_ref), (wk, gk_ref), (wv, gv_ref)), ga_ref)
    unpack_ffn(me, cols_f, gg_ref, gu_ref)
    ggm_ref[...] = gain_grad(((wg, gg_ref), (wu, gu_ref)), gm_ref)


def gain_grad(pairs, gain_ref):
    column = sum(jnp.sum(w[...].astype(f32) * g[...], axis=1, keepdims=True) for w, g in pairs)
    rows = column.shape[0]
    same = lax.broadcasted_iota(jnp.int32, (rows, rows), 0) == lax.broadcasted_iota(jnp.int32, (rows, rows), 1)
    return jnp.sum(jnp.where(same, column, 0.0), axis=0, keepdims=True) / gain_ref[...].astype(f32)


def unpack_attn(me, cols_ref, *outs):
    w_rows, width = outs[0].shape
    part = width // SEQ
    for s in range(SEQ):
        at = 0
        for t in range(part // 128):
            for ref in outs:
                lanes = slice(s * part + t * 128, s * part + t * 128 + 128)
                ref[:, lanes] = cols_ref[me ^ s, at : at + w_rows, :].astype(f32)
                at += w_rows


def unpack_ffn(me, cols_ref, gg_ref, gu_ref):
    w_rows = gg_ref.shape[0]
    inner = gg_ref.shape[1] // SEQ
    main = main_lanes(inner)
    rest = inner - main
    half = main // 128
    for s in range(SEQ):
        slot = me ^ s
        tiles = [cols_ref[slot, t * w_rows : (t + 1) * w_rows, :].astype(f32) for t in range(2 * inner // 128)]
        gg_ref[:, s * inner : (s + 1) * inner] = jnp.concatenate(tiles[:half] + [tiles[-1][:, :rest]], axis=1)
        gu_ref[:, s * inner : (s + 1) * inner] = jnp.concatenate(tiles[half : 2 * half] + [tiles[-1][:, rest:]], axis=1)


def unpack_kernel(me_ref, cols_a, cols_f, wq, wk, wv, wg, wu, ga_ref, gm_ref, gq_ref, gk_ref, gv_ref, gga_ref, gg_ref, gu_ref, ggm_ref):
    unpack_attn(me_ref[0], cols_a, gq_ref, gk_ref, gv_ref)
    gga_ref[...] = gain_grad(((wq, gq_ref), (wk, gk_ref), (wv, gv_ref)), ga_ref)
    unpack_ffn(me_ref[0], cols_f, gg_ref, gu_ref)
    ggm_ref[...] = gain_grad(((wg, gg_ref), (wu, gu_ref)), gm_ref)


def input_grad_kernel(me_ref, *refs):
    *d_refs, w_ref, kept_ref, sent_ref = refs
    step = pl.program_id(0)
    d_qkv = [d[:, i * 128 : i * 128 + 128] for i in range(3) for d in d_refs]
    grad = mul(jnp.concatenate(d_qkv, axis=1), w_ref[...], 1, 1).astype(bf16)
    rows = grad.shape[0]
    for k in range(SEQ):

        @pl.when(step == SEQ - 1 - k)
        def _():
            (sent_ref if k % 2 else kept_ref)[k // 2 * rows : (k // 2 + 1) * rows, :] = grad


def input_grad(me, d_qkv, w):
    length, part = d_qkv[0].shape
    width = w.shape[0]
    rows = length // SEQ
    here = lambda k, m: (m[0] ^ (SEQ - 1 - k), 0)
    return pl.pallas_call(
        input_grad_kernel,
        name="input_grad",
        grid_spec=pltpu.PrefetchScalarGridSpec(
            num_scalar_prefetch=1,
            grid=(SEQ,),
            in_specs=[pl.BlockSpec((rows, part), here)] * len(d_qkv) + [fixed(w.shape)],
            out_specs=[fixed((2 * rows, width))] * 2,
        ),
        out_shape=[jax.ShapeDtypeStruct((2 * rows, width), bf16)] * 2,
        compiler_params=params(16),
    )(me, *d_qkv, w)


def to_core(value):
    return lax.ppermute(value, "seq", [(i, i ^ 1) for i in range(SEQ)])


def to_chip(value):
    return lax.ppermute(value, "seq", [(i, i ^ 2) for i in range(SEQ)])


def to_both(value):
    return lax.ppermute(value, "seq", [(i, i ^ 3) for i in range(SEQ)])


def gather_rel(value):
    far = to_chip(value)
    return value, to_core(value), far, to_core(far)


def exchange_rel(pieces):
    return [pieces[0], to_core(pieces[1]), to_chip(pieces[2]), to_both(pieces[3])]


def scatter_sum(kept, sent):
    sums = add(kept, to_core(sent))
    rows = kept.shape[0] // 2
    return sums[:rows] + to_chip(sums[rows:].astype(bf16)).astype(f32)


def add(a, b):
    return a.astype(f32) + b.astype(f32)


def to_y(value):
    dp = lax.axis_size("dp")
    return lax.ppermute(value, "dp", [(i, i ^ 1) for i in range(dp)])


def to_z(value, hops=1):
    dp = lax.axis_size("dp")
    return lax.ppermute(value, "dp", [(i, (i + 2 * hops) % dp) for i in range(dp)])


def rotary(length, head_width):
    pairs = jnp.arange(head_width // 2, dtype=f32)
    freq = jnp.exp(pairs * (-2.0 * math.log(10000.0) / head_width))
    theta = jnp.arange(length, dtype=jnp.int32).astype(f32)[:, None] * freq[None, :]
    cos, sin = jnp.cos(theta), jnp.sin(theta)
    return jnp.concatenate([cos] * 4, axis=1), jnp.concatenate([-sin, sin] * 2, axis=1)


class Stage:
    def fence(self):
        names = list(vars(self))
        for name, value in zip(names, sync(*[getattr(self, name) for name in names])):
            setattr(self, name, value)


def body_direct(
    tokens, first_values, value_grad_acc, segment_ids, query_weight, key_weight, value_weight, out_weight,
    attn_gain, gate_weight, up_weight, down_weight, mlp_gain, out_grad,
):
    dp = lax.axis_size("dp")
    zs = dp // 2
    rows, width = tokens.shape[1:]
    length = segment_ids.shape[1]
    w_rows = query_weight.shape[0]
    part = width // SEQ
    inner = gate_weight.shape[1] // SEQ
    me = lax.axis_index("seq").astype(jnp.int32)
    mine = lax.axis_index("dp").astype(jnp.int32)
    me_arg = me[None]
    place = jnp.stack([me, me * dp + mine, mine])
    s = Stage()

    half = rows // 2
    *s.cols, s.orows, drows, tok_a, tok_b = pack_attn(
        query_weight, key_weight, value_weight, out_weight, down_weight, attn_gain, mlp_gain, tokens[0]
    )
    s.r, s.tok_far = [drows], [tok_a, tok_b]
    s.tokens, s.first, s.out_grad, s.segments = tokens[0], first_values[0], out_grad[0], segment_ids
    s.gate, s.up = gate_weight, up_weight
    s.fence()
    s.cols = exchange_rel(s.cols)
    s.ry = [to_y(s.r[0])]
    s.r.append(to_z(s.r[0]))
    s.fence()
    s.a = [jnp.concatenate([*s.cols, s.orows])]
    del s.cols, s.orows
    s.tok_far[0] = to_chip(s.tok_far[0])
    s.ay = [to_y(s.a[0])]
    s.a.append(to_z(s.a[0]))
    s.fcols = pack_ffn(place, s.gate, s.up)
    del s.gate, s.up
    s.fence()
    s.ay.append(to_y(s.a[1]))
    s.a.append(to_z(s.a[1]))
    s.f_piece = jnp.concatenate(exchange_rel(s.fcols))
    s.cos, s.sin = rotary(length, width // HEADS)
    del s.fcols
    s.fence()
    ffn_all = lax.all_gather(s.f_piece, "dp", axis=0, tiled=False)
    del s.f_piece
    s.tok_far[1] = to_chip(s.tok_far[1])
    s.ay.append(to_y(s.a[2]))
    s.a.append(to_z(s.a[2]))
    s.tok_near = to_core(s.tokens)
    s.first = [lax.dynamic_slice_in_dim(s.first, (me ^ k) * part, part, 1) for k in range(SEQ)]
    s.og_far = [s.out_grad[:half], s.out_grad[half:]]
    s.fence()
    s.ay.append(to_y(s.a[3]))
    s.first = jnp.concatenate(exchange_rel(s.first))
    tok_far = jnp.concatenate(s.tok_far)
    s.tok = jnp.concatenate([s.tokens, s.tok_near, tok_far, to_core(tok_far)])
    del s.tok_far, s.tok_near
    s.fence()
    s.ry.append(to_y(s.r[1]))
    s.r.append(to_z(s.r[1]))
    s.og_far[0] = to_chip(s.og_far[0])
    s.og = [s.out_grad, to_core(s.out_grad)]
    s.w_qkv, s.w_out, attn_gain_all, mlp_gain_all = assemble_attn(place, s.a + s.ay, width)
    s.attn_gain, s.mlp_gain = attn_gain_all.reshape(1, width), mlp_gain_all.reshape(1, width)
    s.nin, s.q, s.k, s.v = qkv_call(me_arg, s.tok, s.first, s.w_qkv, s.attn_gain, s.cos, s.sin)
    del s.a, s.ay, s.first
    s.fence()
    s.og_far[1] = to_chip(s.og_far[1])
    s.wo = [s.w_out, to_core(s.w_out), to_chip(s.w_out)]
    s.ry.append(to_y(s.r[2]))
    s.r.append(to_z(s.r[2]))
    s.attended, s.lse = attend_call(s.q, s.k, s.v, s.segments)
    del s.w_out
    s.fence()
    att_far = to_chip(s.attended)
    s.w_down = assemble_rows(place, s.r + s.ry + [to_y(s.r[3])], width, inner)
    s.att = [s.attended, to_core(s.attended), att_far]
    s.wo.append(to_core(s.wo[2]))
    og_far = jnp.concatenate(s.og_far)
    s.og = jnp.concatenate([*s.og, og_far, to_core(og_far)])
    del s.r, s.ry, s.og_far
    s.fence()
    s.att.append(to_core(s.att[2]))
    s.fence()
    s.nm, s.hidden, s.d_gu, s.mid, s.dnm, dnm_sent, s.lo, s.lo_sent = ffn_call(
        me_arg, s.tok, s.og, s.att, s.wo, s.mlp_gain, ffn_all, s.w_down
    )
    s.dnm, s.dnm_far = halves(s.dnm, to_core(dnm_sent))
    del s.tok, s.att, s.w_down
    s.fence()
    s.dnm_far = to_chip(s.dnm_far)
    pieces = list(columns_grad(place, s.nm, s.d_gu, dp))
    s.f_kept, s.f_sent = pieces[:zs], pieces[zs:]
    s.g_down = down_grad(after(s.hidden, pieces[0]), s.og)
    g_down = lax.psum_scatter(s.g_down, "dp", scatter_dimension=0, tiled=True)
    del s.nm, s.d_gu, s.hidden, s.og
    s.fence()
    s.f_sent[3] = to_y(s.f_sent[3])
    lo_got = to_core(s.lo_sent)
    s.d_middle, s.d_branch, *s.d_att = simple(
        branch_kernel,
        "branch",
        (s.dnm, s.dnm_far, s.mid, s.out_grad, s.mlp_gain, *s.wo),
        [shaped(f32, rows, width), shaped(bf16, rows, width)] + [shaped(bf16, rows, part)] * SEQ,
    )
    s.lo, s.lo_far = halves(s.lo, lo_got)
    del s.dnm, s.dnm_far, s.wo, s.lo_sent, s.g_down
    s.fence()
    s.d_att = exchange_rel(s.d_att)
    s.f_sent[2] = to_y(s.f_sent[2])
    s.f = to_z(total(s.f_kept[3], s.f_sent[3]))
    s.fence()

    def back(pair, *along):
        return attend_back_call(
            pair, place, s.q, s.k, s.v, s.d_att, s.lse, s.segments, s.cos, s.sin, s.nin, dp, True, along
        )

    def other_chip_values(d_pair):
        return lax.dynamic_slice(d_pair, (((me >> 1) ^ 1) * 2 * rows, 256), (2 * rows, 128))

    s.f_sent[1] = to_y(s.f_sent[1])
    s.f = to_z(total(s.f_kept[2], s.f_sent[2], s.f))
    s.d_branch = [s.d_branch, to_core(s.d_branch), to_chip(s.d_branch)]
    d_pair, kept, sent = back(0, s.f_sent[0])
    s.d_qkv, s.kept, s.sent = [d_pair], [kept], [sent]
    s.fence()
    s.sent[0] = to_y(s.sent[0])
    s.f = to_z(total(s.f_kept[1], s.f_sent[1], s.f))
    s.lo_far = to_chip(s.lo_far)
    s.d_branch.append(to_core(s.d_branch[2]))
    s.values_far = to_chip(other_chip_values(s.d_qkv[0]))
    d_pair, kept, sent = back(1)
    s.d_qkv.append(d_pair)
    s.dnin, s.dnin_sent = input_grad(me_arg, s.d_qkv, s.w_qkv)
    s.kept.append(kept)
    s.sent.append(sent)
    del s.nin, s.d_att, s.w_qkv
    s.fence()

    def over_z(first, *others):
        return [first] + [to_z(piece, j + 1) for j, piece in enumerate(others)]

    s.sent[1] = to_y(s.sent[1])
    s.kept[0] = over_z(*slots(s.kept[0], s.sent[0]))
    s.dnin, s.dnin_far = halves(s.dnin, to_core(s.dnin_sent))
    s.out_kept, s.out_sent = out_projection_grad(place, s.attended, s.d_branch, dp)
    del s.d_branch, s.attended, s.dnin_sent
    s.fence()
    s.kept[1] = over_z(*slots(s.kept[1], s.sent[1]))
    s.out_kept = slots(s.out_kept, to_y(s.out_sent))
    s.dnin_far = to_chip(s.dnin_far)
    s.layer_out = total(s.mid, s.lo, s.lo_far)
    del s.lo, s.lo_far, s.mid
    s.fence()
    s.mine, s.near, far = cut(me_arg, s.kept, (s.f_kept[0], s.sent[0], s.f), s.d_qkv[1])
    s.far = to_chip(far)
    s.out_kept = over_z(*s.out_kept)
    s.token_grad = simple(
        token_grad_kernel,
        "token_grad",
        (s.dnin, s.dnin_far, s.tokens, s.attn_gain, s.d_middle),
        [shaped(bf16, rows, width)],
        60,
    )[0]
    s.g_down = g_down
    del s.kept, s.sent, s.out_sent, s.dnin, s.d_middle, s.f, s.f_kept, s.f_sent
    s.fence()
    count = s.mine.shape[0]
    args = (me_arg, s.near, s.far, *s.d_qkv, s.values_far)
    got = to_core(simple(relay_kernel, "relay", args, [shaped(bf16, 2 * count + SEQ * rows, 128)])[0])
    weights = (query_weight, key_weight, value_weight, gate_weight, up_weight)
    shapes = [(w_rows, width)] * 4 + [(1, w_rows)] + [(w_rows, SEQ * inner)] * 2 + [(1, w_rows), g_down.shape]
    args = (s.mine, s.far, got, *s.out_kept, *weights, attn_gain[None], mlp_gain[None], s.g_down)
    a_rows = 3 * part // 128 * w_rows
    g_q, g_k, g_v, g_out, attn_gain_grad, g_gate, g_up, mlp_gain_grad, g_down = pl.pallas_call(
        finish_kernel,
        name="finish",
        grid=(1,),
        in_specs=[SMEM] + [fixed(x.shape) for x in args],
        out_specs=[fixed(x) for x in shapes],
        out_shape=[shaped(f32, *x) for x in shapes],
        scratch_shapes=[pltpu.VMEM((SEQ, a_rows, 128), bf16), pltpu.VMEM((SEQ, count - a_rows, 128), bf16)],
        compiler_params=params(24),
    )(me_arg, *args)
    value_grad_out = simple(
        value_grad_kernel,
        "value_grad",
        (me_arg, value_grad_acc[0], *s.d_qkv, s.values_far, s.far, got),
        [shaped(f32, rows, width)],
    )[0]
    return (
        s.layer_out[None],
        s.token_grad[None],
        value_grad_out[None],
        g_q,
        g_k,
        g_v,
        g_out,
        attn_gain_grad[0],
        g_gate,
        g_up,
        g_down,
        mlp_gain_grad[0],
    )


def body_plain(
    tokens, first_values, value_grad_acc, segment_ids, query_weight, key_weight, value_weight, out_weight,
    attn_gain, gate_weight, up_weight, down_weight, mlp_gain, out_grad,
):
    dp = lax.axis_size("dp")
    rows, width = tokens.shape[1:]
    length = segment_ids.shape[1]
    w_rows, d_rows = query_weight.shape[0], down_weight.shape[0]
    part = width // SEQ
    inner = gate_weight.shape[1] // SEQ
    main = main_lanes(inner)
    me = lax.axis_index("seq").astype(jnp.int32)
    mine = lax.axis_index("dp").astype(jnp.int32)
    me_arg = me[None]
    place = jnp.stack([me, me * dp + mine, mine])

    def columns(weight, count):
        return weight.reshape(w_rows, SEQ, count).transpose(1, 0, 2)

    owner = jnp.arange(width) // w_rows == me * dp + mine

    def spread(gain):
        full = jnp.where(owner, jnp.tile(gain, width // w_rows), jnp.zeros((), bf16))
        cut = 3 * part
        return jnp.stack([full[:cut], jnp.pad(full[cut:], (0, 2 * cut - width))])

    gains = jnp.concatenate([spread(attn_gain), spread(mlp_gain), jnp.zeros((4, 3 * part), bf16)])
    attn_cols = jnp.concatenate([columns(w, part) for w in (query_weight, key_weight, value_weight)], axis=2)
    attn_cols = jnp.concatenate([attn_cols, jnp.broadcast_to(gains[None], (SEQ,) + gains.shape)], axis=1)
    gate_cols, up_cols = columns(gate_weight, inner), columns(up_weight, inner)
    ffn_cols = jnp.concatenate(
        [gate_cols[:, :, :main], up_cols[:, :, :main], gate_cols[:, :, main:], up_cols[:, :, main:]], axis=2
    )
    attn_cols = lax.all_to_all(attn_cols, "seq", split_axis=0, concat_axis=0, tiled=True)
    ffn_cols = lax.all_to_all(ffn_cols, "seq", split_axis=0, concat_axis=0, tiled=True)
    attn_all = lax.all_gather(attn_cols.reshape(-1, 3 * part), "dp", axis=0, tiled=True)
    attn_all = attn_all.reshape(dp, SEQ, w_rows + 8, 3 * part)
    w_qkv = attn_all[:, :, :w_rows].transpose(1, 0, 2, 3).reshape(width, 3 * part)
    gain_all = jnp.sum(attn_all[:, :, w_rows : w_rows + 4].astype(f32), axis=(0, 1))
    attn_gain_all = jnp.concatenate([gain_all[0], gain_all[1]])[None, :width]
    mlp_gain_all = jnp.concatenate([gain_all[2], gain_all[3]])[None, :width]
    w_out = lax.all_gather(out_weight, "dp", axis=0, tiled=True)
    w_down = lax.all_gather(down_weight, "dp", axis=0, tiled=True)
    ffn_all = lax.all_gather(ffn_cols.reshape(-1, 2 * inner), "dp", axis=0, tiled=True)
    w_ffn = ffn_all.reshape(dp, SEQ, w_rows, 2 * inner).transpose(1, 0, 2, 3).reshape(width, 2 * inner)

    cos, sin = rotary(length, width // HEADS)
    tok = jnp.concatenate(gather_rel(tokens[0]))
    og = jnp.concatenate(gather_rel(out_grad[0]))
    first_cols = first_values[0].reshape(rows, SEQ, part)
    first = exchange_rel([lax.dynamic_index_in_dim(first_cols, me ^ k, 1, keepdims=False) for k in range(SEQ)])
    nin, q, k, v = qkv_call(me_arg, tok, jnp.concatenate(first), w_qkv, attn_gain_all, cos, sin)
    attended, lse = attend_call(q, k, v, segment_ids)
    wo = gather_rel(w_out)
    nm, hidden, d_gu, mid, *sums = ffn_call(me_arg, tok, og, gather_rel(attended), wo, mlp_gain_all, w_ffn, w_down)
    layer_out = (mid + scatter_sum(*sums[2:])).astype(bf16)
    d_middle = out_grad[0].astype(f32) + back_through_norm(scatter_sum(*sums[:2]), mid, mlp_gain_all)
    d_branch = d_middle.astype(bf16)
    d_att = exchange_rel([mul(d_branch, w, 1, 1).astype(bf16) for w in wo])
    d_branch_all = jnp.stack(gather_rel(d_branch))[me ^ jnp.arange(SEQ)].reshape(length, width)
    d_qkv = [
        attend_back_call(pair, place, q, k, v, d_att, lse, segment_ids, cos, sin, nin, dp, False)[0] for pair in range(2)
    ]
    dnin = scatter_sum(*input_grad(me_arg, d_qkv, w_qkv))
    token_grad = d_middle + back_through_norm(dnin, tokens[0].astype(f32), attn_gain_all)
    dv = jnp.concatenate([d[:, 256:] for d in d_qkv], axis=1)
    dv = exchange_rel([lax.dynamic_slice_in_dim(dv, (me ^ i) * rows, rows, 0) for i in range(SEQ)])
    dv = jnp.stack(dv)[me ^ jnp.arange(SEQ)].transpose(1, 0, 2).reshape(rows, width)
    value_grad_out = value_grad_acc[0] + dv.astype(f32)

    def over_dp(grads):
        return lax.psum_scatter(grads.reshape(-1, 128), "dp", scatter_dimension=0, tiled=True)

    def to_rows(sums):
        sums = sums.reshape(SEQ, -1, 128)
        return jnp.stack(exchange_rel([lax.dynamic_index_in_dim(sums, me ^ i, 0, keepdims=False) for i in range(SEQ)]))

    attn_sums = over_dp(columns_grad_plain(nin, jnp.concatenate(d_qkv, axis=1), dp))
    ffn_sums = over_dp(columns_grad_plain(nm, d_gu, dp))
    g_out = lax.psum_scatter(mul(attended, d_branch_all, 0, 0).astype(bf16), "dp", scatter_dimension=0, tiled=True)
    g_down = lax.psum_scatter(mul(hidden, og, 0, 0).astype(bf16), "dp", scatter_dimension=0, tiled=True)
    weights = (query_weight, key_weight, value_weight, gate_weight, up_weight)
    shapes = [(w_rows, width)] * 3 + [(1, w_rows)] + [(w_rows, SEQ * inner)] * 2 + [(1, w_rows)]
    args = (me_arg, to_rows(attn_sums), to_rows(ffn_sums), *weights, attn_gain[None], mlp_gain[None])
    g_q, g_k, g_v, attn_gain_grad, g_gate, g_up, mlp_gain_grad = simple(
        unpack_kernel, "unpack", args, [shaped(f32, *x) for x in shapes]
    )
    return (
        layer_out[None],
        token_grad.astype(bf16)[None],
        value_grad_out[None],
        g_q,
        g_k,
        g_v,
        g_out.astype(f32),
        attn_gain_grad[0],
        g_gate,
        g_up,
        g_down.astype(f32),
        mlp_gain_grad[0],
    )


def solution(mesh):
    token = P("dp", "seq", None)
    weight = P(("seq", "dp"), None)
    gain = P(("seq", "dp"))
    return jax.shard_map(
        body_direct if mesh.shape["dp"] == 8 else body_plain,
        mesh=mesh,
        in_specs=(token, token, token, P("dp", None), weight, weight, weight, weight, gain, weight, weight, weight, gain, token),
        out_specs=(token, token, token, weight, weight, weight, weight, gain, weight, weight, weight, gain),
        check_vma=False,
    )
```

```python
import functools
import math

import jax
import jax.numpy as jnp
from jax import lax
from jax.experimental import pallas as pl
from jax.experimental.pallas import tpu as pltpu
from jax.sharding import PartitionSpec as P

HEADS = 16
DOC_MOST = 512
SEQ = 4
BLOCK = 256

epsilon = 1e-06
masked_value = -1e30
bf16 = jnp.bfloat16
f32 = jnp.float32


def mul(a, b, ca, cb):
    return lax.dot_general(a, b, (((ca,), (cb,)), ((), ())), preferred_element_type=f32)


def params(mib):
    return pltpu.CompilerParams(vmem_limit_bytes=mib << 20)


VMEM = pl.BlockSpec(memory_space=pltpu.VMEM)
SMEM = pl.BlockSpec(memory_space=pltpu.SMEM)


def fixed(shape):
    return pl.BlockSpec(shape, lambda *_: (0,) * len(shape), pipeline_mode=pl.Buffered(1))


def sync(*values):
    return lax.optimization_barrier(values)


def after(value, *earlier):
    return lax.optimization_barrier((value, *earlier))[0]


def half_swap(field):
    lanes = field.shape[-1]
    lane = lax.broadcasted_iota(jnp.int32, field.shape, 1)
    up = pltpu.roll(field, lanes - 32, 1)
    down = pltpu.roll(field, 32, 1)
    return jnp.where(lane % 64 < 32, up, down)


def qkv_kernel(me_ref, tok_ref, first_ref, w_ref, gain_ref, cos_ref, sin_ref, nin_ref, q_ref, k_ref, v_ref):
    x = tok_ref[...].astype(f32)
    scale = lax.rsqrt(jnp.mean(x * x, axis=-1, keepdims=True) + epsilon)
    nin = (x * scale * gain_ref[...]).astype(bf16)
    nin_ref[...] = nin
    lin = mul(nin, w_ref[...], 1, 0)
    cos = jnp.concatenate([cos_ref[...]] * 2, axis=1)
    sin = jnp.concatenate([sin_ref[...]] * 2, axis=1)
    part = lin.shape[1] // 3
    q = lin[:, :part]
    q_ref[...] = ((q * cos + half_swap(q) * sin).astype(bf16).astype(f32) * 0.125).astype(bf16)
    k = lin[:, part : 2 * part]
    k_ref[...] = (k * cos + half_swap(k) * sin).astype(bf16)
    v_ref[...] = (0.5 * lin[:, 2 * part :] + 0.5 * first_ref[...].astype(f32)).astype(bf16)


def qkv_call(me, tok, first, w, gain, cos, sin):
    length, width = tok.shape
    rows = length // SEQ
    part = w.shape[1] // 3
    here = lambda k, m: (m[0] ^ k, 0)
    rel = lambda k, m: (k, 0)
    return pl.pallas_call(
        qkv_kernel,
        name="qkv",
        grid_spec=pltpu.PrefetchScalarGridSpec(
            num_scalar_prefetch=1,
            grid=(SEQ,),
            in_specs=[
                pl.BlockSpec((rows, width), rel),
                pl.BlockSpec((rows, part), rel),
                fixed(w.shape),
                fixed((1, width)),
                pl.BlockSpec((rows, 128), here),
                pl.BlockSpec((rows, 128), here),
            ],
            out_specs=[pl.BlockSpec((rows, width), here)] + [pl.BlockSpec((rows, part), here)] * 3,
        ),
        out_shape=[jax.ShapeDtypeStruct((length, width), bf16)]
        + [jax.ShapeDtypeStruct((length, part), bf16)] * 3,
        compiler_params=params(16),
    )(me, tok, first, w, gain, cos, sin)


def key_range(block):
    return max(0, block * BLOCK - (DOC_MOST // BLOCK) * BLOCK), (block + 1) * BLOCK


def column_of(row_ref):
    return jnp.broadcast_to(row_ref[...].astype(f32), (8, row_ref.shape[1])).T[:, :1]


def allowed_pairs(seg_col, seg_row, block, low, high):
    keys = lax.broadcasted_iota(jnp.int32, (high - low, BLOCK), 0) + low
    rows = lax.broadcasted_iota(jnp.int32, (high - low, BLOCK), 1) + block * BLOCK
    row = seg_row[:, block * BLOCK : (block + 1) * BLOCK].astype(f32)
    return (seg_col[low:high, :] == row) & (keys <= rows)


def head_lanes(field, head):
    lane = lax.broadcasted_iota(jnp.int32, field.shape, 1)
    return jnp.where(lane // 64 == head, field, jnp.zeros_like(field))


def half_rows(head):
    return pl.ds(pl.multiple_of(head * 64, 64), 64)


def attend_kernel(q_ref, k_ref, v_ref, seg_row, o_ref, lse_ref, turned, turned_out):
    length = q_ref.shape[0]
    seg_col = column_of(seg_row)
    turned[...] = v_ref[...].astype(f32).T.astype(bf16)

    def one_head(head, carry):
        for block in range(length // BLOCK):
            low, high = key_range(block)
            allowed = allowed_pairs(seg_col, seg_row, block, low, high)
            here = slice(block * BLOCK, (block + 1) * BLOCK)
            scores = mul(k_ref[low:high, :], head_lanes(q_ref[here, :], head), 1, 1)
            scores = jnp.where(allowed, scores, masked_value)
            top = jnp.max(scores, axis=0, keepdims=True)
            expo = jnp.exp(scores - top)
            total = jnp.sum(expo, axis=0, keepdims=True)
            probs = (expo * (1.0 / total)).astype(bf16)
            turned_out[half_rows(head), here] = mul(turned[half_rows(head), low:high], probs, 1, 0)
            lse_ref[0, pl.ds(head, 1), here] = top + jnp.log(total)
        return carry

    lax.fori_loop(0, 2, one_head, 0)
    for block in range(length // BLOCK):
        here = slice(block * BLOCK, (block + 1) * BLOCK)
        o_ref[here, :] = turned_out[:, here].T.astype(bf16)


def attend_call(q, k, v, seg_row):
    length, part = q.shape
    pairs = part // 128
    lanes = pl.BlockSpec((length, 128), lambda p: (0, p))
    return pl.pallas_call(
        attend_kernel,
        name="attend",
        grid=(pairs,),
        in_specs=[lanes] * 3 + [fixed((1, length))],
        out_specs=[lanes, pl.BlockSpec((1, 2, length), lambda p: (p, 0, 0))],
        out_shape=[jax.ShapeDtypeStruct((length, part), bf16), jax.ShapeDtypeStruct((pairs, 2, length), f32)],
        scratch_shapes=[pltpu.VMEM((128, length), bf16), pltpu.VMEM((128, length), f32)],
        compiler_params=params(24),
    )(q, k, v, seg_row)


def attend_back_kernel(
    dp, pieces, place_ref, q_ref, k_ref, v_ref, d0, d1, d2, d3, lse_ref, seg_row, cos_ref, sin_ref, nin_ref,
    *refs,
):
    outs, (da_ref, dk_sum, dv_sum, work, turned, turned_dq) = refs[:-6], refs[-6:]
    *along, d_ref = outs[: len(outs) - 2 * pieces]
    outs = outs[len(outs) - 2 * pieces :]
    length = q_ref.shape[0]
    rows = d0.shape[0]
    for k, ref in enumerate((d0, d1, d2, d3)):
        da_ref[pl.ds(pl.multiple_of((place_ref[0] ^ k) * rows, rows), rows), :] = ref[...]
    seg_col = column_of(seg_row)
    dk_sum[...] = jnp.zeros_like(dk_sum)
    dv_sum[...] = jnp.zeros_like(dv_sum)
    turned[...] = k_ref[...].astype(f32).T.astype(bf16)

    def one_head(head, carry):
        for block in range(length // BLOCK):
            low, high = key_range(block)
            allowed = allowed_pairs(seg_col, seg_row, block, low, high)
            here = slice(block * BLOCK, (block + 1) * BLOCK)
            q_head = head_lanes(q_ref[here, :], head)
            da_head = head_lanes(da_ref[here, :], head)
            scores = mul(k_ref[low:high, :], q_head, 1, 1)
            probs = jnp.where(allowed, jnp.exp(scores - lse_ref[0, pl.ds(head, 1), here]), 0.0)
            d_probs = mul(v_ref[low:high, :], da_head, 1, 1)
            delta = jnp.sum(probs * d_probs, axis=0, keepdims=True)
            d_scores = (probs * (d_probs - delta)).astype(bf16)
            turned_dq[half_rows(head), here] = mul(turned[half_rows(head), low:high], d_scores, 1, 0)
            dk_sum[low:high, :] += mul(d_scores, q_head, 1, 0)
            dv_sum[low:high, :] += mul(probs.astype(bf16), da_head, 1, 0)
        return carry

    lax.fori_loop(0, 2, one_head, 0)
    for block in range(length // BLOCK):
        here = slice(block * BLOCK, (block + 1) * BLOCK)
        dq = turned_dq[:, here].T * 0.125
        d_ref[here, :128] = (dq * cos_ref[here, :] - half_swap(dq) * sin_ref[here, :]).astype(bf16)
    dk = dk_sum[...]
    d_ref[:, 128:256] = (dk * cos_ref[...] - half_swap(dk) * sin_ref[...]).astype(bf16)
    d_ref[:, 256:] = (0.5 * dv_sum[...]).astype(bf16)
    if not outs:
        return
    kept_ref, sent_ref = outs
    part = work.shape[0]
    w_rows = part // dp
    first = 0
    if along:
        first = along[0].shape[0]
        sent_ref[:first, :] = along[0][...]
    for s in range(SEQ):
        work[...] = mul(nin_ref[:, s * part : (s + 1) * part], d_ref[...], 0, 0).astype(bf16)
        for slot in range(dp):
            here = pl.ds(pl.multiple_of(owner_index(place_ref, dp, slot) * w_rows, w_rows), w_rows)
            for t in range(3):
                at = (s * 3 + t) * w_rows
                piece = work[here, t * 128 : t * 128 + 128]
                if slot < dp // 2:
                    kept_ref[slot, at : at + w_rows, :] = piece
                else:
                    at += first + (slot - dp // 2) * kept_ref.shape[1]
                    sent_ref[at : at + w_rows, :] = piece


def attend_back_call(pair, place, q, k, v, da, lse, seg_row, cos, sin, nin, dp, pieces, along=()):
    length, width = nin.shape
    part = width // SEQ
    lanes = pl.BlockSpec((length, 128), lambda _: (0, pair), pipeline_mode=pl.Buffered(1))
    outs = [(length, 384)]
    if pieces:
        rows = 3 * width // dp
        outs += [(dp // 2, rows, 128), (sum(x.shape[0] for x in along) + dp // 2 * rows, 128)]
    return pl.pallas_call(
        functools.partial(attend_back_kernel, dp, pieces),
        name="attend_back",
        grid=(1,),
        in_specs=[SMEM]
        + [lanes] * 3
        + [pl.BlockSpec((length // SEQ, 128), lambda _: (0, pair), pipeline_mode=pl.Buffered(1))] * 4
        + [pl.BlockSpec((1, 2, length), lambda _: (pair, 0, 0)), fixed((1, length))]
        + [fixed((length, 128))] * 2
        + [fixed(nin.shape)]
        + [fixed(x.shape) for x in along],
        out_specs=[fixed(x) for x in outs],
        out_shape=[jax.ShapeDtypeStruct(x, bf16) for x in outs],
        scratch_shapes=[pltpu.VMEM((length, 128), bf16)]
        + [pltpu.VMEM((length, 128), f32)] * 2
        + [pltpu.VMEM((part, 384), bf16), pltpu.VMEM((128, length), bf16), pltpu.VMEM((128, length), f32)],
        compiler_params=params(60),
    )(place, q, k, v, *da, lse, seg_row, cos, sin, nin, *along)


def main_lanes(inner):
    return inner // 128 * 128


def pack_attn_kernel(
    q_ref, k_ref, v_ref, o_ref, d_ref, ag_ref, mg_ref, tok_ref, c0, c1, c2, c3, orows_ref, drows_ref, *halves_refs
):
    me = lax.axis_index("seq")
    owner = me * lax.axis_size("dp") + lax.axis_index("dp")
    w_rows, width = q_ref.shape
    part = width // SEQ
    lane = lax.broadcasted_iota(jnp.int32, (1, 128), 1)
    spot = lane // w_rows == owner % (128 // w_rows)

    def spread(gain):
        return jnp.where(spot, jnp.concatenate([gain[...].astype(f32)] * (128 // w_rows), axis=1), 0.0)

    row = lax.broadcasted_iota(jnp.int32, (16, 128), 0)
    gains = jnp.where(row == 0, spread(ag_ref), jnp.where(row == 1, spread(mg_ref), 0.0)).astype(bf16)
    for k, out in enumerate((c0, c1, c2, c3)):
        at = 0
        for ref in (q_ref, k_ref, v_ref):
            for t in range(part // 128):
                lanes = pl.ds(pl.multiple_of((me ^ k) * part + t * 128, 128), 128)
                out[at : at + w_rows, :] = ref[:, lanes]
                at += w_rows
        out[at : at + 16, :] = gains
    for ref, out in ((o_ref, orows_ref), (d_ref, drows_ref)):
        rows = ref.shape[0]
        for t in range(width // 128):
            out[t * rows : (t + 1) * rows, :] = ref[:, t * 128 : t * 128 + 128]
    for i, out in enumerate(halves_refs):
        rows = out.shape[0]
        out[...] = tok_ref[i * rows : (i + 1) * rows, :]


def pack_attn(wq, wk, wv, wo, wd, attn_gain, mlp_gain, tok):
    w_rows, width = wq.shape
    tiles = width // 128
    shapes = [(3 * tiles // SEQ * w_rows + 16, 128)] * 4 + [(tiles * w_rows, 128), (tiles * wd.shape[0], 128)]
    shapes += [(tok.shape[0] // 2, width)] * 2
    return pl.pallas_call(
        pack_attn_kernel,
        name="pack_attn",
        grid=(1,),
        in_specs=[fixed(w.shape) for w in (wq, wk, wv, wo, wd)] + [fixed((1, w_rows))] * 2 + [fixed(tok.shape)],
        out_specs=[fixed(x) for x in shapes],
        out_shape=[jax.ShapeDtypeStruct(x, bf16) for x in shapes],
        compiler_params=params(60),
    )(wq, wk, wv, wo, wd, attn_gain[None], mlp_gain[None], tok)


def pack_ffn_kernel(place_ref, g_ref, u_ref, c0, c1, c2, c3):
    me = place_ref[0]
    w_rows = g_ref.shape[0]
    inner = g_ref.shape[1] // SEQ
    main = main_lanes(inner)
    for s in range(SEQ):
        gate, up = g_ref[:, s * inner : (s + 1) * inner], u_ref[:, s * inner : (s + 1) * inner]
        tiles = [field[:, t * 128 : t * 128 + 128] for field in (gate, up) for t in range(main // 128)]
        tiles.append(jnp.concatenate([gate[:, main:], up[:, main:]], axis=1))
        for k, out in enumerate((c0, c1, c2, c3)):

            @pl.when(me ^ k == s)
            def _():
                for t, tile in enumerate(tiles):
                    out[t * w_rows : (t + 1) * w_rows, :] = tile


def pack_ffn(place, wg, wu):
    w_rows = wg.shape[0]
    inner = wg.shape[1] // SEQ
    return pl.pallas_call(
        pack_ffn_kernel,
        name="pack_ffn",
        grid=(1,),
        in_specs=[SMEM] + [fixed(w.shape) for w in (wg, wu)],
        out_specs=[fixed((2 * inner // 128 * w_rows, 128))] * 4,
        out_shape=[jax.ShapeDtypeStruct((2 * inner // 128 * w_rows, 128), bf16)] * 4,
        compiler_params=params(60),
    )(place, wg, wu)


def source_of(place_ref, dp, slot):
    groups = dp // 2
    b, j = slot // groups, slot % groups
    z, y = place_ref[2] // 2, place_ref[2] % 2
    return ((z + groups - j) % groups) * 2 + (y ^ b)


def assemble_attn_kernel(place_ref, *refs):
    dp = len(refs) - 4
    pieces, (w_ref, wo_ref, ag_ref, mg_ref) = refs[:dp], refs[dp:]
    width, lanes = w_ref.shape
    w_rows = width // (SEQ * dp)
    part = width // SEQ
    chunk = lanes // 128 * w_rows + 16
    ag_ref[...] = jnp.zeros_like(ag_ref)
    mg_ref[...] = jnp.zeros_like(mg_ref)
    for slot, piece in enumerate(pieces):
        src = source_of(place_ref, dp, slot)
        for k in range(SEQ):
            s = place_ref[0] ^ k
            row = pl.multiple_of(s * part + src * w_rows, w_rows)
            for t in range(lanes // 128):
                at = k * chunk + t * w_rows
                w_ref[pl.ds(row, w_rows), t * 128 : t * 128 + 128] = piece[at : at + w_rows, :]
            gains = piece[(k + 1) * chunk - 16 : (k + 1) * chunk, :].astype(f32)
            tile = (s * dp + src) * w_rows // 128
            ag_ref[pl.ds(tile, 1), :] += gains[0:1, :]
            mg_ref[pl.ds(tile, 1), :] += gains[1:2, :]
        row = pl.multiple_of(src * w_rows, w_rows)
        for t in range(width // 128):
            at = SEQ * chunk + t * w_rows
            wo_ref[pl.ds(row, w_rows), t * 128 : t * 128 + 128] = piece[at : at + w_rows, :]


def assemble_attn(place, pieces, width):
    shapes = [(width, 3 * width // SEQ), (width // SEQ, width), (width // 128, 128), (width // 128, 128)]
    return pl.pallas_call(
        assemble_attn_kernel,
        name="assemble_attn",
        grid=(1,),
        in_specs=[SMEM] + [fixed(x.shape) for x in pieces],
        out_specs=[fixed(x) for x in shapes],
        out_shape=[jax.ShapeDtypeStruct(x, t) for x, t in zip(shapes, (bf16, bf16, f32, f32))],
        compiler_params=params(12),
    )(place, *pieces)


def assemble_rows_kernel(place_ref, *refs):
    dp = len(refs) - 1
    pieces, out_ref = refs[:dp], refs[dp]
    count = out_ref.shape[0] // dp
    for slot, piece in enumerate(pieces):
        row = pl.multiple_of(source_of(place_ref, dp, slot) * count, 8)
        for t in range(out_ref.shape[1] // 128):
            out_ref[pl.ds(row, count), t * 128 : t * 128 + 128] = piece[t * count : (t + 1) * count, :]


def assemble_rows(place, pieces, width, inner):
    return pl.pallas_call(
        assemble_rows_kernel,
        name="assemble_rows",
        grid=(1,),
        in_specs=[SMEM] + [fixed(x.shape) for x in pieces],
        out_specs=fixed((inner, width)),
        out_shape=jax.ShapeDtypeStruct((inner, width), bf16),
        compiler_params=params(12),
    )(place, *pieces)


def ffn_kernel(me_ref, tok_ref, og_ref, a0, a1, a2, a3, wo0, wo1, wo2, wo3, gain_ref, w_ref, wd_ref, *outs):
    nm_ref, hid_ref, dgu_ref, mid_ref, *lists = outs
    step = pl.program_id(0)
    if len(w_ref.shape) == 3:
        pieces, w_ref = w_ref, lists.pop()
        dp = pieces.shape[0]
        width, lanes = w_ref.shape
        w_rows = width // (SEQ * dp)
        chunk = lanes // 128 * w_rows

        @pl.when(step == 0)
        def _():
            for k in range(SEQ):
                for src in range(dp):
                    row = pl.multiple_of((me_ref[0] ^ k) * (width // SEQ) + src * w_rows, w_rows)
                    for t in range(lanes // 128):
                        at = k * chunk + t * w_rows
                        w_ref[pl.ds(row, w_rows), t * 128 : t * 128 + 128] = pieces[src, at : at + w_rows, :]

    mid = tok_ref[...].astype(f32)
    inner = wd_ref.shape[0]
    main = main_lanes(inner)
    for a, wo in zip((a0, a1, a2, a3), (wo0, wo1, wo2, wo3)):
        mid = mid + mul(a[...], wo[...], 1, 0)
    scale = lax.rsqrt(jnp.mean(mid * mid, axis=-1, keepdims=True) + epsilon)
    nm = (mid * scale * gain_ref[...]).astype(bf16)
    nm_ref[...] = nm
    d_hidden = mul(og_ref[...], wd_ref[...], 1, 1)
    both = mul(nm, w_ref[...], 1, 0)

    def gated(gate, up, grad):
        sig = jax.nn.sigmoid(gate)
        silu = gate * sig
        return (
            (silu * up).astype(bf16),
            (grad * up * (sig * (1.0 + gate * (1.0 - sig)))).astype(bf16),
            (grad * silu).astype(bf16),
        )

    hid_main, dg_main, du_main = gated(both[:, :main], both[:, main : 2 * main], d_hidden[:, :main])
    last = both[:, 2 * main :]
    hid_last, dg_last, du_last = gated(last[:, : inner - main], last[:, inner - main :], d_hidden[:, main:])
    hid_ref[:, :main] = hid_main
    hid_ref[:, main:] = hid_last
    dgu_ref[:, :main] = dg_main
    dgu_ref[:, main : 2 * main] = du_main
    dgu_ref[:, 2 * main :] = jnp.concatenate([dg_last, du_last], axis=1)
    dnm = mul(dgu_ref[...], w_ref[...], 1, 1).astype(bf16)
    lo = mul(hid_ref[...], wd_ref[...], 1, 0).astype(bf16)
    dnm_kept, dnm_sent, lo_kept, lo_sent = lists
    rows = tok_ref.shape[0]
    for k in range(SEQ):

        @pl.when(step == SEQ - 1 - k)
        def _():
            here = slice(k // 2 * rows, (k // 2 + 1) * rows)
            (dnm_sent if k % 2 else dnm_kept)[here, :] = dnm
            (lo_sent if k % 2 else lo_kept)[here, :] = lo

    @pl.when(step == SEQ - 1)
    def _():
        mid_ref[...] = mid


def ffn_call(me, tok, og, att, wo, gain, w, wd):
    length, width = tok.shape
    rows = length // SEQ
    inner = wd.shape[0]
    part = att[0].shape[1]
    rel = lambda k, m: (SEQ - 1 - k, 0)
    here = lambda k, m: (m[0] ^ (SEQ - 1 - k), 0)
    return pl.pallas_call(
        ffn_kernel,
        name="ffn",
        grid_spec=pltpu.PrefetchScalarGridSpec(
            num_scalar_prefetch=1,
            grid=(SEQ,),
            in_specs=[pl.BlockSpec((rows, width), rel)] * 2
            + [pl.BlockSpec((rows, part), here)] * 4
            + [fixed(x.shape) for x in wo]
            + [fixed((1, width)), fixed(w.shape), fixed(wd.shape)],
            out_specs=[
                pl.BlockSpec((rows, width), rel),
                pl.BlockSpec((rows, inner), rel),
                pl.BlockSpec((rows, 2 * inner), rel),
                fixed((rows, width)),
            ]
            + [fixed((2 * rows, width))] * 4,
            scratch_shapes=[pltpu.VMEM((width, 2 * inner), bf16)] * (w.ndim - 2),
        ),
        out_shape=[
            jax.ShapeDtypeStruct((length, width), bf16),
            jax.ShapeDtypeStruct((length, inner), bf16),
            jax.ShapeDtypeStruct((length, 2 * inner), bf16),
            jax.ShapeDtypeStruct((rows, width), f32),
        ]
        + [jax.ShapeDtypeStruct((2 * rows, width), bf16)] * 4,
        compiler_params=params(60),
    )(me, tok, og, *att, *wo, gain, w, wd)


def owner_index(place_ref, dp, slot):
    groups = dp // 2
    b, j = slot // groups, slot % groups
    z, y = place_ref[2] // 2, place_ref[2] % 2
    return ((z + j) % groups) * 2 + (y ^ b)


def columns_grad_kernel(place_ref, act_ref, grad_ref, *refs):
    outs, work = refs[:-1], refs[-1]
    dp = len(outs)
    work[...] = mul(act_ref[...], grad_ref[...], 0, 0).astype(bf16)
    w_rows = work.shape[0] // dp
    for slot, ref in enumerate(outs):
        here = pl.ds(pl.multiple_of(owner_index(place_ref, dp, slot) * w_rows, w_rows), w_rows)
        for t in range(work.shape[1] // 128):
            ref[t * w_rows : (t + 1) * w_rows, :] = work[here, t * 128 : t * 128 + 128]


def columns_grad_plain(act, grad, dp):
    width, lanes = act.shape[1], grad.shape[1]
    w_rows = width // (SEQ * dp)
    grad = mul(act, grad, 0, 0).astype(bf16).reshape(SEQ, dp, w_rows, lanes // 128, 128)
    return grad.transpose(1, 0, 3, 2, 4).reshape(dp, -1, 128)


def columns_grad(place, act, grad, dp):
    length, width = act.shape
    lanes = grad.shape[1]
    part = width // SEQ
    chunk = lanes // 128 * (part // dp)
    return pl.pallas_call(
        columns_grad_kernel,
        name="columns_grad",
        grid_spec=pltpu.PrefetchScalarGridSpec(
            num_scalar_prefetch=1,
            grid=(SEQ,),
            in_specs=[pl.BlockSpec((length, part), lambda s, m: (0, s)), fixed(grad.shape)],
            out_specs=[pl.BlockSpec((chunk, 128), lambda s, m: (s, 0))] * dp,
            scratch_shapes=[pltpu.VMEM((part, lanes), bf16)],
        ),
        out_shape=[jax.ShapeDtypeStruct((SEQ * chunk, 128), bf16)] * dp,
        compiler_params=params(60),
    )(place, act, grad)


def out_grad_kernel(place_ref, act_ref, d0, d1, d2, d3, kept_ref, sent_ref, work):
    rows = d0.shape[0]
    total = 0.0
    for k, ref in enumerate((d0, d1, d2, d3)):
        act = act_ref[pl.ds(pl.multiple_of((place_ref[0] ^ k) * rows, rows), rows), :]
        total = total + mul(act, ref[...], 0, 0)
    work[...] = total.astype(bf16)
    dp = 2 * kept_ref.shape[0]
    count = work.shape[0] // dp
    at = 0
    for slot in range(dp):
        here = pl.ds(pl.multiple_of(owner_index(place_ref, dp, slot) * count, count), count)
        for t in range(work.shape[1] // 128):
            piece = work[here, t * 128 : t * 128 + 128]
            if slot < dp // 2:
                kept_ref[slot, t * count : (t + 1) * count, :] = piece
            else:
                sent_ref[at : at + count, :] = piece
                at += count


def out_projection_grad(place, act, d_branch, dp):
    width = d_branch[0].shape[1]
    part = act.shape[1]
    shape = (dp // 2, width // 128 * (part // dp), 128)
    sent = (shape[0] * shape[1], 128)
    return pl.pallas_call(
        out_grad_kernel,
        name="out_projection_grad",
        grid=(1,),
        in_specs=[SMEM, fixed(act.shape)] + [fixed(x.shape) for x in d_branch],
        out_specs=[fixed(shape), fixed(sent)],
        out_shape=[jax.ShapeDtypeStruct(shape, bf16), jax.ShapeDtypeStruct(sent, bf16)],
        scratch_shapes=[pltpu.VMEM((part, width), bf16)],
        compiler_params=params(24),
    )(place, act, *d_branch)


def down_grad_kernel(act_ref, grad_ref, out_ref):
    out_ref[...] = mul(act_ref[...], grad_ref[...], 0, 0).astype(bf16)


def down_grad(act, grad):
    length, width = grad.shape
    step = 256
    return pl.pallas_call(
        down_grad_kernel,
        name="down_grad",
        grid=(width // step,),
        in_specs=[fixed(act.shape), pl.BlockSpec((length, step), lambda c: (0, c))],
        out_specs=pl.BlockSpec((act.shape[1], step), lambda c: (0, c)),
        out_shape=jax.ShapeDtypeStruct((act.shape[1], width), bf16),
        compiler_params=params(60),
    )(act, grad)


def simple(kernel, name, args, outs, limit=24, half=()):
    half = dict(half)

    def spec(i, x):
        if i not in half:
            return SMEM if x.dtype == jnp.int32 else fixed(x.shape)
        shape = (x.shape[0] // 2, x.shape[1])
        return pl.BlockSpec(shape, lambda _: (half[i], 0), pipeline_mode=pl.Buffered(1))

    return pl.pallas_call(
        kernel,
        name=name,
        grid=(1,),
        in_specs=[spec(i, x) for i, x in enumerate(args)],
        out_specs=[fixed(x.shape) for x in outs],
        out_shape=outs,
        compiler_params=params(limit),
    )(*args)


def shaped(dtype, *shape):
    return jax.ShapeDtypeStruct(shape, dtype)


def sum_kernel(*refs):
    *ins, out = refs
    out[...] = sum(x[...].astype(f32) for x in ins).astype(out.dtype)


def total(*pieces):
    return simple(sum_kernel, "total", pieces, [shaped(bf16, *pieces[0].shape)])[0]


def lower(kept, got):
    rows, width = kept.shape[0] // 2, kept.shape[1]
    return simple(sum_kernel, "lower", (kept, got), [shaped(bf16, rows, width)], half=((0, 1), (1, 1)))[0]


def slots_kernel(kept_ref, got_ref, *outs):
    count = kept_ref.shape[1]
    at = got_ref.shape[0] - len(outs) * count
    for j, out in enumerate(outs):
        got = got_ref[at + j * count : at + (j + 1) * count, :]
        out[...] = (kept_ref[j].astype(f32) + got.astype(f32)).astype(out.dtype)


def slots(kept, got):
    shape = kept.shape[1:]
    outs = [shaped(f32, *shape)] + [shaped(bf16, *shape)] * (kept.shape[0] - 1)
    return simple(slots_kernel, "slots", (kept, got), outs)


def back_through_norm(grad, field, gain):
    scale = lax.rsqrt(jnp.mean(field * field, axis=-1, keepdims=True) + epsilon)
    unit = field * scale
    pressed = grad * gain
    return scale * (pressed - unit * jnp.mean(pressed * unit, axis=-1, keepdims=True))


def branch_kernel(kept_ref, got_ref, far_ref, mid_ref, og_ref, gain_ref, w0, w1, w2, w3, d_mid_ref, d_ref, a0, a1, a2, a3):
    grad = kept_ref[...].astype(f32) + got_ref[...].astype(f32) + far_ref[...].astype(f32)
    d_mid = og_ref[...].astype(f32) + back_through_norm(grad, mid_ref[...], gain_ref[...])
    d_mid_ref[...] = d_mid
    d_branch = d_mid.astype(bf16)
    d_ref[...] = d_branch
    for w, a in ((w0, a0), (w1, a1), (w2, a2), (w3, a3)):
        a[...] = mul(d_branch, w[...], 1, 1).astype(bf16)


def token_grad_kernel(kept_ref, got_ref, far_ref, tok_ref, gain_ref, d_mid_ref, out_ref):
    grad = kept_ref[...].astype(f32) + got_ref[...].astype(f32) + far_ref[...].astype(f32)
    out_ref[...] = (d_mid_ref[...] + back_through_norm(grad, tok_ref[...].astype(f32), gain_ref[...])).astype(bf16)


def cut_kernel(me_ref, *refs):
    ins, d_ref, (mine_ref, near_ref, far_ref) = refs[:-4], refs[-4], refs[-3:]
    groups = [ins[:4], ins[4:8], ins[8:]]
    count = far_ref.shape[0] - 2 * mine_ref.shape[0]
    far_ref[2 * mine_ref.shape[0] :, :] = d_ref[pl.ds(pl.multiple_of(((me_ref[0] >> 1) ^ 1) * count, count), count), 256:]
    me = me_ref[0]
    at = 0
    for pieces in groups:
        chunk = pieces[0].shape[0] // SEQ

        def chunk_of(s):
            here = pl.ds(pl.multiple_of(s * chunk, 8), chunk)
            return sum(x[here, :].astype(f32) for x in pieces).astype(bf16)

        mine_ref[at : at + chunk, :] = chunk_of(me)
        near_ref[at : at + chunk, :] = chunk_of(me ^ 1)
        for core in range(2):
            row = core * mine_ref.shape[0] + at
            far_ref[row : row + chunk, :] = chunk_of(((me >> 1) ^ 1) * 2 + core)
        at += chunk


def cut(me, attn, ffn, d_pair):
    rows = (attn[0][0].shape[0] * 2 + ffn[0].shape[0]) // SEQ
    outs = [shaped(bf16, n, 128) for n in (rows, rows, 2 * rows + d_pair.shape[0] // 2)]
    return simple(cut_kernel, "cut", (me, *attn[0], *attn[1], *ffn, d_pair), outs)


def relay_kernel(me_ref, near, far, d0_ref, d1_ref, far0_ref, out_ref):
    me = me_ref[0]
    core = (me & 1) ^ 1
    count = near.shape[0]
    out_ref[:count, :] = near[...]
    out_ref[count : 2 * count, :] = far[pl.ds(pl.multiple_of(core * count, 8), count), :]
    at = 2 * count
    rows = far0_ref.shape[0] // 2
    first = pl.multiple_of((me ^ 1) * rows, rows)
    for d_ref, far_ref, row in ((d0_ref, far0_ref, 0), (d1_ref, far, 2 * count)):
        out_ref[at : at + rows, :] = d_ref[pl.ds(first, rows), 256:]
        out_ref[at + rows : at + 2 * rows, :] = far_ref[pl.ds(pl.multiple_of(row + core * rows, 8), rows), :]
        at += 2 * rows


def value_grad_kernel(me_ref, acc_ref, d0_ref, d1_ref, far0_ref, far, got_ref, out_ref):
    me = me_ref[0]
    rows = acc_ref.shape[0]
    first = pl.multiple_of(me * rows, rows)
    at = far.shape[0] - 2 * rows

    for p, (d_ref, far_ref, row) in enumerate(((d0_ref, far0_ref, 0), (d1_ref, far, at))):
        pieces = (
            d_ref[pl.ds(first, rows), 256:],
            got_ref[at : at + rows, :],
            far_ref[pl.ds(pl.multiple_of(row + (me & 1) * rows, 8), rows), :],
            got_ref[at + rows : at + 2 * rows, :],
        )
        for k, piece in enumerate(pieces):
            lanes = pl.ds(pl.multiple_of((me ^ k) * 256 + p * 128, 128), 128)
            out_ref[:, lanes] = acc_ref[:, lanes] + piece.astype(f32)
        at += 2 * rows


def finish_kernel(
    me_ref, mine, far, got_ref, o0, o1, o2, o3, wq, wk, wv, wg, wu, ga_ref, gm_ref, down_ref,
    gq_ref, gk_ref, gv_ref, go_ref, gga_ref, gg_ref, gu_ref, ggm_ref, gd_ref, cols_a, cols_f,
):
    me = me_ref[0]
    gd_ref[...] = down_ref[...].astype(f32)
    count = mine.shape[0]
    at = 0
    for cols in (cols_a, cols_f):
        chunk = cols.shape[1]
        cols[0] = mine[at : at + chunk, :]
        cols[2] = far[pl.ds(pl.multiple_of((me & 1) * count + at, 8), chunk), :]
        cols[1] = got_ref[at : at + chunk, :]
        cols[3] = got_ref[count + at : count + at + chunk, :]
        at += chunk
    out = sum(x[...].astype(f32) for x in (o0, o1, o2, o3))
    w_rows, width = gq_ref.shape
    for t in range(width // 128):
        go_ref[:, t * 128 : t * 128 + 128] = out[t * w_rows : (t + 1) * w_rows, :]
    unpack_attn(me, cols_a, gq_ref, gk_ref, gv_ref)
    gga_ref[...] = gain_grad(((wq, gq_ref), (wk, gk_ref), (wv, gv_ref)), ga_ref)
    unpack_ffn(me, cols_f, gg_ref, gu_ref)
    ggm_ref[...] = gain_grad(((wg, gg_ref), (wu, gu_ref)), gm_ref)


def gain_grad(pairs, gain_ref):
    column = sum(jnp.sum(w[...].astype(f32) * g[...], axis=1, keepdims=True) for w, g in pairs)
    rows = column.shape[0]
    same = lax.broadcasted_iota(jnp.int32, (rows, rows), 0) == lax.broadcasted_iota(jnp.int32, (rows, rows), 1)
    return jnp.sum(jnp.where(same, column, 0.0), axis=0, keepdims=True) / gain_ref[...].astype(f32)


def unpack_attn(me, cols_ref, *outs):
    w_rows, width = outs[0].shape
    part = width // SEQ
    for s in range(SEQ):
        at = 0
        for t in range(part // 128):
            for ref in outs:
                lanes = slice(s * part + t * 128, s * part + t * 128 + 128)
                ref[:, lanes] = cols_ref[me ^ s, at : at + w_rows, :].astype(f32)
                at += w_rows


def unpack_ffn(me, cols_ref, gg_ref, gu_ref):
    w_rows = gg_ref.shape[0]
    inner = gg_ref.shape[1] // SEQ
    main = main_lanes(inner)
    rest = inner - main
    half = main // 128
    for s in range(SEQ):
        slot = me ^ s
        tiles = [cols_ref[slot, t * w_rows : (t + 1) * w_rows, :].astype(f32) for t in range(2 * inner // 128)]
        gg_ref[:, s * inner : (s + 1) * inner] = jnp.concatenate(tiles[:half] + [tiles[-1][:, :rest]], axis=1)
        gu_ref[:, s * inner : (s + 1) * inner] = jnp.concatenate(tiles[half : 2 * half] + [tiles[-1][:, rest:]], axis=1)


def unpack_kernel(me_ref, cols_a, cols_f, wq, wk, wv, wg, wu, ga_ref, gm_ref, gq_ref, gk_ref, gv_ref, gga_ref, gg_ref, gu_ref, ggm_ref):
    unpack_attn(me_ref[0], cols_a, gq_ref, gk_ref, gv_ref)
    gga_ref[...] = gain_grad(((wq, gq_ref), (wk, gk_ref), (wv, gv_ref)), ga_ref)
    unpack_ffn(me_ref[0], cols_f, gg_ref, gu_ref)
    ggm_ref[...] = gain_grad(((wg, gg_ref), (wu, gu_ref)), gm_ref)


def input_grad_kernel(me_ref, *refs):
    *d_refs, w_ref, kept_ref, sent_ref = refs
    step = pl.program_id(0)
    d_qkv = [d[:, i * 128 : i * 128 + 128] for i in range(3) for d in d_refs]
    grad = mul(jnp.concatenate(d_qkv, axis=1), w_ref[...], 1, 1).astype(bf16)
    rows = grad.shape[0]
    for k in range(SEQ):

        @pl.when(step == SEQ - 1 - k)
        def _():
            (sent_ref if k % 2 else kept_ref)[k // 2 * rows : (k // 2 + 1) * rows, :] = grad


def input_grad(me, d_qkv, w):
    length, part = d_qkv[0].shape
    width = w.shape[0]
    rows = length // SEQ
    here = lambda k, m: (m[0] ^ (SEQ - 1 - k), 0)
    return pl.pallas_call(
        input_grad_kernel,
        name="input_grad",
        grid_spec=pltpu.PrefetchScalarGridSpec(
            num_scalar_prefetch=1,
            grid=(SEQ,),
            in_specs=[pl.BlockSpec((rows, part), here)] * len(d_qkv) + [fixed(w.shape)],
            out_specs=[fixed((2 * rows, width))] * 2,
        ),
        out_shape=[jax.ShapeDtypeStruct((2 * rows, width), bf16)] * 2,
        compiler_params=params(16),
    )(me, *d_qkv, w)


def to_core(value):
    return lax.ppermute(value, "seq", [(i, i ^ 1) for i in range(SEQ)])


def to_chip(value):
    return lax.ppermute(value, "seq", [(i, i ^ 2) for i in range(SEQ)])


def to_both(value):
    return lax.ppermute(value, "seq", [(i, i ^ 3) for i in range(SEQ)])


def gather_rel(value):
    far = to_chip(value)
    return value, to_core(value), far, to_core(far)


def exchange_rel(pieces):
    return [pieces[0], to_core(pieces[1]), to_chip(pieces[2]), to_both(pieces[3])]


def scatter_sum(kept, sent):
    sums = add(kept, to_core(sent))
    rows = kept.shape[0] // 2
    return sums[:rows] + to_chip(sums[rows:].astype(bf16)).astype(f32)


def add(a, b):
    return a.astype(f32) + b.astype(f32)


def to_y(value):
    dp = lax.axis_size("dp")
    return lax.ppermute(value, "dp", [(i, i ^ 1) for i in range(dp)])


def to_z(value, hops=1):
    dp = lax.axis_size("dp")
    return lax.ppermute(value, "dp", [(i, (i + 2 * hops) % dp) for i in range(dp)])


def rotary(length, head_width):
    pairs = jnp.arange(head_width // 2, dtype=f32)
    freq = jnp.exp(pairs * (-2.0 * math.log(10000.0) / head_width))
    theta = jnp.arange(length, dtype=jnp.int32).astype(f32)[:, None] * freq[None, :]
    cos, sin = jnp.cos(theta), jnp.sin(theta)
    return jnp.concatenate([cos] * 4, axis=1), jnp.concatenate([-sin, sin] * 2, axis=1)


class Stage:
    def fence(self):
        names = list(vars(self))
        for name, value in zip(names, sync(*[getattr(self, name) for name in names])):
            setattr(self, name, value)


def body_direct(
    tokens, first_values, value_grad_acc, segment_ids, query_weight, key_weight, value_weight, out_weight,
    attn_gain, gate_weight, up_weight, down_weight, mlp_gain, out_grad,
):
    dp = lax.axis_size("dp")
    zs = dp // 2
    rows, width = tokens.shape[1:]
    length = segment_ids.shape[1]
    w_rows = query_weight.shape[0]
    part = width // SEQ
    inner = gate_weight.shape[1] // SEQ
    me = lax.axis_index("seq").astype(jnp.int32)
    mine = lax.axis_index("dp").astype(jnp.int32)
    me_arg = me[None]
    place = jnp.stack([me, me * dp + mine, mine])
    s = Stage()

    half = rows // 2
    *s.cols, s.orows, drows, tok_a, tok_b = pack_attn(
        query_weight, key_weight, value_weight, out_weight, down_weight, attn_gain, mlp_gain, tokens[0]
    )
    s.r, s.tok_far = [drows], [tok_a, tok_b]
    s.tokens, s.first, s.out_grad, s.segments = tokens[0], first_values[0], out_grad[0], segment_ids
    s.gate, s.up = gate_weight, up_weight
    s.fence()
    s.cols = exchange_rel(s.cols)
    s.ry = [to_y(s.r[0])]
    s.r.append(to_z(s.r[0]))
    s.fence()
    s.a = [jnp.concatenate([*s.cols, s.orows])]
    del s.cols, s.orows
    s.tok_far[0] = to_chip(s.tok_far[0])
    s.ay = [to_y(s.a[0])]
    s.a.append(to_z(s.a[0]))
    s.fcols = pack_ffn(place, s.gate, s.up)
    del s.gate, s.up
    s.fence()
    s.ay.append(to_y(s.a[1]))
    s.a.append(to_z(s.a[1]))
    s.f_piece = jnp.concatenate(exchange_rel(s.fcols))
    s.cos, s.sin = rotary(length, width // HEADS)
    del s.fcols
    s.fence()
    ffn_all = lax.all_gather(s.f_piece, "dp", axis=0, tiled=False)
    del s.f_piece
    s.tok_far[1] = to_chip(s.tok_far[1])
    s.ay.append(to_y(s.a[2]))
    s.a.append(to_z(s.a[2]))
    s.tok_near = to_core(s.tokens)
    s.first = [lax.dynamic_slice_in_dim(s.first, (me ^ k) * part, part, 1) for k in range(SEQ)]
    s.og_far = [s.out_grad[:half], s.out_grad[half:]]
    s.fence()
    s.ay.append(to_y(s.a[3]))
    s.first = jnp.concatenate(exchange_rel(s.first))
    tok_far = jnp.concatenate(s.tok_far)
    s.tok = jnp.concatenate([s.tokens, s.tok_near, tok_far, to_core(tok_far)])
    del s.tok_far, s.tok_near
    s.fence()
    s.ry.append(to_y(s.r[1]))
    s.r.append(to_z(s.r[1]))
    s.og_far[0] = to_chip(s.og_far[0])
    s.og = [s.out_grad, to_core(s.out_grad)]
    s.w_qkv, s.w_out, attn_gain_all, mlp_gain_all = assemble_attn(place, s.a + s.ay, width)
    s.attn_gain, s.mlp_gain = attn_gain_all.reshape(1, width), mlp_gain_all.reshape(1, width)
    s.nin, s.q, s.k, s.v = qkv_call(me_arg, s.tok, s.first, s.w_qkv, s.attn_gain, s.cos, s.sin)
    del s.a, s.ay, s.first
    s.fence()
    s.og_far[1] = to_chip(s.og_far[1])
    s.wo = [s.w_out, to_core(s.w_out), to_chip(s.w_out)]
    s.ry.append(to_y(s.r[2]))
    s.r.append(to_z(s.r[2]))
    s.attended, s.lse = attend_call(s.q, s.k, s.v, s.segments)
    del s.w_out
    s.fence()
    att_far = to_chip(s.attended)
    s.w_down = assemble_rows(place, s.r + s.ry + [to_y(s.r[3])], width, inner)
    s.att = [s.attended, to_core(s.attended), att_far]
    s.wo.append(to_core(s.wo[2]))
    og_far = jnp.concatenate(s.og_far)
    s.og = jnp.concatenate([*s.og, og_far, to_core(og_far)])
    del s.r, s.ry, s.og_far
    s.fence()
    s.att.append(to_core(s.att[2]))
    s.fence()
    s.nm, s.hidden, s.d_gu, s.mid, s.dnm, dnm_sent, s.lo, s.lo_sent = ffn_call(
        me_arg, s.tok, s.og, s.att, s.wo, s.mlp_gain, ffn_all, s.w_down
    )
    s.dnm_got = to_core(dnm_sent)
    s.dnm_far = lower(s.dnm, s.dnm_got)
    del s.tok, s.att, s.w_down
    s.fence()
    s.dnm_far = to_chip(s.dnm_far)
    pieces = list(columns_grad(place, s.nm, s.d_gu, dp))
    s.f_kept, s.f_sent = pieces[:zs], pieces[zs:]
    s.g_down = down_grad(after(s.hidden, pieces[0]), s.og)
    g_down = lax.psum_scatter(s.g_down, "dp", scatter_dimension=0, tiled=True)
    del s.nm, s.d_gu, s.hidden, s.og
    s.fence()
    s.f_sent[3] = to_y(s.f_sent[3])
    s.lo_got = to_core(s.lo_sent)
    s.d_middle, s.d_branch, *s.d_att = simple(
        branch_kernel,
        "branch",
        (s.dnm, s.dnm_got, s.dnm_far, s.mid, s.out_grad, s.mlp_gain, *s.wo),
        [shaped(f32, rows, width), shaped(bf16, rows, width)] + [shaped(bf16, rows, part)] * SEQ,
        half=((0, 0), (1, 0)),
    )
    s.lo_far = lower(s.lo, s.lo_got)
    del s.dnm, s.dnm_got, s.dnm_far, s.wo, s.lo_sent, s.g_down
    s.fence()
    s.d_att = exchange_rel(s.d_att)
    s.f_sent[2] = to_y(s.f_sent[2])
    s.f = to_z(total(s.f_kept[3], s.f_sent[3]))
    s.fence()

    def back(pair, *along):
        return attend_back_call(
            pair, place, s.q, s.k, s.v, s.d_att, s.lse, s.segments, s.cos, s.sin, s.nin, dp, True, along
        )

    def other_chip_values(d_pair):
        return lax.dynamic_slice(d_pair, (((me >> 1) ^ 1) * 2 * rows, 256), (2 * rows, 128))

    s.f_sent[1] = to_y(s.f_sent[1])
    s.f = to_z(total(s.f_kept[2], s.f_sent[2], s.f))
    s.d_branch = [s.d_branch, to_core(s.d_branch), to_chip(s.d_branch)]
    d_pair, kept, sent = back(0, s.f_sent[0])
    s.d_qkv, s.kept, s.sent = [d_pair], [kept], [sent]
    s.fence()
    s.sent[0] = to_y(s.sent[0])
    s.f = to_z(total(s.f_kept[1], s.f_sent[1], s.f))
    s.lo_far = to_chip(s.lo_far)
    s.d_branch.append(to_core(s.d_branch[2]))
    s.values_far = to_chip(other_chip_values(s.d_qkv[0]))
    d_pair, kept, sent = back(1)
    s.d_qkv.append(d_pair)
    s.dnin, s.dnin_sent = input_grad(me_arg, s.d_qkv, s.w_qkv)
    s.kept.append(kept)
    s.sent.append(sent)
    del s.nin, s.d_att, s.w_qkv
    s.fence()

    def over_z(first, *others):
        return [first] + [to_z(piece, j + 1) for j, piece in enumerate(others)]

    s.sent[1] = to_y(s.sent[1])
    s.kept[0] = over_z(*slots(s.kept[0], s.sent[0]))
    s.dnin_got = to_core(s.dnin_sent)
    s.dnin_far = lower(s.dnin, s.dnin_got)
    s.out_kept, s.out_sent = out_projection_grad(place, s.attended, s.d_branch, dp)
    del s.d_branch, s.attended, s.dnin_sent
    s.fence()
    s.kept[1] = over_z(*slots(s.kept[1], s.sent[1]))
    s.out_kept = slots(s.out_kept, to_y(s.out_sent))
    s.dnin_far = to_chip(s.dnin_far)
    s.layer_out = simple(
        sum_kernel,
        "layer_out",
        (s.mid, s.lo, s.lo_got, s.lo_far),
        [shaped(bf16, rows, width)],
        half=((1, 0), (2, 0)),
    )[0]
    del s.lo, s.lo_got, s.lo_far, s.mid
    s.fence()
    s.mine, s.near, far = cut(me_arg, s.kept, (s.f_kept[0], s.sent[0], s.f), s.d_qkv[1])
    s.far = to_chip(far)
    s.out_kept = over_z(*s.out_kept)
    s.token_grad = simple(
        token_grad_kernel,
        "token_grad",
        (s.dnin, s.dnin_got, s.dnin_far, s.tokens, s.attn_gain, s.d_middle),
        [shaped(bf16, rows, width)],
        60,
        ((0, 0), (1, 0)),
    )[0]
    s.g_down = g_down
    del s.kept, s.sent, s.out_sent, s.dnin, s.dnin_got, s.d_middle, s.f, s.f_kept, s.f_sent
    s.fence()
    count = s.mine.shape[0]
    args = (me_arg, s.near, s.far, *s.d_qkv, s.values_far)
    got = to_core(simple(relay_kernel, "relay", args, [shaped(bf16, 2 * count + SEQ * rows, 128)])[0])
    weights = (query_weight, key_weight, value_weight, gate_weight, up_weight)
    shapes = [(w_rows, width)] * 4 + [(1, w_rows)] + [(w_rows, SEQ * inner)] * 2 + [(1, w_rows), g_down.shape]
    args = (s.mine, s.far, got, *s.out_kept, *weights, attn_gain[None], mlp_gain[None], s.g_down)
    a_rows = 3 * part // 128 * w_rows
    g_q, g_k, g_v, g_out, attn_gain_grad, g_gate, g_up, mlp_gain_grad, g_down = pl.pallas_call(
        finish_kernel,
        name="finish",
        grid=(1,),
        in_specs=[SMEM] + [fixed(x.shape) for x in args],
        out_specs=[fixed(x) for x in shapes],
        out_shape=[shaped(f32, *x) for x in shapes],
        scratch_shapes=[pltpu.VMEM((SEQ, a_rows, 128), bf16), pltpu.VMEM((SEQ, count - a_rows, 128), bf16)],
        compiler_params=params(24),
    )(me_arg, *args)
    value_grad_out = simple(
        value_grad_kernel,
        "value_grad",
        (me_arg, value_grad_acc[0], *s.d_qkv, s.values_far, s.far, got),
        [shaped(f32, rows, width)],
    )[0]
    return (
        s.layer_out[None],
        s.token_grad[None],
        value_grad_out[None],
        g_q,
        g_k,
        g_v,
        g_out,
        attn_gain_grad[0],
        g_gate,
        g_up,
        g_down,
        mlp_gain_grad[0],
    )


def body_plain(
    tokens, first_values, value_grad_acc, segment_ids, query_weight, key_weight, value_weight, out_weight,
    attn_gain, gate_weight, up_weight, down_weight, mlp_gain, out_grad,
):
    dp = lax.axis_size("dp")
    rows, width = tokens.shape[1:]
    length = segment_ids.shape[1]
    w_rows, d_rows = query_weight.shape[0], down_weight.shape[0]
    part = width // SEQ
    inner = gate_weight.shape[1] // SEQ
    main = main_lanes(inner)
    me = lax.axis_index("seq").astype(jnp.int32)
    mine = lax.axis_index("dp").astype(jnp.int32)
    me_arg = me[None]
    place = jnp.stack([me, me * dp + mine, mine])

    def columns(weight, count):
        return weight.reshape(w_rows, SEQ, count).transpose(1, 0, 2)

    owner = jnp.arange(width) // w_rows == me * dp + mine

    def spread(gain):
        full = jnp.where(owner, jnp.tile(gain, width // w_rows), jnp.zeros((), bf16))
        cut = 3 * part
        return jnp.stack([full[:cut], jnp.pad(full[cut:], (0, 2 * cut - width))])

    gains = jnp.concatenate([spread(attn_gain), spread(mlp_gain), jnp.zeros((4, 3 * part), bf16)])
    attn_cols = jnp.concatenate([columns(w, part) for w in (query_weight, key_weight, value_weight)], axis=2)
    attn_cols = jnp.concatenate([attn_cols, jnp.broadcast_to(gains[None], (SEQ,) + gains.shape)], axis=1)
    gate_cols, up_cols = columns(gate_weight, inner), columns(up_weight, inner)
    ffn_cols = jnp.concatenate(
        [gate_cols[:, :, :main], up_cols[:, :, :main], gate_cols[:, :, main:], up_cols[:, :, main:]], axis=2
    )
    attn_cols = lax.all_to_all(attn_cols, "seq", split_axis=0, concat_axis=0, tiled=True)
    ffn_cols = lax.all_to_all(ffn_cols, "seq", split_axis=0, concat_axis=0, tiled=True)
    attn_all = lax.all_gather(attn_cols.reshape(-1, 3 * part), "dp", axis=0, tiled=True)
    attn_all = attn_all.reshape(dp, SEQ, w_rows + 8, 3 * part)
    w_qkv = attn_all[:, :, :w_rows].transpose(1, 0, 2, 3).reshape(width, 3 * part)
    gain_all = jnp.sum(attn_all[:, :, w_rows : w_rows + 4].astype(f32), axis=(0, 1))
    attn_gain_all = jnp.concatenate([gain_all[0], gain_all[1]])[None, :width]
    mlp_gain_all = jnp.concatenate([gain_all[2], gain_all[3]])[None, :width]
    w_out = lax.all_gather(out_weight, "dp", axis=0, tiled=True)
    w_down = lax.all_gather(down_weight, "dp", axis=0, tiled=True)
    ffn_all = lax.all_gather(ffn_cols.reshape(-1, 2 * inner), "dp", axis=0, tiled=True)
    w_ffn = ffn_all.reshape(dp, SEQ, w_rows, 2 * inner).transpose(1, 0, 2, 3).reshape(width, 2 * inner)

    cos, sin = rotary(length, width // HEADS)
    tok = jnp.concatenate(gather_rel(tokens[0]))
    og = jnp.concatenate(gather_rel(out_grad[0]))
    first_cols = first_values[0].reshape(rows, SEQ, part)
    first = exchange_rel([lax.dynamic_index_in_dim(first_cols, me ^ k, 1, keepdims=False) for k in range(SEQ)])
    nin, q, k, v = qkv_call(me_arg, tok, jnp.concatenate(first), w_qkv, attn_gain_all, cos, sin)
    attended, lse = attend_call(q, k, v, segment_ids)
    wo = gather_rel(w_out)
    nm, hidden, d_gu, mid, *sums = ffn_call(me_arg, tok, og, gather_rel(attended), wo, mlp_gain_all, w_ffn, w_down)
    layer_out = (mid + scatter_sum(*sums[2:])).astype(bf16)
    d_middle = out_grad[0].astype(f32) + back_through_norm(scatter_sum(*sums[:2]), mid, mlp_gain_all)
    d_branch = d_middle.astype(bf16)
    d_att = exchange_rel([mul(d_branch, w, 1, 1).astype(bf16) for w in wo])
    d_branch_all = jnp.stack(gather_rel(d_branch))[me ^ jnp.arange(SEQ)].reshape(length, width)
    d_qkv = [
        attend_back_call(pair, place, q, k, v, d_att, lse, segment_ids, cos, sin, nin, dp, False)[0] for pair in range(2)
    ]
    dnin = scatter_sum(*input_grad(me_arg, d_qkv, w_qkv))
    token_grad = d_middle + back_through_norm(dnin, tokens[0].astype(f32), attn_gain_all)
    dv = jnp.concatenate([d[:, 256:] for d in d_qkv], axis=1)
    dv = exchange_rel([lax.dynamic_slice_in_dim(dv, (me ^ i) * rows, rows, 0) for i in range(SEQ)])
    dv = jnp.stack(dv)[me ^ jnp.arange(SEQ)].transpose(1, 0, 2).reshape(rows, width)
    value_grad_out = value_grad_acc[0] + dv.astype(f32)

    def over_dp(grads):
        return lax.psum_scatter(grads.reshape(-1, 128), "dp", scatter_dimension=0, tiled=True)

    def to_rows(sums):
        sums = sums.reshape(SEQ, -1, 128)
        return jnp.stack(exchange_rel([lax.dynamic_index_in_dim(sums, me ^ i, 0, keepdims=False) for i in range(SEQ)]))

    attn_sums = over_dp(columns_grad_plain(nin, jnp.concatenate(d_qkv, axis=1), dp))
    ffn_sums = over_dp(columns_grad_plain(nm, d_gu, dp))
    g_out = lax.psum_scatter(mul(attended, d_branch_all, 0, 0).astype(bf16), "dp", scatter_dimension=0, tiled=True)
    g_down = lax.psum_scatter(mul(hidden, og, 0, 0).astype(bf16), "dp", scatter_dimension=0, tiled=True)
    weights = (query_weight, key_weight, value_weight, gate_weight, up_weight)
    shapes = [(w_rows, width)] * 3 + [(1, w_rows)] + [(w_rows, SEQ * inner)] * 2 + [(1, w_rows)]
    args = (me_arg, to_rows(attn_sums), to_rows(ffn_sums), *weights, attn_gain[None], mlp_gain[None])
    g_q, g_k, g_v, attn_gain_grad, g_gate, g_up, mlp_gain_grad = simple(
        unpack_kernel, "unpack", args, [shaped(f32, *x) for x in shapes]
    )
    return (
        layer_out[None],
        token_grad.astype(bf16)[None],
        value_grad_out[None],
        g_q,
        g_k,
        g_v,
        g_out.astype(f32),
        attn_gain_grad[0],
        g_gate,
        g_up,
        g_down.astype(f32),
        mlp_gain_grad[0],
    )


def solution(mesh):
    token = P("dp", "seq", None)
    weight = P(("seq", "dp"), None)
    gain = P(("seq", "dp"))
    return jax.shard_map(
        body_direct if mesh.shape["dp"] == 8 else body_plain,
        mesh=mesh,
        in_specs=(token, token, token, P("dp", None), weight, weight, weight, weight, gain, weight, weight, weight, gain, token),
        out_specs=(token, token, token, weight, weight, weight, weight, gain, weight, weight, weight, gain),
        check_vma=False,
    )
```

```python
import functools
import math

import jax
import jax.numpy as jnp
from jax import lax
from jax.experimental import pallas as pl
from jax.experimental.pallas import tpu as pltpu
from jax.sharding import PartitionSpec as P

HEADS = 16
DOC_MOST = 512
SEQ = 4
BLOCK = 256

epsilon = 1e-06
masked_value = -1e30
bf16 = jnp.bfloat16
f32 = jnp.float32


def mul(a, b, ca, cb):
    return lax.dot_general(a, b, (((ca,), (cb,)), ((), ())), preferred_element_type=f32)


def params(mib):
    return pltpu.CompilerParams(vmem_limit_bytes=mib << 20)


VMEM = pl.BlockSpec(memory_space=pltpu.VMEM)
SMEM = pl.BlockSpec(memory_space=pltpu.SMEM)


def fixed(shape):
    return pl.BlockSpec(shape, lambda *_: (0,) * len(shape), pipeline_mode=pl.Buffered(1))


def sync(*values):
    return lax.optimization_barrier(values)


def after(value, *earlier):
    return lax.optimization_barrier((value, *earlier))[0]


def half_swap(field):
    lanes = field.shape[-1]
    lane = lax.broadcasted_iota(jnp.int32, field.shape, 1)
    up = pltpu.roll(field, lanes - 32, 1)
    down = pltpu.roll(field, 32, 1)
    return jnp.where(lane % 64 < 32, up, down)


def qkv_kernel(me_ref, tok_ref, first_ref, w_ref, gain_ref, cos_ref, sin_ref, nin_ref, q_ref, k_ref, v_ref):
    x = tok_ref[...].astype(f32)
    scale = lax.rsqrt(jnp.mean(x * x, axis=-1, keepdims=True) + epsilon)
    nin = (x * scale * gain_ref[...]).astype(bf16)
    nin_ref[...] = nin
    lin = mul(nin, w_ref[...], 1, 0)
    cos = jnp.concatenate([cos_ref[...]] * 2, axis=1)
    sin = jnp.concatenate([sin_ref[...]] * 2, axis=1)
    part = lin.shape[1] // 3
    q = lin[:, :part]
    q_ref[...] = ((q * cos + half_swap(q) * sin).astype(bf16).astype(f32) * 0.125).astype(bf16)
    k = lin[:, part : 2 * part]
    k_ref[...] = (k * cos + half_swap(k) * sin).astype(bf16)
    v_ref[...] = (0.5 * lin[:, 2 * part :] + 0.5 * first_ref[...].astype(f32)).astype(bf16)


def qkv_call(me, tok, first, w, gain, cos, sin):
    length, width = tok.shape
    rows = length // SEQ
    part = w.shape[1] // 3
    here = lambda k, m: (m[0] ^ k, 0)
    rel = lambda k, m: (k, 0)
    return pl.pallas_call(
        qkv_kernel,
        name="qkv",
        grid_spec=pltpu.PrefetchScalarGridSpec(
            num_scalar_prefetch=1,
            grid=(SEQ,),
            in_specs=[
                pl.BlockSpec((rows, width), rel),
                pl.BlockSpec((rows, part), rel),
                fixed(w.shape),
                fixed((1, width)),
                pl.BlockSpec((rows, 128), here),
                pl.BlockSpec((rows, 128), here),
            ],
            out_specs=[pl.BlockSpec((rows, width), here)] + [pl.BlockSpec((rows, part), here)] * 3,
        ),
        out_shape=[jax.ShapeDtypeStruct((length, width), bf16)]
        + [jax.ShapeDtypeStruct((length, part), bf16)] * 3,
        compiler_params=params(16),
    )(me, tok, first, w, gain, cos, sin)


def key_range(block):
    return max(0, block * BLOCK - (DOC_MOST // BLOCK) * BLOCK), (block + 1) * BLOCK


def column_of(row_ref):
    return jnp.broadcast_to(row_ref[...].astype(f32), (8, row_ref.shape[1])).T[:, :1]


def allowed_pairs(seg_col, seg_row, block, low, high):
    keys = lax.broadcasted_iota(jnp.int32, (high - low, BLOCK), 0) + low
    rows = lax.broadcasted_iota(jnp.int32, (high - low, BLOCK), 1) + block * BLOCK
    row = seg_row[:, block * BLOCK : (block + 1) * BLOCK].astype(f32)
    return (seg_col[low:high, :] == row) & (keys <= rows)


def head_lanes(field, head):
    lane = lax.broadcasted_iota(jnp.int32, field.shape, 1)
    return jnp.where(lane // 64 == head, field, jnp.zeros_like(field))


def half_rows(head):
    return pl.ds(pl.multiple_of(head * 64, 64), 64)


def attend_kernel(q_ref, k_ref, v_ref, seg_row, o_ref, lse_ref, turned, turned_out):
    length = q_ref.shape[0]
    seg_col = column_of(seg_row)
    turned[...] = v_ref[...].astype(f32).T.astype(bf16)

    def one_head(head, carry):
        for block in range(length // BLOCK):
            low, high = key_range(block)
            allowed = allowed_pairs(seg_col, seg_row, block, low, high)
            here = slice(block * BLOCK, (block + 1) * BLOCK)
            scores = mul(k_ref[low:high, :], head_lanes(q_ref[here, :], head), 1, 1)
            scores = jnp.where(allowed, scores, masked_value)
            top = jnp.max(scores, axis=0, keepdims=True)
            expo = jnp.exp(scores - top)
            total = jnp.sum(expo, axis=0, keepdims=True)
            probs = (expo * (1.0 / total)).astype(bf16)
            turned_out[half_rows(head), here] = mul(turned[half_rows(head), low:high], probs, 1, 0)
            lse_ref[0, pl.ds(head, 1), here] = top + jnp.log(total)
        return carry

    lax.fori_loop(0, 2, one_head, 0)
    for block in range(length // BLOCK):
        here = slice(block * BLOCK, (block + 1) * BLOCK)
        o_ref[here, :] = turned_out[:, here].T.astype(bf16)


def attend_call(q, k, v, seg_row):
    length, part = q.shape
    pairs = part // 128
    lanes = pl.BlockSpec((length, 128), lambda p: (0, p))
    return pl.pallas_call(
        attend_kernel,
        name="attend",
        grid=(pairs,),
        in_specs=[lanes] * 3 + [fixed((1, length))],
        out_specs=[lanes, pl.BlockSpec((1, 2, length), lambda p: (p, 0, 0))],
        out_shape=[jax.ShapeDtypeStruct((length, part), bf16), jax.ShapeDtypeStruct((pairs, 2, length), f32)],
        scratch_shapes=[pltpu.VMEM((128, length), bf16), pltpu.VMEM((128, length), f32)],
        compiler_params=params(24),
    )(q, k, v, seg_row)


def attend_back_kernel(
    dp, pieces, place_ref, q_ref, k_ref, v_ref, d0, d1, d2, d3, lse_ref, seg_row, cos_ref, sin_ref, nin_ref,
    *refs,
):
    outs, (da_ref, dk_sum, dv_sum, work, turned, turned_dq) = refs[:-6], refs[-6:]
    *along, d_ref = outs[: len(outs) - 2 * pieces]
    outs = outs[len(outs) - 2 * pieces :]
    length = q_ref.shape[0]
    rows = d0.shape[0]
    for k, ref in enumerate((d0, d1, d2, d3)):
        da_ref[pl.ds(pl.multiple_of((place_ref[0] ^ k) * rows, rows), rows), :] = ref[...]
    seg_col = column_of(seg_row)
    dk_sum[...] = jnp.zeros_like(dk_sum)
    dv_sum[...] = jnp.zeros_like(dv_sum)
    turned[...] = k_ref[...].astype(f32).T.astype(bf16)

    def one_head(head, carry):
        for block in range(length // BLOCK):
            low, high = key_range(block)
            allowed = allowed_pairs(seg_col, seg_row, block, low, high)
            here = slice(block * BLOCK, (block + 1) * BLOCK)
            q_head = head_lanes(q_ref[here, :], head)
            da_head = head_lanes(da_ref[here, :], head)
            scores = mul(k_ref[low:high, :], q_head, 1, 1)
            probs = jnp.where(allowed, jnp.exp(scores - lse_ref[0, pl.ds(head, 1), here]), 0.0)
            d_probs = mul(v_ref[low:high, :], da_head, 1, 1)
            delta = jnp.sum(probs * d_probs, axis=0, keepdims=True)
            d_scores = (probs * (d_probs - delta)).astype(bf16)
            turned_dq[half_rows(head), here] = mul(turned[half_rows(head), low:high], d_scores, 1, 0)
            dk_sum[low:high, :] += mul(d_scores, q_head, 1, 0)
            dv_sum[low:high, :] += mul(probs.astype(bf16), da_head, 1, 0)
        return carry

    lax.fori_loop(0, 2, one_head, 0)
    for block in range(length // BLOCK):
        here = slice(block * BLOCK, (block + 1) * BLOCK)
        dq = turned_dq[:, here].T * 0.125
        d_ref[here, :128] = (dq * cos_ref[here, :] - half_swap(dq) * sin_ref[here, :]).astype(bf16)
    dk = dk_sum[...]
    d_ref[:, 128:256] = (dk * cos_ref[...] - half_swap(dk) * sin_ref[...]).astype(bf16)
    d_ref[:, 256:] = (0.5 * dv_sum[...]).astype(bf16)
    if not outs:
        return
    kept_ref, sent_ref = outs
    part = work.shape[0]
    w_rows = part // dp
    first = 0
    if along:
        first = along[0].shape[0]
        sent_ref[:first, :] = along[0][...]
    for s in range(SEQ):
        work[...] = mul(nin_ref[:, s * part : (s + 1) * part], d_ref[...], 0, 0).astype(bf16)
        for slot in range(dp):
            here = pl.ds(pl.multiple_of(owner_index(place_ref, dp, slot) * w_rows, w_rows), w_rows)
            for t in range(3):
                at = (s * 3 + t) * w_rows
                piece = work[here, t * 128 : t * 128 + 128]
                if slot < dp // 2:
                    kept_ref[slot, at : at + w_rows, :] = piece
                else:
                    at += first + (slot - dp // 2) * kept_ref.shape[1]
                    sent_ref[at : at + w_rows, :] = piece


def attend_back_call(pair, place, q, k, v, da, lse, seg_row, cos, sin, nin, dp, pieces, along=()):
    length, width = nin.shape
    part = width // SEQ
    lanes = pl.BlockSpec((length, 128), lambda _: (0, pair), pipeline_mode=pl.Buffered(1))
    outs = [(length, 384)]
    if pieces:
        rows = 3 * width // dp
        outs += [(dp // 2, rows, 128), (sum(x.shape[0] for x in along) + dp // 2 * rows, 128)]
    return pl.pallas_call(
        functools.partial(attend_back_kernel, dp, pieces),
        name="attend_back",
        grid=(1,),
        in_specs=[SMEM]
        + [lanes] * 3
        + [pl.BlockSpec((length // SEQ, 128), lambda _: (0, pair), pipeline_mode=pl.Buffered(1))] * 4
        + [pl.BlockSpec((1, 2, length), lambda _: (pair, 0, 0)), fixed((1, length))]
        + [fixed((length, 128))] * 2
        + [fixed(nin.shape)]
        + [fixed(x.shape) for x in along],
        out_specs=[fixed(x) for x in outs],
        out_shape=[jax.ShapeDtypeStruct(x, bf16) for x in outs],
        scratch_shapes=[pltpu.VMEM((length, 128), bf16)]
        + [pltpu.VMEM((length, 128), f32)] * 2
        + [pltpu.VMEM((part, 384), bf16), pltpu.VMEM((128, length), bf16), pltpu.VMEM((128, length), f32)],
        compiler_params=params(60),
    )(place, q, k, v, *da, lse, seg_row, cos, sin, nin, *along)


def main_lanes(inner):
    return inner // 128 * 128


def pack_attn_kernel(
    q_ref, k_ref, v_ref, o_ref, d_ref, ag_ref, mg_ref, tok_ref, c0, c1, c2, c3, orows_ref, drows_ref, *halves_refs
):
    me = lax.axis_index("seq")
    owner = me * lax.axis_size("dp") + lax.axis_index("dp")
    w_rows, width = q_ref.shape
    part = width // SEQ
    lane = lax.broadcasted_iota(jnp.int32, (1, 128), 1)
    spot = lane // w_rows == owner % (128 // w_rows)

    def spread(gain):
        return jnp.where(spot, jnp.concatenate([gain[...].astype(f32)] * (128 // w_rows), axis=1), 0.0)

    row = lax.broadcasted_iota(jnp.int32, (16, 128), 0)
    gains = jnp.where(row == 0, spread(ag_ref), jnp.where(row == 1, spread(mg_ref), 0.0)).astype(bf16)
    for k, out in enumerate((c0, c1, c2, c3)):
        at = 0
        for ref in (q_ref, k_ref, v_ref):
            for t in range(part // 128):
                lanes = pl.ds(pl.multiple_of((me ^ k) * part + t * 128, 128), 128)
                out[at : at + w_rows, :] = ref[:, lanes]
                at += w_rows
        out[at : at + 16, :] = gains
    for ref, out in ((o_ref, orows_ref), (d_ref, drows_ref)):
        rows = ref.shape[0]
        for t in range(width // 128):
            out[t * rows : (t + 1) * rows, :] = ref[:, t * 128 : t * 128 + 128]
    for i, out in enumerate(halves_refs):
        rows = out.shape[0]
        out[...] = tok_ref[i * rows : (i + 1) * rows, :]


def pack_attn(wq, wk, wv, wo, wd, attn_gain, mlp_gain, tok):
    w_rows, width = wq.shape
    tiles = width // 128
    shapes = [(3 * tiles // SEQ * w_rows + 16, 128)] * 4 + [(tiles * w_rows, 128), (tiles * wd.shape[0], 128)]
    shapes += [(tok.shape[0] // 2, width)] * 2
    return pl.pallas_call(
        pack_attn_kernel,
        name="pack_attn",
        grid=(1,),
        in_specs=[fixed(w.shape) for w in (wq, wk, wv, wo, wd)] + [fixed((1, w_rows))] * 2 + [fixed(tok.shape)],
        out_specs=[fixed(x) for x in shapes],
        out_shape=[jax.ShapeDtypeStruct(x, bf16) for x in shapes],
        compiler_params=params(60),
    )(wq, wk, wv, wo, wd, attn_gain[None], mlp_gain[None], tok)


def pack_ffn_kernel(place_ref, g_ref, u_ref, c0, c1, c2, c3):
    me = place_ref[0]
    w_rows = g_ref.shape[0]
    inner = g_ref.shape[1] // SEQ
    main = main_lanes(inner)
    for s in range(SEQ):
        gate, up = g_ref[:, s * inner : (s + 1) * inner], u_ref[:, s * inner : (s + 1) * inner]
        tiles = [field[:, t * 128 : t * 128 + 128] for field in (gate, up) for t in range(main // 128)]
        tiles.append(jnp.concatenate([gate[:, main:], up[:, main:]], axis=1))
        for k, out in enumerate((c0, c1, c2, c3)):

            @pl.when(me ^ k == s)
            def _():
                for t, tile in enumerate(tiles):
                    out[t * w_rows : (t + 1) * w_rows, :] = tile


def pack_ffn(place, wg, wu):
    w_rows = wg.shape[0]
    inner = wg.shape[1] // SEQ
    return pl.pallas_call(
        pack_ffn_kernel,
        name="pack_ffn",
        grid=(1,),
        in_specs=[SMEM] + [fixed(w.shape) for w in (wg, wu)],
        out_specs=[fixed((2 * inner // 128 * w_rows, 128))] * 4,
        out_shape=[jax.ShapeDtypeStruct((2 * inner // 128 * w_rows, 128), bf16)] * 4,
        compiler_params=params(60),
    )(place, wg, wu)


def source_of(place_ref, dp, slot):
    groups = dp // 2
    b, j = slot // groups, slot % groups
    z, y = place_ref[2] // 2, place_ref[2] % 2
    return ((z + groups - j) % groups) * 2 + (y ^ b)


def assemble_attn_kernel(place_ref, *refs):
    dp = len(refs) - 4
    pieces, (w_ref, wo_ref, ag_ref, mg_ref) = refs[:dp], refs[dp:]
    width, lanes = w_ref.shape
    w_rows = width // (SEQ * dp)
    part = width // SEQ
    chunk = lanes // 128 * w_rows + 16
    ag_ref[...] = jnp.zeros_like(ag_ref)
    mg_ref[...] = jnp.zeros_like(mg_ref)
    for slot, piece in enumerate(pieces):
        src = source_of(place_ref, dp, slot)
        for k in range(SEQ):
            s = place_ref[0] ^ k
            row = pl.multiple_of(s * part + src * w_rows, w_rows)
            for t in range(lanes // 128):
                at = k * chunk + t * w_rows
                w_ref[pl.ds(row, w_rows), t * 128 : t * 128 + 128] = piece[at : at + w_rows, :]
            gains = piece[(k + 1) * chunk - 16 : (k + 1) * chunk, :].astype(f32)
            tile = (s * dp + src) * w_rows // 128
            ag_ref[pl.ds(tile, 1), :] += gains[0:1, :]
            mg_ref[pl.ds(tile, 1), :] += gains[1:2, :]
        row = pl.multiple_of(src * w_rows, w_rows)
        for t in range(width // 128):
            at = SEQ * chunk + t * w_rows
            wo_ref[pl.ds(row, w_rows), t * 128 : t * 128 + 128] = piece[at : at + w_rows, :]


def assemble_attn(place, pieces, width):
    shapes = [(width, 3 * width // SEQ), (width // SEQ, width), (width // 128, 128), (width // 128, 128)]
    return pl.pallas_call(
        assemble_attn_kernel,
        name="assemble_attn",
        grid=(1,),
        in_specs=[SMEM] + [fixed(x.shape) for x in pieces],
        out_specs=[fixed(x) for x in shapes],
        out_shape=[jax.ShapeDtypeStruct(x, t) for x, t in zip(shapes, (bf16, bf16, f32, f32))],
        compiler_params=params(12),
    )(place, *pieces)


def assemble_rows_kernel(place_ref, *refs):
    dp = len(refs) - 1
    pieces, out_ref = refs[:dp], refs[dp]
    count = out_ref.shape[0] // dp
    for slot, piece in enumerate(pieces):
        row = pl.multiple_of(source_of(place_ref, dp, slot) * count, 8)
        for t in range(out_ref.shape[1] // 128):
            out_ref[pl.ds(row, count), t * 128 : t * 128 + 128] = piece[t * count : (t + 1) * count, :]


def assemble_rows(place, pieces, width, inner):
    return pl.pallas_call(
        assemble_rows_kernel,
        name="assemble_rows",
        grid=(1,),
        in_specs=[SMEM] + [fixed(x.shape) for x in pieces],
        out_specs=fixed((inner, width)),
        out_shape=jax.ShapeDtypeStruct((inner, width), bf16),
        compiler_params=params(12),
    )(place, *pieces)


def ffn_kernel(me_ref, tok_ref, og_ref, a0, a1, a2, a3, wo0, wo1, wo2, wo3, gain_ref, w_ref, wd_ref, *outs):
    nm_ref, hid_ref, dgu_ref, mid_ref, *lists = outs
    step = pl.program_id(0)
    if len(w_ref.shape) == 3:
        pieces, w_ref = w_ref, lists.pop()
        dp = pieces.shape[0]
        width, lanes = w_ref.shape
        w_rows = width // (SEQ * dp)
        chunk = lanes // 128 * w_rows

        @pl.when(step == 0)
        def _():
            for k in range(SEQ):
                for src in range(dp):
                    row = pl.multiple_of((me_ref[0] ^ k) * (width // SEQ) + src * w_rows, w_rows)
                    for t in range(lanes // 128):
                        at = k * chunk + t * w_rows
                        w_ref[pl.ds(row, w_rows), t * 128 : t * 128 + 128] = pieces[src, at : at + w_rows, :]

    mid = tok_ref[...].astype(f32)
    inner = wd_ref.shape[0]
    main = main_lanes(inner)
    for a, wo in zip((a0, a1, a2, a3), (wo0, wo1, wo2, wo3)):
        mid = mid + mul(a[...], wo[...], 1, 0)
    scale = lax.rsqrt(jnp.mean(mid * mid, axis=-1, keepdims=True) + epsilon)
    nm = (mid * scale * gain_ref[...]).astype(bf16)
    nm_ref[...] = nm
    d_hidden = mul(og_ref[...], wd_ref[...], 1, 1)
    both = mul(nm, w_ref[...], 1, 0)

    def gated(gate, up, grad):
        sig = jax.nn.sigmoid(gate)
        silu = gate * sig
        return (
            (silu * up).astype(bf16),
            (grad * up * (sig * (1.0 + gate * (1.0 - sig)))).astype(bf16),
            (grad * silu).astype(bf16),
        )

    hid_main, dg_main, du_main = gated(both[:, :main], both[:, main : 2 * main], d_hidden[:, :main])
    last = both[:, 2 * main :]
    hid_last, dg_last, du_last = gated(last[:, : inner - main], last[:, inner - main :], d_hidden[:, main:])
    hid_ref[:, :main] = hid_main
    hid_ref[:, main:] = hid_last
    dgu_ref[:, :main] = dg_main
    dgu_ref[:, main : 2 * main] = du_main
    dgu_ref[:, 2 * main :] = jnp.concatenate([dg_last, du_last], axis=1)
    dnm = mul(dgu_ref[...], w_ref[...], 1, 1).astype(bf16)
    lo = mul(hid_ref[...], wd_ref[...], 1, 0).astype(bf16)
    dnm_kept, dnm_sent, lo_kept, lo_sent = lists
    rows = tok_ref.shape[0]
    for k in range(SEQ):

        @pl.when(step == SEQ - 1 - k)
        def _():
            here = slice(k // 2 * rows, (k // 2 + 1) * rows)
            (dnm_sent if k % 2 else dnm_kept)[here, :] = dnm
            (lo_sent if k % 2 else lo_kept)[here, :] = lo

    @pl.when(step == SEQ - 1)
    def _():
        mid_ref[...] = mid


def ffn_call(me, tok, og, att, wo, gain, w, wd):
    length, width = tok.shape
    rows = length // SEQ
    inner = wd.shape[0]
    part = att[0].shape[1]
    rel = lambda k, m: (SEQ - 1 - k, 0)
    here = lambda k, m: (m[0] ^ (SEQ - 1 - k), 0)
    return pl.pallas_call(
        ffn_kernel,
        name="ffn",
        grid_spec=pltpu.PrefetchScalarGridSpec(
            num_scalar_prefetch=1,
            grid=(SEQ,),
            in_specs=[pl.BlockSpec((rows, width), rel)] * 2
            + [pl.BlockSpec((rows, part), here)] * 4
            + [fixed(x.shape) for x in wo]
            + [fixed((1, width)), fixed(w.shape), fixed(wd.shape)],
            out_specs=[
                pl.BlockSpec((rows, width), rel),
                pl.BlockSpec((rows, inner), rel),
                pl.BlockSpec((rows, 2 * inner), rel),
                fixed((rows, width)),
            ]
            + [fixed((2 * rows, width))] * 4,
            scratch_shapes=[pltpu.VMEM((width, 2 * inner), bf16)] * (w.ndim - 2),
        ),
        out_shape=[
            jax.ShapeDtypeStruct((length, width), bf16),
            jax.ShapeDtypeStruct((length, inner), bf16),
            jax.ShapeDtypeStruct((length, 2 * inner), bf16),
            jax.ShapeDtypeStruct((rows, width), f32),
        ]
        + [jax.ShapeDtypeStruct((2 * rows, width), bf16)] * 4,
        compiler_params=params(60),
    )(me, tok, og, *att, *wo, gain, w, wd)


def owner_index(place_ref, dp, slot):
    groups = dp // 2
    b, j = slot // groups, slot % groups
    z, y = place_ref[2] // 2, place_ref[2] % 2
    return ((z + j) % groups) * 2 + (y ^ b)


def columns_grad_kernel(place_ref, act_ref, grad_ref, *refs):
    outs, work = refs[:-1], refs[-1]
    dp = len(outs)
    work[...] = mul(act_ref[...], grad_ref[...], 0, 0).astype(bf16)
    w_rows = work.shape[0] // dp
    for slot, ref in enumerate(outs):
        here = pl.ds(pl.multiple_of(owner_index(place_ref, dp, slot) * w_rows, w_rows), w_rows)
        for t in range(work.shape[1] // 128):
            ref[t * w_rows : (t + 1) * w_rows, :] = work[here, t * 128 : t * 128 + 128]


def columns_grad_plain(act, grad, dp):
    width, lanes = act.shape[1], grad.shape[1]
    w_rows = width // (SEQ * dp)
    grad = mul(act, grad, 0, 0).astype(bf16).reshape(SEQ, dp, w_rows, lanes // 128, 128)
    return grad.transpose(1, 0, 3, 2, 4).reshape(dp, -1, 128)


def columns_grad(place, act, grad, dp):
    length, width = act.shape
    lanes = grad.shape[1]
    part = width // SEQ
    chunk = lanes // 128 * (part // dp)
    return pl.pallas_call(
        columns_grad_kernel,
        name="columns_grad",
        grid_spec=pltpu.PrefetchScalarGridSpec(
            num_scalar_prefetch=1,
            grid=(SEQ,),
            in_specs=[pl.BlockSpec((length, part), lambda s, m: (0, s)), fixed(grad.shape)],
            out_specs=[pl.BlockSpec((chunk, 128), lambda s, m: (s, 0))] * dp,
            scratch_shapes=[pltpu.VMEM((part, lanes), bf16)],
        ),
        out_shape=[jax.ShapeDtypeStruct((SEQ * chunk, 128), bf16)] * dp,
        compiler_params=params(60),
    )(place, act, grad)


def out_grad_kernel(place_ref, act_ref, d0, d1, d2, d3, kept_ref, sent_ref, work):
    rows = d0.shape[0]
    total = 0.0
    for k, ref in enumerate((d0, d1, d2, d3)):
        act = act_ref[pl.ds(pl.multiple_of((place_ref[0] ^ k) * rows, rows), rows), :]
        total = total + mul(act, ref[...], 0, 0)
    work[...] = total.astype(bf16)
    dp = 2 * kept_ref.shape[0]
    count = work.shape[0] // dp
    at = 0
    for slot in range(dp):
        here = pl.ds(pl.multiple_of(owner_index(place_ref, dp, slot) * count, count), count)
        for t in range(work.shape[1] // 128):
            piece = work[here, t * 128 : t * 128 + 128]
            if slot < dp // 2:
                kept_ref[slot, t * count : (t + 1) * count, :] = piece
            else:
                sent_ref[at : at + count, :] = piece
                at += count


def out_projection_grad(place, act, d_branch, dp):
    width = d_branch[0].shape[1]
    part = act.shape[1]
    shape = (dp // 2, width // 128 * (part // dp), 128)
    sent = (shape[0] * shape[1], 128)
    return pl.pallas_call(
        out_grad_kernel,
        name="out_projection_grad",
        grid=(1,),
        in_specs=[SMEM, fixed(act.shape)] + [fixed(x.shape) for x in d_branch],
        out_specs=[fixed(shape), fixed(sent)],
        out_shape=[jax.ShapeDtypeStruct(shape, bf16), jax.ShapeDtypeStruct(sent, bf16)],
        scratch_shapes=[pltpu.VMEM((part, width), bf16)],
        compiler_params=params(24),
    )(place, act, *d_branch)


def down_grad_kernel(act_ref, grad_ref, out_ref):
    out_ref[...] = mul(act_ref[...], grad_ref[...], 0, 0).astype(bf16)


def down_grad(act, grad):
    length, width = grad.shape
    step = 256
    return pl.pallas_call(
        down_grad_kernel,
        name="down_grad",
        grid=(width // step,),
        in_specs=[fixed(act.shape), pl.BlockSpec((length, step), lambda c: (0, c))],
        out_specs=pl.BlockSpec((act.shape[1], step), lambda c: (0, c)),
        out_shape=jax.ShapeDtypeStruct((act.shape[1], width), bf16),
        compiler_params=params(60),
    )(act, grad)


def simple(kernel, name, args, outs, limit=24):
    return pl.pallas_call(
        kernel,
        name=name,
        grid=(1,),
        in_specs=[SMEM if x.dtype == jnp.int32 else fixed(x.shape) for x in args],
        out_specs=[fixed(x.shape) for x in outs],
        out_shape=outs,
        compiler_params=params(limit),
    )(*args)


def shaped(dtype, *shape):
    return jax.ShapeDtypeStruct(shape, dtype)


def sum_kernel(*refs):
    *ins, out = refs
    out[...] = sum(x[...].astype(f32) for x in ins).astype(out.dtype)


def total(*pieces):
    return simple(sum_kernel, "total", pieces, [shaped(bf16, *pieces[0].shape)])[0]


def halves_kernel(kept_ref, got_ref, near_ref, far_ref):
    rows = near_ref.shape[0]
    near_ref[...] = kept_ref[:rows, :].astype(f32) + got_ref[:rows, :].astype(f32)
    far_ref[...] = (kept_ref[rows:, :].astype(f32) + got_ref[rows:, :].astype(f32)).astype(bf16)


def halves(kept, got):
    rows, width = kept.shape[0] // 2, kept.shape[1]
    return simple(halves_kernel, "halves", (kept, got), [shaped(f32, rows, width), shaped(bf16, rows, width)])


def slots_kernel(kept_ref, got_ref, *outs):
    count = kept_ref.shape[1]
    at = got_ref.shape[0] - len(outs) * count
    for j, out in enumerate(outs):
        got = got_ref[at + j * count : at + (j + 1) * count, :]
        out[...] = (kept_ref[j].astype(f32) + got.astype(f32)).astype(out.dtype)


def slots(kept, got):
    shape = kept.shape[1:]
    outs = [shaped(f32, *shape)] + [shaped(bf16, *shape)] * (kept.shape[0] - 1)
    return simple(slots_kernel, "slots", (kept, got), outs)


def back_through_norm(grad, field, gain):
    scale = lax.rsqrt(jnp.mean(field * field, axis=-1, keepdims=True) + epsilon)
    unit = field * scale
    pressed = grad * gain
    return scale * (pressed - unit * jnp.mean(pressed * unit, axis=-1, keepdims=True))


def branch_kernel(near_ref, far_ref, mid_ref, og_ref, gain_ref, w0, w1, w2, w3, d_mid_ref, d_ref, a0, a1, a2, a3):
    grad = near_ref[...] + far_ref[...].astype(f32)
    d_mid = og_ref[...].astype(f32) + back_through_norm(grad, mid_ref[...], gain_ref[...])
    d_mid_ref[...] = d_mid
    d_branch = d_mid.astype(bf16)
    d_ref[...] = d_branch
    for w, a in ((w0, a0), (w1, a1), (w2, a2), (w3, a3)):
        a[...] = mul(d_branch, w[...], 1, 1).astype(bf16)


def token_grad_kernel(near_ref, far_ref, tok_ref, gain_ref, d_mid_ref, out_ref):
    grad = near_ref[...] + far_ref[...].astype(f32)
    out_ref[...] = (d_mid_ref[...] + back_through_norm(grad, tok_ref[...].astype(f32), gain_ref[...])).astype(bf16)


def cut_kernel(me_ref, *refs):
    ins, d_ref, (mine_ref, near_ref, far_ref) = refs[:-4], refs[-4], refs[-3:]
    groups = [ins[:4], ins[4:8], ins[8:]]
    count = far_ref.shape[0] - 2 * mine_ref.shape[0]
    far_ref[2 * mine_ref.shape[0] :, :] = d_ref[pl.ds(pl.multiple_of(((me_ref[0] >> 1) ^ 1) * count, count), count), 256:]
    me = me_ref[0]
    at = 0
    for pieces in groups:
        chunk = pieces[0].shape[0] // SEQ

        def chunk_of(s):
            here = pl.ds(pl.multiple_of(s * chunk, 8), chunk)
            return sum(x[here, :].astype(f32) for x in pieces).astype(bf16)

        mine_ref[at : at + chunk, :] = chunk_of(me)
        near_ref[at : at + chunk, :] = chunk_of(me ^ 1)
        for core in range(2):
            row = core * mine_ref.shape[0] + at
            far_ref[row : row + chunk, :] = chunk_of(((me >> 1) ^ 1) * 2 + core)
        at += chunk


def cut(me, attn, ffn, d_pair):
    rows = (attn[0][0].shape[0] * 2 + ffn[0].shape[0]) // SEQ
    outs = [shaped(bf16, n, 128) for n in (rows, rows, 2 * rows + d_pair.shape[0] // 2)]
    return simple(cut_kernel, "cut", (me, *attn[0], *attn[1], *ffn, d_pair), outs)


def relay_kernel(me_ref, near, far, d0_ref, d1_ref, far0_ref, out_ref):
    me = me_ref[0]
    core = (me & 1) ^ 1
    count = near.shape[0]
    out_ref[:count, :] = near[...]
    out_ref[count : 2 * count, :] = far[pl.ds(pl.multiple_of(core * count, 8), count), :]
    at = 2 * count
    rows = far0_ref.shape[0] // 2
    first = pl.multiple_of((me ^ 1) * rows, rows)
    for d_ref, far_ref, row in ((d0_ref, far0_ref, 0), (d1_ref, far, 2 * count)):
        out_ref[at : at + rows, :] = d_ref[pl.ds(first, rows), 256:]
        out_ref[at + rows : at + 2 * rows, :] = far_ref[pl.ds(pl.multiple_of(row + core * rows, 8), rows), :]
        at += 2 * rows


def value_grad_kernel(me_ref, acc_ref, d0_ref, d1_ref, far0_ref, far, got_ref, out_ref):
    me = me_ref[0]
    rows = acc_ref.shape[0]
    first = pl.multiple_of(me * rows, rows)
    at = far.shape[0] - 2 * rows

    for p, (d_ref, far_ref, row) in enumerate(((d0_ref, far0_ref, 0), (d1_ref, far, at))):
        pieces = (
            d_ref[pl.ds(first, rows), 256:],
            got_ref[at : at + rows, :],
            far_ref[pl.ds(pl.multiple_of(row + (me & 1) * rows, 8), rows), :],
            got_ref[at + rows : at + 2 * rows, :],
        )
        for k, piece in enumerate(pieces):
            lanes = pl.ds(pl.multiple_of((me ^ k) * 256 + p * 128, 128), 128)
            out_ref[:, lanes] = acc_ref[:, lanes] + piece.astype(f32)
        at += 2 * rows


def finish_kernel(
    me_ref, mine, far, got_ref, o0, o1, o2, o3, wq, wk, wv, wg, wu, ga_ref, gm_ref, down_ref,
    gq_ref, gk_ref, gv_ref, go_ref, gga_ref, gg_ref, gu_ref, ggm_ref, gd_ref, cols_a, cols_f,
):
    me = me_ref[0]
    gd_ref[...] = down_ref[...].astype(f32)
    count = mine.shape[0]
    at = 0
    for cols in (cols_a, cols_f):
        chunk = cols.shape[1]
        cols[0] = mine[at : at + chunk, :]
        cols[2] = far[pl.ds(pl.multiple_of((me & 1) * count + at, 8), chunk), :]
        cols[1] = got_ref[at : at + chunk, :]
        cols[3] = got_ref[count + at : count + at + chunk, :]
        at += chunk
    out = sum(x[...].astype(f32) for x in (o0, o1, o2, o3))
    w_rows, width = gq_ref.shape
    for t in range(width // 128):
        go_ref[:, t * 128 : t * 128 + 128] = out[t * w_rows : (t + 1) * w_rows, :]
    unpack_attn(me, cols_a, gq_ref, gk_ref, gv_ref)
    gga_ref[...] = gain_grad(((wq, gq_ref), (wk, gk_ref), (wv, gv_ref)), ga_ref)
    unpack_ffn(me, cols_f, gg_ref, gu_ref)
    ggm_ref[...] = gain_grad(((wg, gg_ref), (wu, gu_ref)), gm_ref)


def gain_grad(pairs, gain_ref):
    column = sum(jnp.sum(w[...].astype(f32) * g[...], axis=1, keepdims=True) for w, g in pairs)
    rows = column.shape[0]
    same = lax.broadcasted_iota(jnp.int32, (rows, rows), 0) == lax.broadcasted_iota(jnp.int32, (rows, rows), 1)
    return jnp.sum(jnp.where(same, column, 0.0), axis=0, keepdims=True) / gain_ref[...].astype(f32)


def unpack_attn(me, cols_ref, *outs):
    w_rows, width = outs[0].shape
    part = width // SEQ
    for s in range(SEQ):
        at = 0
        for t in range(part // 128):
            for ref in outs:
                lanes = slice(s * part + t * 128, s * part + t * 128 + 128)
                ref[:, lanes] = cols_ref[me ^ s, at : at + w_rows, :].astype(f32)
                at += w_rows


def unpack_ffn(me, cols_ref, gg_ref, gu_ref):
    w_rows = gg_ref.shape[0]
    inner = gg_ref.shape[1] // SEQ
    main = main_lanes(inner)
    rest = inner - main
    half = main // 128
    for s in range(SEQ):
        slot = me ^ s
        tiles = [cols_ref[slot, t * w_rows : (t + 1) * w_rows, :].astype(f32) for t in range(2 * inner // 128)]
        gg_ref[:, s * inner : (s + 1) * inner] = jnp.concatenate(tiles[:half] + [tiles[-1][:, :rest]], axis=1)
        gu_ref[:, s * inner : (s + 1) * inner] = jnp.concatenate(tiles[half : 2 * half] + [tiles[-1][:, rest:]], axis=1)


def unpack_kernel(me_ref, cols_a, cols_f, wq, wk, wv, wg, wu, ga_ref, gm_ref, gq_ref, gk_ref, gv_ref, gga_ref, gg_ref, gu_ref, ggm_ref):
    unpack_attn(me_ref[0], cols_a, gq_ref, gk_ref, gv_ref)
    gga_ref[...] = gain_grad(((wq, gq_ref), (wk, gk_ref), (wv, gv_ref)), ga_ref)
    unpack_ffn(me_ref[0], cols_f, gg_ref, gu_ref)
    ggm_ref[...] = gain_grad(((wg, gg_ref), (wu, gu_ref)), gm_ref)


def input_grad_kernel(me_ref, *refs):
    *d_refs, w_ref, kept_ref, sent_ref = refs
    step = pl.program_id(0)
    d_qkv = [d[:, i * 128 : i * 128 + 128] for i in range(3) for d in d_refs]
    grad = mul(jnp.concatenate(d_qkv, axis=1), w_ref[...], 1, 1).astype(bf16)
    rows = grad.shape[0]
    for k in range(SEQ):

        @pl.when(step == SEQ - 1 - k)
        def _():
            (sent_ref if k % 2 else kept_ref)[k // 2 * rows : (k // 2 + 1) * rows, :] = grad


def input_grad(me, d_qkv, w):
    length, part = d_qkv[0].shape
    width = w.shape[0]
    rows = length // SEQ
    here = lambda k, m: (m[0] ^ (SEQ - 1 - k), 0)
    return pl.pallas_call(
        input_grad_kernel,
        name="input_grad",
        grid_spec=pltpu.PrefetchScalarGridSpec(
            num_scalar_prefetch=1,
            grid=(SEQ,),
            in_specs=[pl.BlockSpec((rows, part), here)] * len(d_qkv) + [fixed(w.shape)],
            out_specs=[fixed((2 * rows, width))] * 2,
        ),
        out_shape=[jax.ShapeDtypeStruct((2 * rows, width), bf16)] * 2,
        compiler_params=params(16),
    )(me, *d_qkv, w)


def to_core(value):
    return lax.ppermute(value, "seq", [(i, i ^ 1) for i in range(SEQ)])


def to_chip(value):
    return lax.ppermute(value, "seq", [(i, i ^ 2) for i in range(SEQ)])


def to_both(value):
    return lax.ppermute(value, "seq", [(i, i ^ 3) for i in range(SEQ)])


def gather_rel(value):
    far = to_chip(value)
    return value, to_core(value), far, to_core(far)


def exchange_rel(pieces):
    return [pieces[0], to_core(pieces[1]), to_chip(pieces[2]), to_both(pieces[3])]


def scatter_sum(kept, sent):
    sums = add(kept, to_core(sent))
    rows = kept.shape[0] // 2
    return sums[:rows] + to_chip(sums[rows:].astype(bf16)).astype(f32)


def add(a, b):
    return a.astype(f32) + b.astype(f32)


def to_y(value):
    dp = lax.axis_size("dp")
    return lax.ppermute(value, "dp", [(i, i ^ 1) for i in range(dp)])


def to_z(value, hops=1):
    dp = lax.axis_size("dp")
    return lax.ppermute(value, "dp", [(i, (i + 2 * hops) % dp) for i in range(dp)])


def rotary(length, head_width):
    pairs = jnp.arange(head_width // 2, dtype=f32)
    freq = jnp.exp(pairs * (-2.0 * math.log(10000.0) / head_width))
    theta = jnp.arange(length, dtype=jnp.int32).astype(f32)[:, None] * freq[None, :]
    cos, sin = jnp.cos(theta), jnp.sin(theta)
    return jnp.concatenate([cos] * 4, axis=1), jnp.concatenate([-sin, sin] * 2, axis=1)


class Stage:
    def fence(self):
        names = list(vars(self))
        for name, value in zip(names, sync(*[getattr(self, name) for name in names])):
            setattr(self, name, value)


def body_direct(
    tokens, first_values, value_grad_acc, segment_ids, query_weight, key_weight, value_weight, out_weight,
    attn_gain, gate_weight, up_weight, down_weight, mlp_gain, out_grad,
):
    dp = lax.axis_size("dp")
    zs = dp // 2
    rows, width = tokens.shape[1:]
    length = segment_ids.shape[1]
    w_rows = query_weight.shape[0]
    part = width // SEQ
    inner = gate_weight.shape[1] // SEQ
    me = lax.axis_index("seq").astype(jnp.int32)
    mine = lax.axis_index("dp").astype(jnp.int32)
    me_arg = me[None]
    place = jnp.stack([me, me * dp + mine, mine])
    s = Stage()

    half = rows // 2
    *s.cols, s.orows, drows, tok_a, tok_b = pack_attn(
        query_weight, key_weight, value_weight, out_weight, down_weight, attn_gain, mlp_gain, tokens[0]
    )
    s.r, s.tok_far = [drows], [tok_a, tok_b]
    s.tokens, s.first, s.out_grad, s.segments = tokens[0], first_values[0], out_grad[0], segment_ids
    s.gate, s.up = gate_weight, up_weight
    s.fence()
    s.cols = exchange_rel(s.cols)
    down = after(s.r[0], s.cols[1])
    down_near, down_next = to_y(down), to_z(down)
    s.fence()
    s.ry = [down_near]
    s.r.append(down_next)
    s.a = [jnp.concatenate([*s.cols, s.orows])]
    del s.cols, s.orows
    s.tok_far[0] = to_chip(s.tok_far[0])
    s.ay = [to_y(s.a[0])]
    s.a.append(to_z(s.a[0]))
    s.fcols = pack_ffn(place, s.gate, s.up)
    del s.gate, s.up
    s.fence()
    s.ay.append(to_y(s.a[1]))
    s.a.append(to_z(s.a[1]))
    s.f_piece = jnp.concatenate(exchange_rel(s.fcols))
    s.cos, s.sin = rotary(length, width // HEADS)
    del s.fcols
    s.fence()
    ffn_all = lax.all_gather(s.f_piece, "dp", axis=0, tiled=False)
    del s.f_piece
    s.tok_far[1] = to_chip(s.tok_far[1])
    s.ay.append(to_y(s.a[2]))
    s.a.append(to_z(s.a[2]))
    s.tok_near = to_core(s.tokens)
    s.first = [lax.dynamic_slice_in_dim(s.first, (me ^ k) * part, part, 1) for k in range(SEQ)]
    s.og_far = [s.out_grad[:half], s.out_grad[half:]]
    s.fence()
    s.ay.append(to_y(s.a[3]))
    s.first = jnp.concatenate(exchange_rel(s.first))
    tok_far = jnp.concatenate(s.tok_far)
    s.tok = jnp.concatenate([s.tokens, s.tok_near, tok_far, to_core(tok_far)])
    del s.tok_far, s.tok_near
    s.fence()
    s.ry.append(to_y(s.r[1]))
    s.r.append(to_z(s.r[1]))
    s.og_far[0] = to_chip(s.og_far[0])
    s.og = [s.out_grad, to_core(s.out_grad)]
    s.w_qkv, s.w_out, attn_gain_all, mlp_gain_all = assemble_attn(place, s.a + s.ay, width)
    s.attn_gain, s.mlp_gain = attn_gain_all.reshape(1, width), mlp_gain_all.reshape(1, width)
    s.nin, s.q, s.k, s.v = qkv_call(me_arg, s.tok, s.first, s.w_qkv, s.attn_gain, s.cos, s.sin)
    del s.a, s.ay, s.first
    s.fence()
    s.og_far[1] = to_chip(s.og_far[1])
    s.wo = [s.w_out, to_core(s.w_out), to_chip(s.w_out)]
    s.ry.append(to_y(s.r[2]))
    s.r.append(to_z(s.r[2]))
    s.attended, s.lse = attend_call(s.q, s.k, s.v, s.segments)
    del s.w_out
    s.fence()
    att_far = to_chip(s.attended)
    s.w_down = assemble_rows(place, s.r + s.ry + [to_y(s.r[3])], width, inner)
    s.att = [s.attended, to_core(s.attended), att_far]
    s.wo.append(to_core(s.wo[2]))
    og_far = jnp.concatenate(s.og_far)
    s.og = jnp.concatenate([*s.og, og_far, to_core(og_far)])
    del s.r, s.ry, s.og_far
    s.fence()
    s.att.append(to_core(s.att[2]))
    s.fence()
    s.nm, s.hidden, s.d_gu, s.mid, s.dnm, dnm_sent, s.lo, s.lo_sent = ffn_call(
        me_arg, s.tok, s.og, s.att, s.wo, s.mlp_gain, ffn_all, s.w_down
    )
    s.dnm, s.dnm_far = halves(s.dnm, to_core(dnm_sent))
    del s.tok, s.att, s.w_down
    s.fence()
    s.dnm_far = to_chip(s.dnm_far)
    pieces = list(columns_grad(place, s.nm, s.d_gu, dp))
    s.f_kept, s.f_sent = pieces[:zs], pieces[zs:]
    s.g_down = down_grad(after(s.hidden, pieces[0]), s.og)
    g_down = lax.psum_scatter(s.g_down, "dp", scatter_dimension=0, tiled=True)
    del s.nm, s.d_gu, s.hidden, s.og
    s.fence()
    s.f_sent[3] = to_y(s.f_sent[3])
    lo_got = to_core(s.lo_sent)
    s.d_middle, s.d_branch, *s.d_att = simple(
        branch_kernel,
        "branch",
        (s.dnm, s.dnm_far, s.mid, s.out_grad, s.mlp_gain, *s.wo),
        [shaped(f32, rows, width), shaped(bf16, rows, width)] + [shaped(bf16, rows, part)] * SEQ,
    )
    s.lo, s.lo_far = halves(s.lo, lo_got)
    del s.dnm, s.dnm_far, s.wo, s.lo_sent, s.g_down
    s.fence()
    s.d_att = exchange_rel(s.d_att)
    s.f_sent[2] = to_y(s.f_sent[2])
    s.f = to_z(total(s.f_kept[3], s.f_sent[3]))
    s.fence()

    def back(pair, *along):
        return attend_back_call(
            pair, place, s.q, s.k, s.v, s.d_att, s.lse, s.segments, s.cos, s.sin, s.nin, dp, True, along
        )

    def other_chip_values(d_pair):
        return lax.dynamic_slice(d_pair, (((me >> 1) ^ 1) * 2 * rows, 256), (2 * rows, 128))

    s.f_sent[1] = to_y(s.f_sent[1])
    s.f = to_z(total(s.f_kept[2], s.f_sent[2], s.f))
    s.d_branch = [s.d_branch, to_core(s.d_branch), to_chip(s.d_branch)]
    d_pair, kept, sent = back(0, s.f_sent[0])
    s.d_qkv, s.kept, s.sent = [d_pair], [kept], [sent]
    s.fence()
    s.sent[0] = to_y(s.sent[0])
    s.f = to_z(total(s.f_kept[1], s.f_sent[1], s.f))
    s.lo_far = to_chip(s.lo_far)
    s.d_branch.append(to_core(s.d_branch[2]))
    s.values_far = to_chip(other_chip_values(s.d_qkv[0]))
    d_pair, kept, sent = back(1)
    s.d_qkv.append(d_pair)
    s.dnin, s.dnin_sent = input_grad(me_arg, s.d_qkv, s.w_qkv)
    s.kept.append(kept)
    s.sent.append(sent)
    del s.nin, s.d_att, s.w_qkv
    s.fence()

    def over_z(first, *others):
        return [first] + [to_z(piece, j + 1) for j, piece in enumerate(others)]

    s.sent[1] = to_y(s.sent[1])
    s.kept[0] = over_z(*slots(s.kept[0], s.sent[0]))
    s.dnin, s.dnin_far = halves(s.dnin, to_core(s.dnin_sent))
    s.out_kept, s.out_sent = out_projection_grad(place, s.attended, s.d_branch, dp)
    del s.d_branch, s.attended, s.dnin_sent
    s.fence()
    s.kept[1] = over_z(*slots(s.kept[1], s.sent[1]))
    s.out_kept = slots(s.out_kept, to_y(s.out_sent))
    s.dnin_far = to_chip(s.dnin_far)
    s.layer_out = total(s.mid, s.lo, s.lo_far)
    del s.lo, s.lo_far, s.mid
    s.fence()
    s.mine, s.near, far = cut(me_arg, s.kept, (s.f_kept[0], s.sent[0], s.f), s.d_qkv[1])
    s.far = to_chip(far)
    s.out_kept = over_z(*s.out_kept)
    s.token_grad = simple(
        token_grad_kernel,
        "token_grad",
        (s.dnin, s.dnin_far, s.tokens, s.attn_gain, s.d_middle),
        [shaped(bf16, rows, width)],
        60,
    )[0]
    s.g_down = g_down
    del s.kept, s.sent, s.out_sent, s.dnin, s.d_middle, s.f, s.f_kept, s.f_sent
    s.fence()
    count = s.mine.shape[0]
    args = (me_arg, s.near, s.far, *s.d_qkv, s.values_far)
    got = to_core(simple(relay_kernel, "relay", args, [shaped(bf16, 2 * count + SEQ * rows, 128)])[0])
    weights = (query_weight, key_weight, value_weight, gate_weight, up_weight)
    shapes = [(w_rows, width)] * 4 + [(1, w_rows)] + [(w_rows, SEQ * inner)] * 2 + [(1, w_rows), g_down.shape]
    args = (s.mine, s.far, got, *s.out_kept, *weights, attn_gain[None], mlp_gain[None], s.g_down)
    a_rows = 3 * part // 128 * w_rows
    g_q, g_k, g_v, g_out, attn_gain_grad, g_gate, g_up, mlp_gain_grad, g_down = pl.pallas_call(
        finish_kernel,
        name="finish",
        grid=(1,),
        in_specs=[SMEM] + [fixed(x.shape) for x in args],
        out_specs=[fixed(x) for x in shapes],
        out_shape=[shaped(f32, *x) for x in shapes],
        scratch_shapes=[pltpu.VMEM((SEQ, a_rows, 128), bf16), pltpu.VMEM((SEQ, count - a_rows, 128), bf16)],
        compiler_params=params(24),
    )(me_arg, *args)
    value_grad_out = simple(
        value_grad_kernel,
        "value_grad",
        (me_arg, value_grad_acc[0], *s.d_qkv, s.values_far, s.far, got),
        [shaped(f32, rows, width)],
    )[0]
    return (
        s.layer_out[None],
        s.token_grad[None],
        value_grad_out[None],
        g_q,
        g_k,
        g_v,
        g_out,
        attn_gain_grad[0],
        g_gate,
        g_up,
        g_down,
        mlp_gain_grad[0],
    )


def body_plain(
    tokens, first_values, value_grad_acc, segment_ids, query_weight, key_weight, value_weight, out_weight,
    attn_gain, gate_weight, up_weight, down_weight, mlp_gain, out_grad,
):
    dp = lax.axis_size("dp")
    rows, width = tokens.shape[1:]
    length = segment_ids.shape[1]
    w_rows, d_rows = query_weight.shape[0], down_weight.shape[0]
    part = width // SEQ
    inner = gate_weight.shape[1] // SEQ
    main = main_lanes(inner)
    me = lax.axis_index("seq").astype(jnp.int32)
    mine = lax.axis_index("dp").astype(jnp.int32)
    me_arg = me[None]
    place = jnp.stack([me, me * dp + mine, mine])

    def columns(weight, count):
        return weight.reshape(w_rows, SEQ, count).transpose(1, 0, 2)

    owner = jnp.arange(width) // w_rows == me * dp + mine

    def spread(gain):
        full = jnp.where(owner, jnp.tile(gain, width // w_rows), jnp.zeros((), bf16))
        cut = 3 * part
        return jnp.stack([full[:cut], jnp.pad(full[cut:], (0, 2 * cut - width))])

    gains = jnp.concatenate([spread(attn_gain), spread(mlp_gain), jnp.zeros((4, 3 * part), bf16)])
    attn_cols = jnp.concatenate([columns(w, part) for w in (query_weight, key_weight, value_weight)], axis=2)
    attn_cols = jnp.concatenate([attn_cols, jnp.broadcast_to(gains[None], (SEQ,) + gains.shape)], axis=1)
    gate_cols, up_cols = columns(gate_weight, inner), columns(up_weight, inner)
    ffn_cols = jnp.concatenate(
        [gate_cols[:, :, :main], up_cols[:, :, :main], gate_cols[:, :, main:], up_cols[:, :, main:]], axis=2
    )
    attn_cols = lax.all_to_all(attn_cols, "seq", split_axis=0, concat_axis=0, tiled=True)
    ffn_cols = lax.all_to_all(ffn_cols, "seq", split_axis=0, concat_axis=0, tiled=True)
    attn_all = lax.all_gather(attn_cols.reshape(-1, 3 * part), "dp", axis=0, tiled=True)
    attn_all = attn_all.reshape(dp, SEQ, w_rows + 8, 3 * part)
    w_qkv = attn_all[:, :, :w_rows].transpose(1, 0, 2, 3).reshape(width, 3 * part)
    gain_all = jnp.sum(attn_all[:, :, w_rows : w_rows + 4].astype(f32), axis=(0, 1))
    attn_gain_all = jnp.concatenate([gain_all[0], gain_all[1]])[None, :width]
    mlp_gain_all = jnp.concatenate([gain_all[2], gain_all[3]])[None, :width]
    w_out = lax.all_gather(out_weight, "dp", axis=0, tiled=True)
    w_down = lax.all_gather(down_weight, "dp", axis=0, tiled=True)
    ffn_all = lax.all_gather(ffn_cols.reshape(-1, 2 * inner), "dp", axis=0, tiled=True)
    w_ffn = ffn_all.reshape(dp, SEQ, w_rows, 2 * inner).transpose(1, 0, 2, 3).reshape(width, 2 * inner)

    cos, sin = rotary(length, width // HEADS)
    tok = jnp.concatenate(gather_rel(tokens[0]))
    og = jnp.concatenate(gather_rel(out_grad[0]))
    first_cols = first_values[0].reshape(rows, SEQ, part)
    first = exchange_rel([lax.dynamic_index_in_dim(first_cols, me ^ k, 1, keepdims=False) for k in range(SEQ)])
    nin, q, k, v = qkv_call(me_arg, tok, jnp.concatenate(first), w_qkv, attn_gain_all, cos, sin)
    attended, lse = attend_call(q, k, v, segment_ids)
    wo = gather_rel(w_out)
    nm, hidden, d_gu, mid, *sums = ffn_call(me_arg, tok, og, gather_rel(attended), wo, mlp_gain_all, w_ffn, w_down)
    layer_out = (mid + scatter_sum(*sums[2:])).astype(bf16)
    d_middle = out_grad[0].astype(f32) + back_through_norm(scatter_sum(*sums[:2]), mid, mlp_gain_all)
    d_branch = d_middle.astype(bf16)
    d_att = exchange_rel([mul(d_branch, w, 1, 1).astype(bf16) for w in wo])
    d_branch_all = jnp.stack(gather_rel(d_branch))[me ^ jnp.arange(SEQ)].reshape(length, width)
    d_qkv = [
        attend_back_call(pair, place, q, k, v, d_att, lse, segment_ids, cos, sin, nin, dp, False)[0] for pair in range(2)
    ]
    dnin = scatter_sum(*input_grad(me_arg, d_qkv, w_qkv))
    token_grad = d_middle + back_through_norm(dnin, tokens[0].astype(f32), attn_gain_all)
    dv = jnp.concatenate([d[:, 256:] for d in d_qkv], axis=1)
    dv = exchange_rel([lax.dynamic_slice_in_dim(dv, (me ^ i) * rows, rows, 0) for i in range(SEQ)])
    dv = jnp.stack(dv)[me ^ jnp.arange(SEQ)].transpose(1, 0, 2).reshape(rows, width)
    value_grad_out = value_grad_acc[0] + dv.astype(f32)

    def over_dp(grads):
        return lax.psum_scatter(grads.reshape(-1, 128), "dp", scatter_dimension=0, tiled=True)

    def to_rows(sums):
        sums = sums.reshape(SEQ, -1, 128)
        return jnp.stack(exchange_rel([lax.dynamic_index_in_dim(sums, me ^ i, 0, keepdims=False) for i in range(SEQ)]))

    attn_sums = over_dp(columns_grad_plain(nin, jnp.concatenate(d_qkv, axis=1), dp))
    ffn_sums = over_dp(columns_grad_plain(nm, d_gu, dp))
    g_out = lax.psum_scatter(mul(attended, d_branch_all, 0, 0).astype(bf16), "dp", scatter_dimension=0, tiled=True)
    g_down = lax.psum_scatter(mul(hidden, og, 0, 0).astype(bf16), "dp", scatter_dimension=0, tiled=True)
    weights = (query_weight, key_weight, value_weight, gate_weight, up_weight)
    shapes = [(w_rows, width)] * 3 + [(1, w_rows)] + [(w_rows, SEQ * inner)] * 2 + [(1, w_rows)]
    args = (me_arg, to_rows(attn_sums), to_rows(ffn_sums), *weights, attn_gain[None], mlp_gain[None])
    g_q, g_k, g_v, attn_gain_grad, g_gate, g_up, mlp_gain_grad = simple(
        unpack_kernel, "unpack", args, [shaped(f32, *x) for x in shapes]
    )
    return (
        layer_out[None],
        token_grad.astype(bf16)[None],
        value_grad_out[None],
        g_q,
        g_k,
        g_v,
        g_out.astype(f32),
        attn_gain_grad[0],
        g_gate,
        g_up,
        g_down.astype(f32),
        mlp_gain_grad[0],
    )


def solution(mesh):
    token = P("dp", "seq", None)
    weight = P(("seq", "dp"), None)
    gain = P(("seq", "dp"))
    return jax.shard_map(
        body_direct if mesh.shape["dp"] == 8 else body_plain,
        mesh=mesh,
        in_specs=(token, token, token, P("dp", None), weight, weight, weight, weight, gain, weight, weight, weight, gain, token),
        out_specs=(token, token, token, weight, weight, weight, weight, gain, weight, weight, weight, gain),
        check_vma=False,
    )
```

```python
import functools
import math

import jax
import jax.numpy as jnp
from jax import lax
from jax.experimental import pallas as pl
from jax.experimental.pallas import tpu as pltpu
from jax.sharding import PartitionSpec as P

HEADS = 16
DOC_MOST = 512
SEQ = 4
BLOCK = 256

epsilon = 1e-06
masked_value = -1e30
bf16 = jnp.bfloat16
f32 = jnp.float32


def mul(a, b, ca, cb):
    return lax.dot_general(a, b, (((ca,), (cb,)), ((), ())), preferred_element_type=f32)


def params(mib):
    return pltpu.CompilerParams(vmem_limit_bytes=mib << 20)


VMEM = pl.BlockSpec(memory_space=pltpu.VMEM)
SMEM = pl.BlockSpec(memory_space=pltpu.SMEM)


def fixed(shape):
    return pl.BlockSpec(shape, lambda *_: (0,) * len(shape), pipeline_mode=pl.Buffered(1))


def sync(*values):
    return lax.optimization_barrier(values)


def after(value, *earlier):
    return lax.optimization_barrier((value, *earlier))[0]


def half_swap(field):
    lanes = field.shape[-1]
    lane = lax.broadcasted_iota(jnp.int32, field.shape, 1)
    up = pltpu.roll(field, lanes - 32, 1)
    down = pltpu.roll(field, 32, 1)
    return jnp.where(lane % 64 < 32, up, down)


def qkv_kernel(me_ref, tok_ref, first_ref, w_ref, gain_ref, cos_ref, sin_ref, nin_ref, q_ref, k_ref, v_ref):
    x = tok_ref[...].astype(f32)
    scale = lax.rsqrt(jnp.mean(x * x, axis=-1, keepdims=True) + epsilon)
    nin = (x * scale * gain_ref[...]).astype(bf16)
    nin_ref[...] = nin
    lin = mul(nin, w_ref[...], 1, 0)
    cos = jnp.concatenate([cos_ref[...]] * 2, axis=1)
    sin = jnp.concatenate([sin_ref[...]] * 2, axis=1)
    part = lin.shape[1] // 3
    q = lin[:, :part]
    q_ref[...] = ((q * cos + half_swap(q) * sin).astype(bf16).astype(f32) * 0.125).astype(bf16)
    k = lin[:, part : 2 * part]
    k_ref[...] = (k * cos + half_swap(k) * sin).astype(bf16)
    v_ref[...] = (0.5 * lin[:, 2 * part :] + 0.5 * first_ref[...].astype(f32)).astype(bf16)


def qkv_call(me, tok, first, w, gain, cos, sin):
    length, width = tok.shape
    rows = length // SEQ
    part = w.shape[1] // 3
    here = lambda k, m: (m[0] ^ k, 0)
    rel = lambda k, m: (k, 0)
    return pl.pallas_call(
        qkv_kernel,
        name="qkv",
        grid_spec=pltpu.PrefetchScalarGridSpec(
            num_scalar_prefetch=1,
            grid=(SEQ,),
            in_specs=[
                pl.BlockSpec((rows, width), rel),
                pl.BlockSpec((rows, part), rel),
                fixed(w.shape),
                fixed((1, width)),
                pl.BlockSpec((rows, 128), here),
                pl.BlockSpec((rows, 128), here),
            ],
            out_specs=[pl.BlockSpec((rows, width), here)] + [pl.BlockSpec((rows, part), here)] * 3,
        ),
        out_shape=[jax.ShapeDtypeStruct((length, width), bf16)]
        + [jax.ShapeDtypeStruct((length, part), bf16)] * 3,
        compiler_params=params(16),
    )(me, tok, first, w, gain, cos, sin)


def key_range(block):
    return max(0, block * BLOCK - (DOC_MOST // BLOCK) * BLOCK), (block + 1) * BLOCK


def column_of(row_ref):
    return jnp.broadcast_to(row_ref[...].astype(f32), (8, row_ref.shape[1])).T[:, :1]


def allowed_pairs(seg_col, seg_row, block, low, high):
    keys = lax.broadcasted_iota(jnp.int32, (high - low, BLOCK), 0) + low
    rows = lax.broadcasted_iota(jnp.int32, (high - low, BLOCK), 1) + block * BLOCK
    row = seg_row[:, block * BLOCK : (block + 1) * BLOCK].astype(f32)
    return (seg_col[low:high, :] == row) & (keys <= rows)


def head_lanes(field, head):
    lane = lax.broadcasted_iota(jnp.int32, field.shape, 1)
    return jnp.where(lane // 64 == head, field, jnp.zeros_like(field))


def half_rows(head):
    return pl.ds(pl.multiple_of(head * 64, 64), 64)


def attend_kernel(q_ref, k_ref, v_ref, seg_row, o_ref, lse_ref, turned, turned_out):
    length = q_ref.shape[0]
    seg_col = column_of(seg_row)
    turned[...] = v_ref[...].astype(f32).T.astype(bf16)

    def one_head(head, carry):
        for block in range(length // BLOCK):
            low, high = key_range(block)
            allowed = allowed_pairs(seg_col, seg_row, block, low, high)
            here = slice(block * BLOCK, (block + 1) * BLOCK)
            scores = mul(k_ref[low:high, :], head_lanes(q_ref[here, :], head), 1, 1)
            scores = jnp.where(allowed, scores, masked_value)
            top = jnp.max(scores, axis=0, keepdims=True)
            expo = jnp.exp(scores - top)
            total = jnp.sum(expo, axis=0, keepdims=True)
            probs = (expo * (1.0 / total)).astype(bf16)
            turned_out[half_rows(head), here] = mul(turned[half_rows(head), low:high], probs, 1, 0)
            lse_ref[0, pl.ds(head, 1), here] = top + jnp.log(total)
        return carry

    lax.fori_loop(0, 2, one_head, 0)
    for block in range(length // BLOCK):
        here = slice(block * BLOCK, (block + 1) * BLOCK)
        o_ref[here, :] = turned_out[:, here].T.astype(bf16)


def attend_call(q, k, v, seg_row):
    length, part = q.shape
    pairs = part // 128
    lanes = pl.BlockSpec((length, 128), lambda p: (0, p))
    return pl.pallas_call(
        attend_kernel,
        name="attend",
        grid=(pairs,),
        in_specs=[lanes] * 3 + [fixed((1, length))],
        out_specs=[lanes, pl.BlockSpec((1, 2, length), lambda p: (p, 0, 0))],
        out_shape=[jax.ShapeDtypeStruct((length, part), bf16), jax.ShapeDtypeStruct((pairs, 2, length), f32)],
        scratch_shapes=[pltpu.VMEM((128, length), bf16), pltpu.VMEM((128, length), f32)],
        compiler_params=params(24),
    )(q, k, v, seg_row)


def attend_back_kernel(
    dp, pieces, place_ref, q_ref, k_ref, v_ref, d0, d1, d2, d3, lse_ref, seg_row, cos_ref, sin_ref, nin_ref,
    *refs,
):
    outs, (da_ref, dk_sum, dv_sum, work, turned, turned_dq) = refs[:-6], refs[-6:]
    *along, d_ref = outs[: len(outs) - 2 * pieces]
    outs = outs[len(outs) - 2 * pieces :]
    length = q_ref.shape[0]
    rows = d0.shape[0]
    for k, ref in enumerate((d0, d1, d2, d3)):
        da_ref[pl.ds(pl.multiple_of((place_ref[0] ^ k) * rows, rows), rows), :] = ref[...]
    seg_col = column_of(seg_row)
    dk_sum[...] = jnp.zeros_like(dk_sum)
    dv_sum[...] = jnp.zeros_like(dv_sum)
    turned[...] = k_ref[...].astype(f32).T.astype(bf16)

    def one_head(head, carry):
        for block in range(length // BLOCK):
            low, high = key_range(block)
            allowed = allowed_pairs(seg_col, seg_row, block, low, high)
            here = slice(block * BLOCK, (block + 1) * BLOCK)
            q_head = head_lanes(q_ref[here, :], head)
            da_head = head_lanes(da_ref[here, :], head)
            scores = mul(k_ref[low:high, :], q_head, 1, 1)
            probs = jnp.where(allowed, jnp.exp(scores - lse_ref[0, pl.ds(head, 1), here]), 0.0)
            d_probs = mul(v_ref[low:high, :], da_head, 1, 1)
            delta = jnp.sum(probs * d_probs, axis=0, keepdims=True)
            d_scores = (probs * (d_probs - delta)).astype(bf16)
            turned_dq[half_rows(head), here] = mul(turned[half_rows(head), low:high], d_scores, 1, 0)
            dk_sum[low:high, :] += mul(d_scores, q_head, 1, 0)
            dv_sum[low:high, :] += mul(probs.astype(bf16), da_head, 1, 0)
        return carry

    lax.fori_loop(0, 2, one_head, 0)
    for block in range(length // BLOCK):
        here = slice(block * BLOCK, (block + 1) * BLOCK)
        dq = turned_dq[:, here].T * 0.125
        d_ref[here, :128] = (dq * cos_ref[here, :] - half_swap(dq) * sin_ref[here, :]).astype(bf16)
    dk = dk_sum[...]
    d_ref[:, 128:256] = (dk * cos_ref[...] - half_swap(dk) * sin_ref[...]).astype(bf16)
    d_ref[:, 256:] = (0.5 * dv_sum[...]).astype(bf16)
    if not outs:
        return
    kept_ref, sent_ref = outs
    part = work.shape[0]
    w_rows = part // dp
    first = 0
    if along:
        first = along[0].shape[0]
        sent_ref[:first, :] = along[0][...]
    for s in range(SEQ):
        work[...] = mul(nin_ref[:, s * part : (s + 1) * part], d_ref[...], 0, 0).astype(bf16)
        for slot in range(dp):
            here = pl.ds(pl.multiple_of(owner_index(place_ref, dp, slot) * w_rows, w_rows), w_rows)
            for t in range(3):
                at = (s * 3 + t) * w_rows
                piece = work[here, t * 128 : t * 128 + 128]
                if slot < dp // 2:
                    kept_ref[slot, at : at + w_rows, :] = piece
                else:
                    at += first + (slot - dp // 2) * kept_ref.shape[1]
                    sent_ref[at : at + w_rows, :] = piece


def attend_back_call(pair, place, q, k, v, da, lse, seg_row, cos, sin, nin, dp, pieces, along=()):
    length, width = nin.shape
    part = width // SEQ
    lanes = pl.BlockSpec((length, 128), lambda _: (0, pair), pipeline_mode=pl.Buffered(1))
    outs = [(length, 384)]
    if pieces:
        rows = 3 * width // dp
        outs += [(dp // 2, rows, 128), (sum(x.shape[0] for x in along) + dp // 2 * rows, 128)]
    return pl.pallas_call(
        functools.partial(attend_back_kernel, dp, pieces),
        name="attend_back",
        grid=(1,),
        in_specs=[SMEM]
        + [lanes] * 3
        + [pl.BlockSpec((length // SEQ, 128), lambda _: (0, pair), pipeline_mode=pl.Buffered(1))] * 4
        + [pl.BlockSpec((1, 2, length), lambda _: (pair, 0, 0)), fixed((1, length))]
        + [fixed((length, 128))] * 2
        + [fixed(nin.shape)]
        + [fixed(x.shape) for x in along],
        out_specs=[fixed(x) for x in outs],
        out_shape=[jax.ShapeDtypeStruct(x, bf16) for x in outs],
        scratch_shapes=[pltpu.VMEM((length, 128), bf16)]
        + [pltpu.VMEM((length, 128), f32)] * 2
        + [pltpu.VMEM((part, 384), bf16), pltpu.VMEM((128, length), bf16), pltpu.VMEM((128, length), f32)],
        compiler_params=params(60),
    )(place, q, k, v, *da, lse, seg_row, cos, sin, nin, *along)


def main_lanes(inner):
    return inner // 128 * 128


def pack_attn_kernel(
    q_ref, k_ref, v_ref, o_ref, d_ref, ag_ref, mg_ref, tok_ref, c0, c1, c2, c3, orows_ref, drows_ref, *halves_refs
):
    me = lax.axis_index("seq")
    owner = me * lax.axis_size("dp") + lax.axis_index("dp")
    w_rows, width = q_ref.shape
    part = width // SEQ
    lane = lax.broadcasted_iota(jnp.int32, (1, 128), 1)
    spot = lane // w_rows == owner % (128 // w_rows)

    def spread(gain):
        return jnp.where(spot, jnp.concatenate([gain[...].astype(f32)] * (128 // w_rows), axis=1), 0.0)

    row = lax.broadcasted_iota(jnp.int32, (16, 128), 0)
    gains = jnp.where(row == 0, spread(ag_ref), jnp.where(row == 1, spread(mg_ref), 0.0)).astype(bf16)
    for k, out in enumerate((c0, c1, c2, c3)):
        at = 0
        for ref in (q_ref, k_ref, v_ref):
            for t in range(part // 128):
                lanes = pl.ds(pl.multiple_of((me ^ k) * part + t * 128, 128), 128)
                out[at : at + w_rows, :] = ref[:, lanes]
                at += w_rows
        out[at : at + 16, :] = gains
    for ref, out in ((o_ref, orows_ref), (d_ref, drows_ref)):
        rows = ref.shape[0]
        for t in range(width // 128):
            out[t * rows : (t + 1) * rows, :] = ref[:, t * 128 : t * 128 + 128]
    for i, out in enumerate(halves_refs):
        rows = out.shape[0]
        out[...] = tok_ref[i * rows : (i + 1) * rows, :]


def pack_attn(wq, wk, wv, wo, wd, attn_gain, mlp_gain, tok):
    w_rows, width = wq.shape
    tiles = width // 128
    shapes = [(3 * tiles // SEQ * w_rows + 16, 128)] * 4 + [(tiles * w_rows, 128), (tiles * wd.shape[0], 128)]
    shapes += [(tok.shape[0] // 2, width)] * 2
    return pl.pallas_call(
        pack_attn_kernel,
        name="pack_attn",
        grid=(1,),
        in_specs=[fixed(w.shape) for w in (wq, wk, wv, wo, wd)] + [fixed((1, w_rows))] * 2 + [fixed(tok.shape)],
        out_specs=[fixed(x) for x in shapes],
        out_shape=[jax.ShapeDtypeStruct(x, bf16) for x in shapes],
        compiler_params=params(60),
    )(wq, wk, wv, wo, wd, attn_gain[None], mlp_gain[None], tok)


def pack_ffn_kernel(place_ref, g_ref, u_ref, c0, c1, c2, c3):
    me = place_ref[0]
    w_rows = g_ref.shape[0]
    inner = g_ref.shape[1] // SEQ
    main = main_lanes(inner)
    for s in range(SEQ):
        gate, up = g_ref[:, s * inner : (s + 1) * inner], u_ref[:, s * inner : (s + 1) * inner]
        tiles = [field[:, t * 128 : t * 128 + 128] for field in (gate, up) for t in range(main // 128)]
        tiles.append(jnp.concatenate([gate[:, main:], up[:, main:]], axis=1))
        for k, out in enumerate((c0, c1, c2, c3)):

            @pl.when(me ^ k == s)
            def _():
                for t, tile in enumerate(tiles):
                    out[t * w_rows : (t + 1) * w_rows, :] = tile


def pack_ffn(place, wg, wu):
    w_rows = wg.shape[0]
    inner = wg.shape[1] // SEQ
    return pl.pallas_call(
        pack_ffn_kernel,
        name="pack_ffn",
        grid=(1,),
        in_specs=[SMEM] + [fixed(w.shape) for w in (wg, wu)],
        out_specs=[fixed((2 * inner // 128 * w_rows, 128))] * 4,
        out_shape=[jax.ShapeDtypeStruct((2 * inner // 128 * w_rows, 128), bf16)] * 4,
        compiler_params=params(60),
    )(place, wg, wu)


def source_of(place_ref, dp, slot):
    groups = dp // 2
    b, j = slot // groups, slot % groups
    z, y = place_ref[2] // 2, place_ref[2] % 2
    return ((z + groups - j) % groups) * 2 + (y ^ b)


def assemble_attn_kernel(place_ref, *refs):
    dp = len(refs) - 4
    pieces, (w_ref, wo_ref, ag_ref, mg_ref) = refs[:dp], refs[dp:]
    width, lanes = w_ref.shape
    w_rows = width // (SEQ * dp)
    part = width // SEQ
    chunk = lanes // 128 * w_rows + 16
    ag_ref[...] = jnp.zeros_like(ag_ref)
    mg_ref[...] = jnp.zeros_like(mg_ref)
    for slot, piece in enumerate(pieces):
        src = source_of(place_ref, dp, slot)
        for k in range(SEQ):
            s = place_ref[0] ^ k
            row = pl.multiple_of(s * part + src * w_rows, w_rows)
            for t in range(lanes // 128):
                at = k * chunk + t * w_rows
                w_ref[pl.ds(row, w_rows), t * 128 : t * 128 + 128] = piece[at : at + w_rows, :]
            gains = piece[(k + 1) * chunk - 16 : (k + 1) * chunk, :].astype(f32)
            tile = (s * dp + src) * w_rows // 128
            ag_ref[pl.ds(tile, 1), :] += gains[0:1, :]
            mg_ref[pl.ds(tile, 1), :] += gains[1:2, :]
        row = pl.multiple_of(src * w_rows, w_rows)
        for t in range(width // 128):
            at = SEQ * chunk + t * w_rows
            wo_ref[pl.ds(row, w_rows), t * 128 : t * 128 + 128] = piece[at : at + w_rows, :]


def assemble_attn(place, pieces, width):
    shapes = [(width, 3 * width // SEQ), (width // SEQ, width), (width // 128, 128), (width // 128, 128)]
    return pl.pallas_call(
        assemble_attn_kernel,
        name="assemble_attn",
        grid=(1,),
        in_specs=[SMEM] + [fixed(x.shape) for x in pieces],
        out_specs=[fixed(x) for x in shapes],
        out_shape=[jax.ShapeDtypeStruct(x, t) for x, t in zip(shapes, (bf16, bf16, f32, f32))],
        compiler_params=params(12),
    )(place, *pieces)


def assemble_rows_kernel(place_ref, *refs):
    dp = len(refs) - 1
    pieces, out_ref = refs[:dp], refs[dp]
    count = out_ref.shape[0] // dp
    for slot, piece in enumerate(pieces):
        row = pl.multiple_of(source_of(place_ref, dp, slot) * count, 8)
        for t in range(out_ref.shape[1] // 128):
            out_ref[pl.ds(row, count), t * 128 : t * 128 + 128] = piece[t * count : (t + 1) * count, :]


def assemble_rows(place, pieces, width, inner):
    return pl.pallas_call(
        assemble_rows_kernel,
        name="assemble_rows",
        grid=(1,),
        in_specs=[SMEM] + [fixed(x.shape) for x in pieces],
        out_specs=fixed((inner, width)),
        out_shape=jax.ShapeDtypeStruct((inner, width), bf16),
        compiler_params=params(12),
    )(place, *pieces)


def ffn_kernel(me_ref, tok_ref, og_ref, a0, a1, a2, a3, wo0, wo1, wo2, wo3, gain_ref, w_ref, wd_ref, *outs):
    nm_ref, hid_ref, dgu_ref, mid_ref, *lists = outs
    step = pl.program_id(0)
    if len(w_ref.shape) == 3:
        pieces, w_ref = w_ref, lists.pop()
        dp = pieces.shape[0]
        width, lanes = w_ref.shape
        w_rows = width // (SEQ * dp)
        chunk = lanes // 128 * w_rows

        @pl.when(step == 0)
        def _():
            for k in range(SEQ):
                for src in range(dp):
                    row = pl.multiple_of((me_ref[0] ^ k) * (width // SEQ) + src * w_rows, w_rows)
                    for t in range(lanes // 128):
                        at = k * chunk + t * w_rows
                        w_ref[pl.ds(row, w_rows), t * 128 : t * 128 + 128] = pieces[src, at : at + w_rows, :]

    mid = tok_ref[...].astype(f32)
    inner = wd_ref.shape[0]
    main = main_lanes(inner)
    for a, wo in zip((a0, a1, a2, a3), (wo0, wo1, wo2, wo3)):
        mid = mid + mul(a[...], wo[...], 1, 0)
    scale = lax.rsqrt(jnp.mean(mid * mid, axis=-1, keepdims=True) + epsilon)
    nm = (mid * scale * gain_ref[...]).astype(bf16)
    nm_ref[...] = nm
    d_hidden = mul(og_ref[...], wd_ref[...], 1, 1)
    both = mul(nm, w_ref[...], 1, 0)

    def gated(gate, up, grad):
        sig = jax.nn.sigmoid(gate)
        silu = gate * sig
        return (
            (silu * up).astype(bf16),
            (grad * up * (sig * (1.0 + gate * (1.0 - sig)))).astype(bf16),
            (grad * silu).astype(bf16),
        )

    hid_main, dg_main, du_main = gated(both[:, :main], both[:, main : 2 * main], d_hidden[:, :main])
    last = both[:, 2 * main :]
    hid_last, dg_last, du_last = gated(last[:, : inner - main], last[:, inner - main :], d_hidden[:, main:])
    hid_ref[:, :main] = hid_main
    hid_ref[:, main:] = hid_last
    dgu_ref[:, :main] = dg_main
    dgu_ref[:, main : 2 * main] = du_main
    dgu_ref[:, 2 * main :] = jnp.concatenate([dg_last, du_last], axis=1)
    dnm = mul(dgu_ref[...], w_ref[...], 1, 1).astype(bf16)
    lo = mul(hid_ref[...], wd_ref[...], 1, 0).astype(bf16)
    dnm_kept, dnm_sent, lo_kept, lo_sent = lists
    rows = tok_ref.shape[0]
    for k in range(SEQ):

        @pl.when(step == SEQ - 1 - k)
        def _():
            here = slice(k // 2 * rows, (k // 2 + 1) * rows)
            (dnm_sent if k % 2 else dnm_kept)[here, :] = dnm
            (lo_sent if k % 2 else lo_kept)[here, :] = lo

    @pl.when(step == SEQ - 1)
    def _():
        mid_ref[...] = mid


def ffn_call(me, tok, og, att, wo, gain, w, wd):
    length, width = tok.shape
    rows = length // SEQ
    inner = wd.shape[0]
    part = att[0].shape[1]
    rel = lambda k, m: (SEQ - 1 - k, 0)
    here = lambda k, m: (m[0] ^ (SEQ - 1 - k), 0)
    return pl.pallas_call(
        ffn_kernel,
        name="ffn",
        grid_spec=pltpu.PrefetchScalarGridSpec(
            num_scalar_prefetch=1,
            grid=(SEQ,),
            in_specs=[pl.BlockSpec((rows, width), rel)] * 2
            + [pl.BlockSpec((rows, part), here)] * 4
            + [fixed(x.shape) for x in wo]
            + [fixed((1, width)), fixed(w.shape), fixed(wd.shape)],
            out_specs=[
                pl.BlockSpec((rows, width), rel),
                pl.BlockSpec((rows, inner), rel),
                pl.BlockSpec((rows, 2 * inner), rel),
                fixed((rows, width)),
            ]
            + [fixed((2 * rows, width))] * 4,
            scratch_shapes=[pltpu.VMEM((width, 2 * inner), bf16)] * (w.ndim - 2),
        ),
        out_shape=[
            jax.ShapeDtypeStruct((length, width), bf16),
            jax.ShapeDtypeStruct((length, inner), bf16),
            jax.ShapeDtypeStruct((length, 2 * inner), bf16),
            jax.ShapeDtypeStruct((rows, width), f32),
        ]
        + [jax.ShapeDtypeStruct((2 * rows, width), bf16)] * 4,
        compiler_params=params(60),
    )(me, tok, og, *att, *wo, gain, w, wd)


def owner_index(place_ref, dp, slot):
    groups = dp // 2
    b, j = slot // groups, slot % groups
    z, y = place_ref[2] // 2, place_ref[2] % 2
    return ((z + j) % groups) * 2 + (y ^ b)


def columns_grad_kernel(place_ref, act_ref, grad_ref, *refs):
    outs, work = refs[:-1], refs[-1]
    dp = len(outs)
    work[...] = mul(act_ref[...], grad_ref[...], 0, 0).astype(bf16)
    w_rows = work.shape[0] // dp
    for slot, ref in enumerate(outs):
        here = pl.ds(pl.multiple_of(owner_index(place_ref, dp, slot) * w_rows, w_rows), w_rows)
        for t in range(work.shape[1] // 128):
            ref[t * w_rows : (t + 1) * w_rows, :] = work[here, t * 128 : t * 128 + 128]


def columns_grad_plain(act, grad, dp):
    width, lanes = act.shape[1], grad.shape[1]
    w_rows = width // (SEQ * dp)
    grad = mul(act, grad, 0, 0).astype(bf16).reshape(SEQ, dp, w_rows, lanes // 128, 128)
    return grad.transpose(1, 0, 3, 2, 4).reshape(dp, -1, 128)


def columns_grad(place, act, grad, dp):
    length, width = act.shape
    lanes = grad.shape[1]
    part = width // SEQ
    chunk = lanes // 128 * (part // dp)
    return pl.pallas_call(
        columns_grad_kernel,
        name="columns_grad",
        grid_spec=pltpu.PrefetchScalarGridSpec(
            num_scalar_prefetch=1,
            grid=(SEQ,),
            in_specs=[pl.BlockSpec((length, part), lambda s, m: (0, s)), fixed(grad.shape)],
            out_specs=[pl.BlockSpec((chunk, 128), lambda s, m: (s, 0))] * dp,
            scratch_shapes=[pltpu.VMEM((part, lanes), bf16)],
        ),
        out_shape=[jax.ShapeDtypeStruct((SEQ * chunk, 128), bf16)] * dp,
        compiler_params=params(60),
    )(place, act, grad)


def out_grad_kernel(place_ref, act_ref, d0, d1, d2, d3, kept_ref, sent_ref, work):
    rows = d0.shape[0]
    total = 0.0
    for k, ref in enumerate((d0, d1, d2, d3)):
        act = act_ref[pl.ds(pl.multiple_of((place_ref[0] ^ k) * rows, rows), rows), :]
        total = total + mul(act, ref[...], 0, 0)
    work[...] = total.astype(bf16)
    dp = 2 * kept_ref.shape[0]
    count = work.shape[0] // dp
    at = 0
    for slot in range(dp):
        here = pl.ds(pl.multiple_of(owner_index(place_ref, dp, slot) * count, count), count)
        for t in range(work.shape[1] // 128):
            piece = work[here, t * 128 : t * 128 + 128]
            if slot < dp // 2:
                kept_ref[slot, t * count : (t + 1) * count, :] = piece
            else:
                sent_ref[at : at + count, :] = piece
                at += count


def out_projection_grad(place, act, d_branch, dp):
    width = d_branch[0].shape[1]
    part = act.shape[1]
    shape = (dp // 2, width // 128 * (part // dp), 128)
    sent = (shape[0] * shape[1], 128)
    return pl.pallas_call(
        out_grad_kernel,
        name="out_projection_grad",
        grid=(1,),
        in_specs=[SMEM, fixed(act.shape)] + [fixed(x.shape) for x in d_branch],
        out_specs=[fixed(shape), fixed(sent)],
        out_shape=[jax.ShapeDtypeStruct(shape, bf16), jax.ShapeDtypeStruct(sent, bf16)],
        scratch_shapes=[pltpu.VMEM((part, width), bf16)],
        compiler_params=params(24),
    )(place, act, *d_branch)


def down_grad_kernel(act_ref, grad_ref, out_ref):
    out_ref[...] = mul(act_ref[...], grad_ref[...], 0, 0).astype(bf16)


def down_grad(act, grad):
    length, width = grad.shape
    step = 256
    return pl.pallas_call(
        down_grad_kernel,
        name="down_grad",
        grid=(width // step,),
        in_specs=[fixed(act.shape), pl.BlockSpec((length, step), lambda c: (0, c))],
        out_specs=pl.BlockSpec((act.shape[1], step), lambda c: (0, c)),
        out_shape=jax.ShapeDtypeStruct((act.shape[1], width), bf16),
        compiler_params=params(60),
    )(act, grad)


def simple(kernel, name, args, outs, limit=24, half=()):
    half = dict(half)

    def spec(i, x):
        if i not in half:
            return SMEM if x.dtype == jnp.int32 else fixed(x.shape)
        shape = (x.shape[0] // 2, x.shape[1])
        return pl.BlockSpec(shape, lambda _: (half[i], 0), pipeline_mode=pl.Buffered(1))

    return pl.pallas_call(
        kernel,
        name=name,
        grid=(1,),
        in_specs=[spec(i, x) for i, x in enumerate(args)],
        out_specs=[fixed(x.shape) for x in outs],
        out_shape=outs,
        compiler_params=params(limit),
    )(*args)


def shaped(dtype, *shape):
    return jax.ShapeDtypeStruct(shape, dtype)


def sum_kernel(*refs):
    *ins, out = refs
    out[...] = sum(x[...].astype(f32) for x in ins).astype(out.dtype)


def total(*pieces):
    return simple(sum_kernel, "total", pieces, [shaped(bf16, *pieces[0].shape)])[0]


def lower(kept, got):
    rows, width = kept.shape[0] // 2, kept.shape[1]
    return simple(sum_kernel, "lower", (kept, got), [shaped(bf16, rows, width)], half=((0, 1), (1, 1)))[0]


def slots_kernel(kept_ref, got_ref, *outs):
    count = kept_ref.shape[1]
    at = got_ref.shape[0] - len(outs) * count
    for j, out in enumerate(outs):
        got = got_ref[at + j * count : at + (j + 1) * count, :]
        out[...] = (kept_ref[j].astype(f32) + got.astype(f32)).astype(out.dtype)


def slots(kept, got):
    shape = kept.shape[1:]
    outs = [shaped(f32, *shape)] + [shaped(bf16, *shape)] * (kept.shape[0] - 1)
    return simple(slots_kernel, "slots", (kept, got), outs)


def back_through_norm(grad, field, gain):
    scale = lax.rsqrt(jnp.mean(field * field, axis=-1, keepdims=True) + epsilon)
    unit = field * scale
    pressed = grad * gain
    return scale * (pressed - unit * jnp.mean(pressed * unit, axis=-1, keepdims=True))


def branch_kernel(kept_ref, got_ref, far_ref, mid_ref, og_ref, gain_ref, w0, w1, w2, w3, d_mid_ref, d_ref, a0, a1, a2, a3):
    grad = kept_ref[...].astype(f32) + got_ref[...].astype(f32) + far_ref[...].astype(f32)
    d_mid = og_ref[...].astype(f32) + back_through_norm(grad, mid_ref[...], gain_ref[...])
    d_mid_ref[...] = d_mid
    d_branch = d_mid.astype(bf16)
    d_ref[...] = d_branch
    for w, a in ((w0, a0), (w1, a1), (w2, a2), (w3, a3)):
        a[...] = mul(d_branch, w[...], 1, 1).astype(bf16)


def token_grad_kernel(kept_ref, got_ref, far_ref, tok_ref, gain_ref, d_mid_ref, out_ref):
    grad = kept_ref[...].astype(f32) + got_ref[...].astype(f32) + far_ref[...].astype(f32)
    out_ref[...] = (d_mid_ref[...] + back_through_norm(grad, tok_ref[...].astype(f32), gain_ref[...])).astype(bf16)


def cut_kernel(me_ref, *refs):
    ins, d_ref, (mine_ref, near_ref, far_ref) = refs[:-4], refs[-4], refs[-3:]
    groups = [ins[:4], ins[4:8], ins[8:]]
    count = far_ref.shape[0] - 2 * mine_ref.shape[0]
    far_ref[2 * mine_ref.shape[0] :, :] = d_ref[pl.ds(pl.multiple_of(((me_ref[0] >> 1) ^ 1) * count, count), count), 256:]
    me = me_ref[0]
    at = 0
    for pieces in groups:
        chunk = pieces[0].shape[0] // SEQ

        def chunk_of(s):
            here = pl.ds(pl.multiple_of(s * chunk, 8), chunk)
            return sum(x[here, :].astype(f32) for x in pieces).astype(bf16)

        mine_ref[at : at + chunk, :] = chunk_of(me)
        near_ref[at : at + chunk, :] = chunk_of(me ^ 1)
        for core in range(2):
            row = core * mine_ref.shape[0] + at
            far_ref[row : row + chunk, :] = chunk_of(((me >> 1) ^ 1) * 2 + core)
        at += chunk


def cut(me, attn, ffn, d_pair):
    rows = (attn[0][0].shape[0] * 2 + ffn[0].shape[0]) // SEQ
    outs = [shaped(bf16, n, 128) for n in (rows, rows, 2 * rows + d_pair.shape[0] // 2)]
    return simple(cut_kernel, "cut", (me, *attn[0], *attn[1], *ffn, d_pair), outs)


def relay_kernel(me_ref, near, far, d0_ref, d1_ref, far0_ref, out_ref):
    me = me_ref[0]
    core = (me & 1) ^ 1
    count = near.shape[0]
    out_ref[:count, :] = near[...]
    out_ref[count : 2 * count, :] = far[pl.ds(pl.multiple_of(core * count, 8), count), :]
    at = 2 * count
    rows = far0_ref.shape[0] // 2
    first = pl.multiple_of((me ^ 1) * rows, rows)
    for d_ref, far_ref, row in ((d0_ref, far0_ref, 0), (d1_ref, far, 2 * count)):
        out_ref[at : at + rows, :] = d_ref[pl.ds(first, rows), 256:]
        out_ref[at + rows : at + 2 * rows, :] = far_ref[pl.ds(pl.multiple_of(row + core * rows, 8), rows), :]
        at += 2 * rows


def value_grad_kernel(me_ref, acc_ref, d0_ref, d1_ref, far0_ref, far, got_ref, out_ref):
    me = me_ref[0]
    rows = acc_ref.shape[0]
    first = pl.multiple_of(me * rows, rows)
    at = far.shape[0] - 2 * rows

    for p, (d_ref, far_ref, row) in enumerate(((d0_ref, far0_ref, 0), (d1_ref, far, at))):
        pieces = (
            d_ref[pl.ds(first, rows), 256:],
            got_ref[at : at + rows, :],
            far_ref[pl.ds(pl.multiple_of(row + (me & 1) * rows, 8), rows), :],
            got_ref[at + rows : at + 2 * rows, :],
        )
        for k, piece in enumerate(pieces):
            lanes = pl.ds(pl.multiple_of((me ^ k) * 256 + p * 128, 128), 128)
            out_ref[:, lanes] = acc_ref[:, lanes] + piece.astype(f32)
        at += 2 * rows


def finish_kernel(
    me_ref, mine, far, got_ref, o0, o1, o2, o3, wq, wk, wv, wg, wu, ga_ref, gm_ref, down_ref,
    gq_ref, gk_ref, gv_ref, go_ref, gga_ref, gg_ref, gu_ref, ggm_ref, gd_ref, cols_a, cols_f,
):
    me = me_ref[0]
    gd_ref[...] = down_ref[...].astype(f32)
    count = mine.shape[0]
    at = 0
    for cols in (cols_a, cols_f):
        chunk = cols.shape[1]
        cols[0] = mine[at : at + chunk, :]
        cols[2] = far[pl.ds(pl.multiple_of((me & 1) * count + at, 8), chunk), :]
        cols[1] = got_ref[at : at + chunk, :]
        cols[3] = got_ref[count + at : count + at + chunk, :]
        at += chunk
    out = sum(x[...].astype(f32) for x in (o0, o1, o2, o3))
    w_rows, width = gq_ref.shape
    for t in range(width // 128):
        go_ref[:, t * 128 : t * 128 + 128] = out[t * w_rows : (t + 1) * w_rows, :]
    unpack_attn(me, cols_a, gq_ref, gk_ref, gv_ref)
    gga_ref[...] = gain_grad(((wq, gq_ref), (wk, gk_ref), (wv, gv_ref)), ga_ref)
    unpack_ffn(me, cols_f, gg_ref, gu_ref)
    ggm_ref[...] = gain_grad(((wg, gg_ref), (wu, gu_ref)), gm_ref)


def gain_grad(pairs, gain_ref):
    column = sum(jnp.sum(w[...].astype(f32) * g[...], axis=1, keepdims=True) for w, g in pairs)
    rows = column.shape[0]
    same = lax.broadcasted_iota(jnp.int32, (rows, rows), 0) == lax.broadcasted_iota(jnp.int32, (rows, rows), 1)
    return jnp.sum(jnp.where(same, column, 0.0), axis=0, keepdims=True) / gain_ref[...].astype(f32)


def unpack_attn(me, cols_ref, *outs):
    w_rows, width = outs[0].shape
    part = width // SEQ
    for s in range(SEQ):
        at = 0
        for t in range(part // 128):
            for ref in outs:
                lanes = slice(s * part + t * 128, s * part + t * 128 + 128)
                ref[:, lanes] = cols_ref[me ^ s, at : at + w_rows, :].astype(f32)
                at += w_rows


def unpack_ffn(me, cols_ref, gg_ref, gu_ref):
    w_rows = gg_ref.shape[0]
    inner = gg_ref.shape[1] // SEQ
    main = main_lanes(inner)
    rest = inner - main
    half = main // 128
    for s in range(SEQ):
        slot = me ^ s
        tiles = [cols_ref[slot, t * w_rows : (t + 1) * w_rows, :].astype(f32) for t in range(2 * inner // 128)]
        gg_ref[:, s * inner : (s + 1) * inner] = jnp.concatenate(tiles[:half] + [tiles[-1][:, :rest]], axis=1)
        gu_ref[:, s * inner : (s + 1) * inner] = jnp.concatenate(tiles[half : 2 * half] + [tiles[-1][:, rest:]], axis=1)


def unpack_kernel(me_ref, cols_a, cols_f, wq, wk, wv, wg, wu, ga_ref, gm_ref, gq_ref, gk_ref, gv_ref, gga_ref, gg_ref, gu_ref, ggm_ref):
    unpack_attn(me_ref[0], cols_a, gq_ref, gk_ref, gv_ref)
    gga_ref[...] = gain_grad(((wq, gq_ref), (wk, gk_ref), (wv, gv_ref)), ga_ref)
    unpack_ffn(me_ref[0], cols_f, gg_ref, gu_ref)
    ggm_ref[...] = gain_grad(((wg, gg_ref), (wu, gu_ref)), gm_ref)


def input_grad_kernel(me_ref, *refs):
    *d_refs, w_ref, kept_ref, sent_ref = refs
    step = pl.program_id(0)
    d_qkv = [d[:, i * 128 : i * 128 + 128] for i in range(3) for d in d_refs]
    grad = mul(jnp.concatenate(d_qkv, axis=1), w_ref[...], 1, 1).astype(bf16)
    rows = grad.shape[0]
    for k in range(SEQ):

        @pl.when(step == SEQ - 1 - k)
        def _():
            (sent_ref if k % 2 else kept_ref)[k // 2 * rows : (k // 2 + 1) * rows, :] = grad


def input_grad(me, d_qkv, w):
    length, part = d_qkv[0].shape
    width = w.shape[0]
    rows = length // SEQ
    here = lambda k, m: (m[0] ^ (SEQ - 1 - k), 0)
    return pl.pallas_call(
        input_grad_kernel,
        name="input_grad",
        grid_spec=pltpu.PrefetchScalarGridSpec(
            num_scalar_prefetch=1,
            grid=(SEQ,),
            in_specs=[pl.BlockSpec((rows, part), here)] * len(d_qkv) + [fixed(w.shape)],
            out_specs=[fixed((2 * rows, width))] * 2,
        ),
        out_shape=[jax.ShapeDtypeStruct((2 * rows, width), bf16)] * 2,
        compiler_params=params(16),
    )(me, *d_qkv, w)


def to_core(value):
    return lax.ppermute(value, "seq", [(i, i ^ 1) for i in range(SEQ)])


def to_chip(value):
    return lax.ppermute(value, "seq", [(i, i ^ 2) for i in range(SEQ)])


def to_both(value):
    return lax.ppermute(value, "seq", [(i, i ^ 3) for i in range(SEQ)])


def gather_rel(value):
    far = to_chip(value)
    return value, to_core(value), far, to_core(far)


def exchange_rel(pieces):
    return [pieces[0], to_core(pieces[1]), to_chip(pieces[2]), to_both(pieces[3])]


def scatter_sum(kept, sent):
    sums = add(kept, to_core(sent))
    rows = kept.shape[0] // 2
    return sums[:rows] + to_chip(sums[rows:].astype(bf16)).astype(f32)


def add(a, b):
    return a.astype(f32) + b.astype(f32)


def to_y(value):
    dp = lax.axis_size("dp")
    return lax.ppermute(value, "dp", [(i, i ^ 1) for i in range(dp)])


def to_z(value, hops=1):
    dp = lax.axis_size("dp")
    return lax.ppermute(value, "dp", [(i, (i + 2 * hops) % dp) for i in range(dp)])


def rotary(length, head_width):
    pairs = jnp.arange(head_width // 2, dtype=f32)
    freq = jnp.exp(pairs * (-2.0 * math.log(10000.0) / head_width))
    theta = jnp.arange(length, dtype=jnp.int32).astype(f32)[:, None] * freq[None, :]
    cos, sin = jnp.cos(theta), jnp.sin(theta)
    return jnp.concatenate([cos] * 4, axis=1), jnp.concatenate([-sin, sin] * 2, axis=1)


class Stage:
    def fence(self):
        names = list(vars(self))
        for name, value in zip(names, sync(*[getattr(self, name) for name in names])):
            setattr(self, name, value)


def body_direct(
    tokens, first_values, value_grad_acc, segment_ids, query_weight, key_weight, value_weight, out_weight,
    attn_gain, gate_weight, up_weight, down_weight, mlp_gain, out_grad,
):
    dp = lax.axis_size("dp")
    zs = dp // 2
    rows, width = tokens.shape[1:]
    length = segment_ids.shape[1]
    w_rows = query_weight.shape[0]
    part = width // SEQ
    inner = gate_weight.shape[1] // SEQ
    me = lax.axis_index("seq").astype(jnp.int32)
    mine = lax.axis_index("dp").astype(jnp.int32)
    me_arg = me[None]
    place = jnp.stack([me, me * dp + mine, mine])
    s = Stage()

    half = rows // 2
    *s.cols, s.orows, drows, tok_a, tok_b = pack_attn(
        query_weight, key_weight, value_weight, out_weight, down_weight, attn_gain, mlp_gain, tokens[0]
    )
    s.r, s.tok_far = [drows], [tok_a, tok_b]
    s.tokens, s.first, s.out_grad, s.segments = tokens[0], first_values[0], out_grad[0], segment_ids
    s.gate, s.up = gate_weight, up_weight
    s.fence()
    s.cols = exchange_rel(s.cols)
    down = after(s.r[0], s.cols[1])
    down_near, down_next = to_y(down), to_z(down)
    s.fence()
    s.ry = [down_near]
    s.r.append(down_next)
    s.a = [jnp.concatenate([*s.cols, s.orows])]
    del s.cols, s.orows
    s.tok_far[0] = to_chip(s.tok_far[0])
    s.ay = [to_y(s.a[0])]
    s.a.append(to_z(s.a[0]))
    s.fcols = pack_ffn(place, s.gate, s.up)
    del s.gate, s.up
    s.fence()
    s.ay.append(to_y(s.a[1]))
    s.a.append(to_z(s.a[1]))
    s.f_piece = jnp.concatenate(exchange_rel(s.fcols))
    s.cos, s.sin = rotary(length, width // HEADS)
    del s.fcols
    s.fence()
    ffn_all = lax.all_gather(s.f_piece, "dp", axis=0, tiled=False)
    del s.f_piece
    s.tok_far[1] = to_chip(s.tok_far[1])
    s.ay.append(to_y(s.a[2]))
    s.a.append(to_z(s.a[2]))
    s.tok_near = to_core(s.tokens)
    s.first = [lax.dynamic_slice_in_dim(s.first, (me ^ k) * part, part, 1) for k in range(SEQ)]
    s.og_far = [s.out_grad[:half], s.out_grad[half:]]
    s.fence()
    s.ay.append(to_y(s.a[3]))
    s.first = jnp.concatenate(exchange_rel(s.first))
    tok_far = jnp.concatenate(s.tok_far)
    s.tok = jnp.concatenate([s.tokens, s.tok_near, tok_far, to_core(tok_far)])
    del s.tok_far, s.tok_near
    s.fence()
    s.ry.append(to_y(s.r[1]))
    s.r.append(to_z(s.r[1]))
    s.og_far[0] = to_chip(s.og_far[0])
    s.og = [s.out_grad, to_core(s.out_grad)]
    s.w_qkv, s.w_out, attn_gain_all, mlp_gain_all = assemble_attn(place, s.a + s.ay, width)
    s.attn_gain, s.mlp_gain = attn_gain_all.reshape(1, width), mlp_gain_all.reshape(1, width)
    s.nin, s.q, s.k, s.v = qkv_call(me_arg, s.tok, s.first, s.w_qkv, s.attn_gain, s.cos, s.sin)
    del s.a, s.ay, s.first
    s.fence()
    s.og_far[1] = to_chip(s.og_far[1])
    s.wo = [s.w_out, to_core(s.w_out), to_chip(s.w_out)]
    s.ry.append(to_y(s.r[2]))
    s.r.append(to_z(s.r[2]))
    s.attended, s.lse = attend_call(s.q, s.k, s.v, s.segments)
    del s.w_out
    s.fence()
    att_far = to_chip(s.attended)
    s.w_down = assemble_rows(place, s.r + s.ry + [to_y(s.r[3])], width, inner)
    s.att = [s.attended, to_core(s.attended), att_far]
    s.wo.append(to_core(s.wo[2]))
    og_far = jnp.concatenate(s.og_far)
    s.og = jnp.concatenate([*s.og, og_far, to_core(og_far)])
    del s.r, s.ry, s.og_far
    s.fence()
    s.att.append(to_core(s.att[2]))
    s.fence()
    s.nm, s.hidden, s.d_gu, s.mid, s.dnm, dnm_sent, s.lo, s.lo_sent = ffn_call(
        me_arg, s.tok, s.og, s.att, s.wo, s.mlp_gain, ffn_all, s.w_down
    )
    s.dnm_got = to_core(dnm_sent)
    s.dnm_far = lower(s.dnm, s.dnm_got)
    del s.tok, s.att, s.w_down
    s.fence()
    s.dnm_far = to_chip(s.dnm_far)
    pieces = list(columns_grad(place, s.nm, s.d_gu, dp))
    s.f_kept, s.f_sent = pieces[:zs], pieces[zs:]
    s.g_down = down_grad(after(s.hidden, pieces[0]), s.og)
    g_down = lax.psum_scatter(s.g_down, "dp", scatter_dimension=0, tiled=True)
    del s.nm, s.d_gu, s.hidden, s.og
    s.fence()
    s.f_sent[3] = to_y(s.f_sent[3])
    s.lo_got = to_core(s.lo_sent)
    s.d_middle, s.d_branch, *s.d_att = simple(
        branch_kernel,
        "branch",
        (s.dnm, s.dnm_got, s.dnm_far, s.mid, s.out_grad, s.mlp_gain, *s.wo),
        [shaped(f32, rows, width), shaped(bf16, rows, width)] + [shaped(bf16, rows, part)] * SEQ,
        half=((0, 0), (1, 0)),
    )
    s.lo_far = lower(s.lo, s.lo_got)
    del s.dnm, s.dnm_got, s.dnm_far, s.wo, s.lo_sent, s.g_down
    s.fence()
    s.d_att = exchange_rel(s.d_att)
    s.f_sent[2] = to_y(s.f_sent[2])
    s.f = to_z(total(s.f_kept[3], s.f_sent[3]))
    s.fence()

    def back(pair, *along):
        return attend_back_call(
            pair, place, s.q, s.k, s.v, s.d_att, s.lse, s.segments, s.cos, s.sin, s.nin, dp, True, along
        )

    def other_chip_values(d_pair):
        return lax.dynamic_slice(d_pair, (((me >> 1) ^ 1) * 2 * rows, 256), (2 * rows, 128))

    s.f_sent[1] = to_y(s.f_sent[1])
    s.f = to_z(total(s.f_kept[2], s.f_sent[2], s.f))
    s.d_branch = [s.d_branch, to_core(s.d_branch), to_chip(s.d_branch)]
    d_pair, kept, sent = back(0, s.f_sent[0])
    s.d_qkv, s.kept, s.sent = [d_pair], [kept], [sent]
    s.fence()
    s.sent[0] = to_y(s.sent[0])
    s.f = to_z(total(s.f_kept[1], s.f_sent[1], s.f))
    s.lo_far = to_chip(s.lo_far)
    s.d_branch.append(to_core(s.d_branch[2]))
    s.values_far = to_chip(other_chip_values(s.d_qkv[0]))
    d_pair, kept, sent = back(1)
    s.d_qkv.append(d_pair)
    s.dnin, s.dnin_sent = input_grad(me_arg, s.d_qkv, s.w_qkv)
    s.kept.append(kept)
    s.sent.append(sent)
    del s.nin, s.d_att, s.w_qkv
    s.fence()

    def over_z(first, *others):
        return [first] + [to_z(piece, j + 1) for j, piece in enumerate(others)]

    s.sent[1] = to_y(s.sent[1])
    s.kept[0] = over_z(*slots(s.kept[0], s.sent[0]))
    s.dnin_got = to_core(s.dnin_sent)
    s.dnin_far = lower(s.dnin, s.dnin_got)
    s.out_kept, s.out_sent = out_projection_grad(place, s.attended, s.d_branch, dp)
    del s.d_branch, s.attended, s.dnin_sent
    s.fence()
    s.kept[1] = over_z(*slots(s.kept[1], s.sent[1]))
    s.out_kept = slots(s.out_kept, to_y(s.out_sent))
    s.dnin_far = to_chip(s.dnin_far)
    s.layer_out = simple(
        sum_kernel,
        "layer_out",
        (s.mid, s.lo, s.lo_got, s.lo_far),
        [shaped(bf16, rows, width)],
        half=((1, 0), (2, 0)),
    )[0]
    del s.lo, s.lo_got, s.lo_far, s.mid
    s.fence()
    s.mine, s.near, far = cut(me_arg, s.kept, (s.f_kept[0], s.sent[0], s.f), s.d_qkv[1])
    s.far = to_chip(far)
    s.out_kept = over_z(*s.out_kept)
    s.token_grad = simple(
        token_grad_kernel,
        "token_grad",
        (s.dnin, s.dnin_got, s.dnin_far, s.tokens, s.attn_gain, s.d_middle),
        [shaped(bf16, rows, width)],
        60,
        ((0, 0), (1, 0)),
    )[0]
    s.g_down = g_down
    del s.kept, s.sent, s.out_sent, s.dnin, s.dnin_got, s.d_middle, s.f, s.f_kept, s.f_sent
    s.fence()
    count = s.mine.shape[0]
    args = (me_arg, s.near, s.far, *s.d_qkv, s.values_far)
    got = to_core(simple(relay_kernel, "relay", args, [shaped(bf16, 2 * count + SEQ * rows, 128)])[0])
    weights = (query_weight, key_weight, value_weight, gate_weight, up_weight)
    shapes = [(w_rows, width)] * 4 + [(1, w_rows)] + [(w_rows, SEQ * inner)] * 2 + [(1, w_rows), g_down.shape]
    args = (s.mine, s.far, got, *s.out_kept, *weights, attn_gain[None], mlp_gain[None], s.g_down)
    a_rows = 3 * part // 128 * w_rows
    g_q, g_k, g_v, g_out, attn_gain_grad, g_gate, g_up, mlp_gain_grad, g_down = pl.pallas_call(
        finish_kernel,
        name="finish",
        grid=(1,),
        in_specs=[SMEM] + [fixed(x.shape) for x in args],
        out_specs=[fixed(x) for x in shapes],
        out_shape=[shaped(f32, *x) for x in shapes],
        scratch_shapes=[pltpu.VMEM((SEQ, a_rows, 128), bf16), pltpu.VMEM((SEQ, count - a_rows, 128), bf16)],
        compiler_params=params(24),
    )(me_arg, *args)
    value_grad_out = simple(
        value_grad_kernel,
        "value_grad",
        (me_arg, value_grad_acc[0], *s.d_qkv, s.values_far, s.far, got),
        [shaped(f32, rows, width)],
    )[0]
    return (
        s.layer_out[None],
        s.token_grad[None],
        value_grad_out[None],
        g_q,
        g_k,
        g_v,
        g_out,
        attn_gain_grad[0],
        g_gate,
        g_up,
        g_down,
        mlp_gain_grad[0],
    )


def body_plain(
    tokens, first_values, value_grad_acc, segment_ids, query_weight, key_weight, value_weight, out_weight,
    attn_gain, gate_weight, up_weight, down_weight, mlp_gain, out_grad,
):
    dp = lax.axis_size("dp")
    rows, width = tokens.shape[1:]
    length = segment_ids.shape[1]
    w_rows, d_rows = query_weight.shape[0], down_weight.shape[0]
    part = width // SEQ
    inner = gate_weight.shape[1] // SEQ
    main = main_lanes(inner)
    me = lax.axis_index("seq").astype(jnp.int32)
    mine = lax.axis_index("dp").astype(jnp.int32)
    me_arg = me[None]
    place = jnp.stack([me, me * dp + mine, mine])

    def columns(weight, count):
        return weight.reshape(w_rows, SEQ, count).transpose(1, 0, 2)

    owner = jnp.arange(width) // w_rows == me * dp + mine

    def spread(gain):
        full = jnp.where(owner, jnp.tile(gain, width // w_rows), jnp.zeros((), bf16))
        cut = 3 * part
        return jnp.stack([full[:cut], jnp.pad(full[cut:], (0, 2 * cut - width))])

    gains = jnp.concatenate([spread(attn_gain), spread(mlp_gain), jnp.zeros((4, 3 * part), bf16)])
    attn_cols = jnp.concatenate([columns(w, part) for w in (query_weight, key_weight, value_weight)], axis=2)
    attn_cols = jnp.concatenate([attn_cols, jnp.broadcast_to(gains[None], (SEQ,) + gains.shape)], axis=1)
    gate_cols, up_cols = columns(gate_weight, inner), columns(up_weight, inner)
    ffn_cols = jnp.concatenate(
        [gate_cols[:, :, :main], up_cols[:, :, :main], gate_cols[:, :, main:], up_cols[:, :, main:]], axis=2
    )
    attn_cols = lax.all_to_all(attn_cols, "seq", split_axis=0, concat_axis=0, tiled=True)
    ffn_cols = lax.all_to_all(ffn_cols, "seq", split_axis=0, concat_axis=0, tiled=True)
    attn_all = lax.all_gather(attn_cols.reshape(-1, 3 * part), "dp", axis=0, tiled=True)
    attn_all = attn_all.reshape(dp, SEQ, w_rows + 8, 3 * part)
    w_qkv = attn_all[:, :, :w_rows].transpose(1, 0, 2, 3).reshape(width, 3 * part)
    gain_all = jnp.sum(attn_all[:, :, w_rows : w_rows + 4].astype(f32), axis=(0, 1))
    attn_gain_all = jnp.concatenate([gain_all[0], gain_all[1]])[None, :width]
    mlp_gain_all = jnp.concatenate([gain_all[2], gain_all[3]])[None, :width]
    w_out = lax.all_gather(out_weight, "dp", axis=0, tiled=True)
    w_down = lax.all_gather(down_weight, "dp", axis=0, tiled=True)
    ffn_all = lax.all_gather(ffn_cols.reshape(-1, 2 * inner), "dp", axis=0, tiled=True)
    w_ffn = ffn_all.reshape(dp, SEQ, w_rows, 2 * inner).transpose(1, 0, 2, 3).reshape(width, 2 * inner)

    cos, sin = rotary(length, width // HEADS)
    tok = jnp.concatenate(gather_rel(tokens[0]))
    og = jnp.concatenate(gather_rel(out_grad[0]))
    first_cols = first_values[0].reshape(rows, SEQ, part)
    first = exchange_rel([lax.dynamic_index_in_dim(first_cols, me ^ k, 1, keepdims=False) for k in range(SEQ)])
    nin, q, k, v = qkv_call(me_arg, tok, jnp.concatenate(first), w_qkv, attn_gain_all, cos, sin)
    attended, lse = attend_call(q, k, v, segment_ids)
    wo = gather_rel(w_out)
    nm, hidden, d_gu, mid, *sums = ffn_call(me_arg, tok, og, gather_rel(attended), wo, mlp_gain_all, w_ffn, w_down)
    layer_out = (mid + scatter_sum(*sums[2:])).astype(bf16)
    d_middle = out_grad[0].astype(f32) + back_through_norm(scatter_sum(*sums[:2]), mid, mlp_gain_all)
    d_branch = d_middle.astype(bf16)
    d_att = exchange_rel([mul(d_branch, w, 1, 1).astype(bf16) for w in wo])
    d_branch_all = jnp.stack(gather_rel(d_branch))[me ^ jnp.arange(SEQ)].reshape(length, width)
    d_qkv = [
        attend_back_call(pair, place, q, k, v, d_att, lse, segment_ids, cos, sin, nin, dp, False)[0] for pair in range(2)
    ]
    dnin = scatter_sum(*input_grad(me_arg, d_qkv, w_qkv))
    token_grad = d_middle + back_through_norm(dnin, tokens[0].astype(f32), attn_gain_all)
    dv = jnp.concatenate([d[:, 256:] for d in d_qkv], axis=1)
    dv = exchange_rel([lax.dynamic_slice_in_dim(dv, (me ^ i) * rows, rows, 0) for i in range(SEQ)])
    dv = jnp.stack(dv)[me ^ jnp.arange(SEQ)].transpose(1, 0, 2).reshape(rows, width)
    value_grad_out = value_grad_acc[0] + dv.astype(f32)

    def over_dp(grads):
        return lax.psum_scatter(grads.reshape(-1, 128), "dp", scatter_dimension=0, tiled=True)

    def to_rows(sums):
        sums = sums.reshape(SEQ, -1, 128)
        return jnp.stack(exchange_rel([lax.dynamic_index_in_dim(sums, me ^ i, 0, keepdims=False) for i in range(SEQ)]))

    attn_sums = over_dp(columns_grad_plain(nin, jnp.concatenate(d_qkv, axis=1), dp))
    ffn_sums = over_dp(columns_grad_plain(nm, d_gu, dp))
    g_out = lax.psum_scatter(mul(attended, d_branch_all, 0, 0).astype(bf16), "dp", scatter_dimension=0, tiled=True)
    g_down = lax.psum_scatter(mul(hidden, og, 0, 0).astype(bf16), "dp", scatter_dimension=0, tiled=True)
    weights = (query_weight, key_weight, value_weight, gate_weight, up_weight)
    shapes = [(w_rows, width)] * 3 + [(1, w_rows)] + [(w_rows, SEQ * inner)] * 2 + [(1, w_rows)]
    args = (me_arg, to_rows(attn_sums), to_rows(ffn_sums), *weights, attn_gain[None], mlp_gain[None])
    g_q, g_k, g_v, attn_gain_grad, g_gate, g_up, mlp_gain_grad = simple(
        unpack_kernel, "unpack", args, [shaped(f32, *x) for x in shapes]
    )
    return (
        layer_out[None],
        token_grad.astype(bf16)[None],
        value_grad_out[None],
        g_q,
        g_k,
        g_v,
        g_out.astype(f32),
        attn_gain_grad[0],
        g_gate,
        g_up,
        g_down.astype(f32),
        mlp_gain_grad[0],
    )


def solution(mesh):
    token = P("dp", "seq", None)
    weight = P(("seq", "dp"), None)
    gain = P(("seq", "dp"))
    return jax.shard_map(
        body_direct if mesh.shape["dp"] == 8 else body_plain,
        mesh=mesh,
        in_specs=(token, token, token, P("dp", None), weight, weight, weight, weight, gain, weight, weight, weight, gain, token),
        out_specs=(token, token, token, weight, weight, weight, weight, gain, weight, weight, weight, gain),
        check_vma=False,
    )
```
